512 devices in a mesh: dom: 128 (over y, x_lo, z), head: 4 (over x_hi, core).
Axes of the slice: x: 4 (x_hi: 2, x_lo: 2; x = x_hi * 2 + x_lo), y: 4, z: 16, core: 2. Of those that a mesh axis runs over, the one named last changes fastest.
Arguments:
- node_features: bfloat16 [16384, 1024], P('dom', 'head'), may hold values from -60 to 60
- cotangent: bfloat16 [16384, 1024], P('dom', 'head'), may hold values from -3 to 3
- proj_weights: bfloat16 [1024, 4, 1024], P('dom', None, 'head'), may hold values from -0.21875 to 0.21875
- local_mask: int32 [128, 1], P('dom'), may hold values 0 or 1
- matching: int32 [3, 128], P(None, 'dom'), may hold values from 0 to 0, as said below
Outputs:
- input_grad: bfloat16 [16384, 1024], P('dom', 'head')
- weight_grads: float32 [1024, 3, 1024], P('dom', None, 'head')
The draws below stay inside these ranges and needn't reach their ends.
Inputs may be any that keep to these rules, and one draw needn't show every extreme that they name: `matching`: in each round, the 1 entries of the blocks of one partition are a permutation of 0 to 0.
All inputs are finite; a program needn't handle non-finite values. No bound on the sum of `local_mask` on one device may be relied on, other than what follows from the above.
Results may differ from the reference program's by a relative error of at most 0.0095.
The reference program's roundings to bfloat16 on the way (of `out_grad`, `probs_low`, `score_grad` and `head_partial`) count: a program that leaves them out, or rounds other values in their place, can miss the bound.
Values may be sent and summed in bfloat16 or wider, within the bound.
No kernel may reach another device: no remote copies, remote signals or barrier semaphores. Data moves between devices by JAX's collectives and lax.ppermute only.
A program may use at most 64 MiB of HBM per device.

```python
import jax
import jax.numpy as jnp
from jax import lax

D = 1024
HEAD_DIM = 64
BLOCK = 128
BLK_DEV = 1
ROUNDS = 3
BLOCKS = 128
NODES = 16384
N_HEAD = 4


def draw_node_features(key, part):
    first = jax.random.fold_in(jax.random.fold_in(key, 11), 0)
    base = jnp.clip(jax.random.normal(first, (NODES, D), jnp.float32), -6.0, 6.0)
    return base.astype(jnp.bfloat16)


def draw_proj_weights(key, part):
    first = jax.random.fold_in(jax.random.fold_in(key, 23), 0)
    base = jnp.clip(jax.random.normal(first, (D, 4, D), jnp.float32), -6.0, 6.0) * D ** (-0.5)
    return base.astype(jnp.bfloat16)


def draw_matching(key, part):
    keys = jax.random.split(jax.random.fold_in(key, 37), ROUNDS * (BLOCKS // BLK_DEV))
    orders = jax.vmap(lambda single: jax.random.permutation(single, BLK_DEV))(keys)
    return orders.reshape(ROUNDS, BLOCKS).astype(jnp.int32)


def plant(result, stream_key, low, top_value):
    longest = result.shape.index(max(result.shape))
    spots = []
    for shift in (0, 1):
        where = [jax.random.randint(jax.random.fold_in(stream_key, axis), (), 0, length) for axis, length in enumerate(result.shape)]
        where[longest] = (where[longest] + shift) % result.shape[longest]
        spots.append(tuple(where))
    return result.at[spots[0]].set(low).at[spots[1]].set(top_value)


def block_levels(rng, dims, cuts, low, high):
    level, own = 1.0, jax.random.fold_in(rng, 6)
    for axis_at, parts in cuts:
        heights = jnp.exp(jax.random.uniform(jax.random.fold_in(own, axis_at), (parts,), jnp.float32, low / len(cuts), high / len(cuts)))
        level = level * jnp.repeat(heights, dims[axis_at] // parts).reshape([-1 if axis == axis_at else 1 for axis in range(len(dims))])
    return level


def normal_values(own_key, dims, deviation, bound, pieces=(), held_as=jnp.bfloat16):
    values = jax.random.normal(own_key, dims, jnp.float32) * deviation
    if len(pieces) > 0:
        values = block_levels(own_key, dims, pieces, -0.22, 0.18) * values
    return jnp.clip(values, min=-bound, max=bound).astype(held_as)


def setup_inputs(seed: int = 0) -> dict:
    key_of = jax.random.split(jax.random.key(seed), 6)
    return {
        "node_features": draw_node_features(jax.random.fold_in(key_of[5], 71), 0),
        "cotangent": normal_values(key_of[1], (NODES, D), 0.5, 3.0, ((0, 128), (1, 4))),
        "proj_weights": draw_proj_weights(jax.random.fold_in(key_of[5], 71), 0),
        "local_mask": plant((jax.random.randint(key_of[3], (BLOCKS, BLK_DEV), 0, 2) < 1).astype(jnp.int32), jax.random.fold_in(key_of[3], 1), 0, 1),
        "matching": draw_matching(jax.random.fold_in(key_of[5], 71), 0),
    }


def round_offsets(parts_count):
    return [1 + (index * parts_count) // (ROUNDS + 1) for index in range(ROUNDS)]


def split_heads(array):
    return array.reshape(array.shape[:-1] + (array.shape[-1] // HEAD_DIM, HEAD_DIM))


def join_heads(array):
    return array.reshape(array.shape[:-2] + (array.shape[-2] * array.shape[-1],))


def product(form, left, right):
    return jnp.einsum(form, left.astype(jnp.float32), right.astype(jnp.float32))


def place(blocks, order):
    return jnp.zeros_like(blocks).at[order].set(blocks)


def rounded(array):
    return lax.optimization_barrier(array.astype(jnp.bfloat16)).astype(jnp.float32)


def add_rows(target, begin, update):
    current = lax.dynamic_slice_in_dim(target, begin, update.shape[0], 0)
    return lax.dynamic_update_slice_in_dim(target, current + update, begin, 0)


def attend(query_blocks, grad_blocks, local_keys, local_values, remote_keys, remote_values, allowed):
    scale = HEAD_DIM ** -0.5
    query_heads = split_heads(query_blocks)
    grad_heads = split_heads(grad_blocks)
    key_local = split_heads(local_keys)
    value_local = split_heads(local_values)
    key_remote = split_heads(remote_keys)
    value_remote = split_heads(remote_values)
    local_scores = product("bqhd,khd->bhqk", query_heads, key_local) * scale
    local_scores = jnp.where(allowed[:, None, None, :], local_scores, -1e30)
    remote_scores = product("bqhd,bkhd->bhqk", query_heads, key_remote) * scale
    scores = jnp.concatenate([local_scores, remote_scores], axis=3)
    highest = jnp.max(scores, axis=3, keepdims=True)
    exponent = jnp.exp(scores - highest)
    total = jnp.sum(exponent, axis=3, keepdims=True)
    attn_probs = exponent / total
    probs_low = attn_probs.astype(jnp.bfloat16)
    prob_grad = jnp.concatenate([product("bqhd,khd->bhqk", grad_heads, value_local),
                                 product("bqhd,bkhd->bhqk", grad_heads, value_remote)], axis=3)
    inner = jnp.sum(attn_probs * prob_grad, axis=3, keepdims=True)
    score_grad = (attn_probs * (prob_grad - inner) * scale).astype(jnp.bfloat16)
    local_count = local_keys.shape[0]
    grad_local, grad_remote = score_grad[..., :local_count], score_grad[..., local_count:]
    low_local, low_remote = probs_low[..., :local_count], probs_low[..., local_count:]
    grad_query = join_heads(product("bhqk,khd->bqhd", grad_local, key_local)
                            + product("bhqk,bkhd->bqhd", grad_remote, key_remote))
    grad_key = join_heads(product("bhqk,bqhd->khd", grad_local, query_heads))
    grad_value = join_heads(product("bhqk,bqhd->khd", low_local, grad_heads))
    key_back = join_heads(product("bhqk,bqhd->bkhd", grad_remote, query_heads))
    value_back = join_heads(product("bhqk,bqhd->bkhd", low_remote, grad_heads))
    return grad_query, grad_key, grad_value, key_back, value_back


def reference(node_features, cotangent, proj_weights, local_mask, matching):
    parts_count = BLOCKS // BLK_DEV
    row_count = BLK_DEV * BLOCK
    feat_width = node_features.shape[1]
    query_rows = jnp.dot(node_features, proj_weights[:, 0, :], preferred_element_type=jnp.float32).astype(jnp.bfloat16)
    key_rows = jnp.dot(node_features, proj_weights[:, 1, :], preferred_element_type=jnp.float32).astype(jnp.bfloat16)
    value_rows = jnp.dot(node_features, proj_weights[:, 2, :], preferred_element_type=jnp.float32).astype(jnp.bfloat16)
    out_grad = jnp.dot(cotangent, proj_weights[:, 3, :], preferred_element_type=jnp.float32).astype(jnp.bfloat16)
    offsets = round_offsets(parts_count)
    diagonal_mask = jnp.eye(BLK_DEV, dtype=bool)

    def rows_at(array, begin):
        return lax.dynamic_slice_in_dim(array, begin, row_count, 0)

    def device_step(carry, device):
        key_total, value_total = carry
        begin = device * row_count
        mask_rows = lax.dynamic_slice_in_dim(local_mask, device * BLK_DEV, BLK_DEV, 0)
        allowed = jnp.repeat((mask_rows > 0) | diagonal_mask, BLOCK, axis=1)
        orders = lax.dynamic_slice_in_dim(matching, device * BLK_DEV, BLK_DEV, 1)
        sources = [((device - shift) % parts_count) * row_count for shift in offsets]
        remote_keys = jnp.concatenate(
            [rows_at(key_rows, sources[index]).reshape(BLK_DEV, BLOCK, feat_width)[orders[index]] for index in range(ROUNDS)], axis=1)
        remote_values = jnp.concatenate(
            [rows_at(value_rows, sources[index]).reshape(BLK_DEV, BLOCK, feat_width)[orders[index]] for index in range(ROUNDS)], axis=1)
        grad_query, grad_key, grad_value, key_back, value_back = attend(
            rows_at(query_rows, begin).reshape(BLK_DEV, BLOCK, feat_width),
            rows_at(out_grad, begin).reshape(BLK_DEV, BLOCK, feat_width),
            rows_at(key_rows, begin), rows_at(value_rows, begin), remote_keys, remote_values, allowed)
        key_total = add_rows(key_total, begin, grad_key)
        value_total = add_rows(value_total, begin, grad_value)
        for index in range(ROUNDS):
            lower = index * BLOCK
            key_total = add_rows(key_total, sources[index],
                                 rounded(place(key_back[:, lower:lower + BLOCK], orders[index]).reshape(row_count, feat_width)))
            value_total = add_rows(value_total, sources[index],
                                   rounded(place(value_back[:, lower:lower + BLOCK], orders[index]).reshape(row_count, feat_width)))
        return (key_total, value_total), grad_query.reshape(row_count, feat_width)

    empty = jnp.zeros((BLOCKS * BLOCK, feat_width), jnp.float32)
    (key_total, value_total), query_total = lax.scan(device_step, (empty, empty), jnp.arange(parts_count, dtype=jnp.int32))
    grad_query = query_total.reshape(BLOCKS * BLOCK, feat_width).astype(jnp.bfloat16)
    grad_key = key_total.astype(jnp.bfloat16)
    grad_value = value_total.astype(jnp.bfloat16)
    grads = (grad_query, grad_key, grad_value)
    group = feat_width // N_HEAD
    input_total = jnp.zeros((BLOCKS * BLOCK, feat_width), jnp.float32)
    for column_group in range(N_HEAD):
        lower = column_group * group
        head_partial = jnp.zeros((BLOCKS * BLOCK, feat_width), jnp.float32)
        for index in range(3):
            head_partial = head_partial + lax.dot_general(
                grads[index][:, lower:lower + group], proj_weights[:, index, lower:lower + group],
                (((1,), (1,)), ((), ())), preferred_element_type=jnp.float32)
        input_total = input_total + head_partial.astype(jnp.bfloat16).astype(jnp.float32)
    input_grad = input_total.astype(jnp.bfloat16)
    weight_grads = jnp.stack([jnp.dot(node_features.T, gradient, preferred_element_type=jnp.float32) for gradient in grads], axis=1)
    return input_grad, weight_grads
```

```python
import jax
import jax.numpy as jnp
from jax import lax
from jax.sharding import Mesh
from jax.sharding import PartitionSpec as P

HEAD_DIM = 64
BLOCK = 128
ROUNDS = 3
Y, XL, Z, XH, CORE = 4, 2, 16, 2, 2
AXES = ("y", "xl", "z", "xh", "core")
RING = ("xl", "z")
RING_SIZE = XL * Z
F32 = jnp.float32
BF16 = jnp.bfloat16


def product(form, left, right):
    return jnp.einsum(form, left, right, preferred_element_type=F32)


def swapped(block, axis):
    return lax.ppermute(block, axis, [(0, 1), (1, 0)])


def shifted(block, distance):
    route = [(i, (i + distance) % RING_SIZE) for i in range(RING_SIZE)]
    return lax.ppermute(block, RING, route)


def attend(query, out_grad, keys, values, allowed):
    scale = HEAD_DIM ** (-0.5)
    scores = product("bqd,bkd->bqk", query, keys) * scale
    scores = jnp.where(allowed, scores, -1e30)
    highest = jnp.max(scores, axis=2, keepdims=True)
    exponent = jnp.exp(scores - highest)
    total = jnp.sum(exponent, axis=2, keepdims=True)
    attn_probs = exponent / total
    probs_low = attn_probs.astype(BF16)
    prob_grad = product("bqd,bkd->bqk", out_grad, values)
    inner = jnp.sum(attn_probs * prob_grad, axis=2, keepdims=True)
    score_grad = (attn_probs * (prob_grad - inner) * scale).astype(BF16)
    grad_query = product("bqk,bkd->bqd", score_grad, keys)
    key_side = product("bqk,bqd->bkd", score_grad, query)
    value_side = product("bqk,bqd->bkd", probs_low, out_grad)
    return grad_query, key_side, value_side


def shards(node_features, cotangent, proj_weights, local_mask, matching):
    y = lax.axis_index("y")
    xl = lax.axis_index("xl")
    z = lax.axis_index("z")
    xh = lax.axis_index("xh")
    core = lax.axis_index("core")
    ring_at = xl * Z + z
    head = xh * CORE + core

    packed = jnp.concatenate(
        [node_features, cotangent, proj_weights.reshape(32, 256)], axis=0
    )
    packed = lax.all_gather(packed, "y", axis=0)
    quarter = packed[:, :256]
    weight_y = packed[:, 256:].reshape(Y, 8, 4, Y, HEAD_DIM)
    weight_y = lax.dynamic_index_in_dim(weight_y, y, 3, keepdims=False)
    weight_y = weight_y.reshape(32, 256)

    other_core = swapped(quarter, "core")
    weights = jnp.concatenate(
        [weight_y, proj_weights[:, :3].reshape(24, 256)], axis=0
    )
    weights = lax.all_gather(weights, "xl", axis=0)
    weights, other_core = lax.optimization_barrier((weights, other_core))
    halves = jnp.stack([quarter, other_core])
    other_half = swapped(halves, "xh")
    weights = lax.all_gather(weights, "z", axis=0)

    first = weights[:, :, :32].reshape(Z, XL, XH, CORE, 8, 256)
    first = first.transpose(2, 3, 1, 0, 4, 5).reshape(XH, CORE, 256, 256)
    first = jnp.where(core == 0, first, first[:, ::-1])
    first = jnp.where(xh == 0, first, first[::-1])
    first = first.reshape(1024, 256)
    second = weights[:, :, 32:].reshape(Z, XL, 8, 768)
    second = second.transpose(1, 0, 2, 3).reshape(256, 768)

    pieces = jnp.concatenate([halves, other_half], axis=0)
    features = pieces[:, :, :BLOCK].reshape(4, 512, 256)
    cotangents = pieces[:, :, BLOCK:].reshape(4, 512, 256)
    feature_rows = features.transpose(1, 0, 2).reshape(512, 1024)
    cotangent_rows = cotangents.transpose(1, 0, 2).reshape(512, 1024)
    own_features = lax.dynamic_index_in_dim(features, head ^ y, 0, keepdims=False)

    key_value = jnp.dot(
        feature_rows, first[:, 64:192], preferred_element_type=F32
    ).astype(BF16)
    arrived = shifted(key_value, 1)
    query = jnp.dot(feature_rows, first[:, :64], preferred_element_type=F32).astype(BF16)
    out_grad = jnp.dot(cotangent_rows, first[:, 192:], preferred_element_type=F32).astype(
        BF16
    )
    query = query.reshape(Y, BLOCK, HEAD_DIM)
    out_grad = out_grad.reshape(Y, BLOCK, HEAD_DIM)
    key_value = key_value.reshape(Y, BLOCK, 2 * HEAD_DIM)
    arrived = arrived.reshape(Y, BLOCK, 2 * HEAD_DIM)
    arrived = jnp.where(ring_at == 0, jnp.roll(arrived, 1, axis=0), arrived)
    listed = jnp.concatenate(
        [key_value] + [jnp.roll(arrived, r, axis=0) for r in range(ROUNDS)], axis=1
    )
    mask = lax.all_gather(local_mask, "y", axis=0).reshape(Y, 1)
    usable = jnp.repeat((mask > 0) | jnp.eye(1, dtype=bool), BLOCK, axis=1)
    usable = jnp.concatenate([usable, jnp.ones((Y, ROUNDS * BLOCK), bool)], axis=1)
    grad_query, key_side, value_side = attend(
        query,
        out_grad,
        listed[..., :HEAD_DIM],
        listed[..., HEAD_DIM:],
        usable[:, None, :],
    )
    both = jnp.concatenate([key_side, value_side], axis=2)
    back = 0.0
    for r in range(ROUNDS):
        lower = (1 + r) * BLOCK
        part = both[:, lower : lower + BLOCK].astype(BF16).astype(F32)
        back = back + jnp.roll(part, -r, axis=0)
    back = jnp.where(ring_at == 0, jnp.roll(back, -1, axis=0), back)
    both = (both[:, :BLOCK] + shifted(back, -1)).astype(BF16)
    grads = jnp.concatenate([grad_query.astype(BF16), both], axis=2)
    grads = lax.all_gather(grads.reshape(512, 192), "y", axis=0)
    grads = grads.reshape(Y, 512, 3, HEAD_DIM).transpose(1, 2, 0, 3).reshape(512, 768)

    term = lax.dot_general(
        own_features, grads, (((0,), (0,)), ((), ())), preferred_element_type=F32
    ).reshape(XL, 128, 768)
    kept = lax.dynamic_index_in_dim(term, xl, 0, keepdims=False)
    sent = lax.dynamic_index_in_dim(term, 1 - xl, 0, keepdims=False)
    other = swapped(sent, "xl")

    partial = lax.dot_general(
        grads, second, (((1,), (1,)), ((), ())), preferred_element_type=F32
    ).astype(BF16)
    partial = lax.all_to_all(partial, ("xh", "core"), 0, 0, tiled=True)
    partial, other = lax.optimization_barrier((partial, other))
    total = jnp.sum(partial.reshape(4, BLOCK, 256).astype(F32), axis=0).astype(BF16)
    route = [(a * 4 + b, b * 4 + a) for a in range(4) for b in range(4)]
    input_grad = lax.ppermute(total, ("y", "xh", "core"), route)

    term = kept + other
    term = lax.all_to_all(term, "z", 0, 0, tiled=True)
    term = jnp.sum(term.reshape(Z, 8, 768), axis=0)
    weight_grads = term.reshape(8, 3, 256)
    return (input_grad, weight_grads)


def solution(mesh):
    fine = Mesh(mesh.devices.reshape(Y, XL, Z, XH, CORE), AXES)
    dom = ("y", "xl", "z")
    head = ("xh", "core")
    return jax.shard_map(
        shards,
        mesh=fine,
        in_specs=(
            P(dom, head),
            P(dom, head),
            P(dom, None, head),
            P(dom, None),
            P(None, dom),
        ),
        out_specs=(P(dom, head), P(dom, None, head)),
        check_vma=False,
    )
```

```python
import jax
import jax.numpy as jnp
from jax import lax
from jax.experimental import pallas as pl
from jax.experimental.pallas import tpu as pltpu
from jax.sharding import Mesh
from jax.sharding import PartitionSpec as P

HEAD_DIM = 64
BLOCK = 128
ROUNDS = 3
Y, XL, Z, XH, CORE = 4, 2, 16, 2, 2
AXES = ("y", "xl", "z", "xh", "core")
DOM = ("y", "xl", "z")
RING = ("xl", "z")
RING_SIZE = XL * Z
F32 = jnp.float32
BF16 = jnp.bfloat16
SMEM = pl.BlockSpec(memory_space=pltpu.SMEM)
VMEM = pl.BlockSpec(memory_space=pltpu.VMEM)


def swapped(block, axis):
    return lax.ppermute(block, axis, [(0, 1), (1, 0)])


def shifted(block, distance):
    route = [(i, (i + distance) % RING_SIZE) for i in range(RING_SIZE)]
    return lax.ppermute(block, RING, route)


def matmul(left, right, dims):
    return lax.dot_general(left, right, (dims, ((), ())), preferred_element_type=F32)


def low_lanes(shape):
    return lax.broadcasted_iota(jnp.int32, shape, len(shape) - 1) < HEAD_DIM


def kernel_call(kernel, shapes, specs, flops, size, args):
    return pl.pallas_call(
        kernel,
        out_shape=shapes,
        in_specs=specs,
        out_specs=[VMEM] * len(shapes),
        compiler_params=pltpu.CompilerParams(vmem_limit_bytes=16 * 1024 * 1024),
        cost_estimate=pl.CostEstimate(flops=flops, bytes_accessed=size, transcendentals=0),
    )(*args)


def project_features(order, p0, p1, p2, p3, weights, key_value, query):
    total = jnp.zeros((Y * BLOCK, 256), F32)
    for index, piece in enumerate((p0, p1, p2, p3)):
        rows = weights[pl.ds(order[index] * 256, 256), :]
        total += matmul(piece[:, :BLOCK].reshape(Y * BLOCK, 256), rows, ((1,), (0,)))
    key_value[...] = total[:, :BLOCK].astype(BF16)
    query[...] = total[:, BLOCK:].astype(BF16)


def project_cotangents(order, p0, p1, p2, p3, weights, query, both):
    total = jnp.zeros((Y * BLOCK, BLOCK), F32)
    for index, piece in enumerate((p0, p1, p2, p3)):
        rows = weights[pl.ds(order[index] * 256, 256), BLOCK:]
        total += matmul(piece[:, BLOCK:].reshape(Y * BLOCK, 256), rows, ((1,), (0,)))
    low = low_lanes((Y * BLOCK, BLOCK))
    both[...] = jnp.where(low, query[...], total.astype(BF16))


def attend(scalars, both, own, arrived, local, back, grad_query):
    scale = HEAD_DIM ** (-0.5)
    low = low_lanes((BLOCK, BLOCK))
    zero = jnp.zeros((BLOCK, BLOCK), BF16)
    wrap = scalars[0]
    back[...] = jnp.zeros((Y, BLOCK, BLOCK), F32)
    for block in range(Y):
        pair = both[block]
        stacked = jnp.concatenate(
            [jnp.where(low, pair, zero), jnp.where(low, zero, pair)], axis=0
        )
        sources = [lax.rem(block - r - wrap + 2 * Y, Y) for r in range(ROUNDS)]
        listed = jnp.concatenate([own[block]] + [arrived[s] for s in sources], axis=0)
        inner = matmul(stacked, listed, ((1,), (1,)))
        scores = inner[:BLOCK] * scale
        prob_grad = inner[BLOCK:]
        usable = scalars[1 + block] > 0
        local_scores = jnp.where(usable, scores[:, :BLOCK], -1e30)
        scores = jnp.concatenate([local_scores, scores[:, BLOCK:]], axis=1)
        exponent = jnp.exp(scores - jnp.max(scores, axis=1, keepdims=True))
        total = jnp.sum(exponent, axis=1, keepdims=True)
        probs = exponent * (1.0 / total)
        mean = jnp.sum(probs * prob_grad, axis=1, keepdims=True)
        score_grad = (probs * (prob_grad - mean) * scale).astype(BF16)
        query_side = matmul(score_grad, listed, ((1,), (0,)))
        grad_query[block] = jnp.where(low, query_side, 0.0).astype(BF16)
        terms = jnp.concatenate([score_grad, probs.astype(BF16)], axis=0)
        key_side = matmul(terms, stacked, ((0,), (0,)))
        local[block] = key_side[:BLOCK]
        for r in range(ROUNDS):
            lower = (1 + r) * BLOCK
            part = key_side[lower : lower + BLOCK].astype(BF16).astype(F32)
            back[sources[r]] += part


def weight_terms(order, p0, p1, p2, p3, local, returned, grad_query, term, grads):
    sides = (local[...] + returned[...]).astype(BF16)
    both = jnp.concatenate([sides, grad_query[...]], axis=2)
    for block in range(Y):
        grads[block] = both[block, :, : 3 * HEAD_DIM].T
    both = both.reshape(Y * BLOCK, 256)
    for index, piece in enumerate((p0, p1, p2, p3)):
        rows = piece[:, :BLOCK].reshape(Y * BLOCK, 256)
        product = matmul(rows, both, ((0,), (0,)))
        term[pl.ds(order[index] * 256, 256), :] = product.astype(BF16)


def input_terms(place, grads, weights, ours, theirs):
    own, core = place[0], place[1]
    for half in range(XH):
        for out, side in ((ours, core), (theirs, 1 - core)):
            total = jnp.zeros((BLOCK, 256), F32)
            lower = (half * CORE + side) * 256
            for source in range(Y):
                rows = weights[source, pl.ds(lower, 256), :HEAD_DIM * 3]
                left = grads[source, own]
                total += matmul(left, rows, ((0,), (1,)))
            out[half] = total.astype(BF16)


def sum_weight_terms(terms, out):
    sums = [
        jnp.sum(terms[s * RING_SIZE : (s + 1) * RING_SIZE].astype(F32), axis=0)
        for s in range(Y)
    ]
    for place, lower in ((1, 0), (2, HEAD_DIM), (0, 2 * HEAD_DIM)):
        out[place] = jnp.concatenate(
            [part[:, lower : lower + HEAD_DIM] for part in sums], axis=1
        )


def shards(node_features, cotangent, proj_weights, local_mask, matching):
    xl = lax.axis_index("xl")
    z = lax.axis_index("z")
    xh = lax.axis_index("xh")
    core = lax.axis_index("core")
    head = xh * CORE + core
    place = jnp.stack([lax.axis_index("y"), core]).astype(jnp.int32)
    order = jnp.stack([head, head ^ 2, head ^ 1, head ^ 3]).astype(jnp.int32)

    rows = jnp.concatenate([proj_weights[:, 1:3], proj_weights[:, :1], proj_weights[:, 3:]], 1)
    rows = rows.reshape(8, 4, Y, HEAD_DIM).transpose(2, 0, 1, 3)
    rows = jnp.broadcast_to(rows.reshape(Y, 1, 8, 256), (Y, RING_SIZE, 8, 256))
    packed = jnp.concatenate([node_features, cotangent], axis=0)
    rows, packed = lax.optimization_barrier((rows, packed))
    weights = lax.all_to_all(rows.reshape(1024, 256), DOM, 0, 0, tiled=True)

    p0 = lax.all_gather(packed, "y", axis=0)
    p1 = swapped(p0, "xh")
    p2 = swapped(p0, "core")
    p3 = swapped(p1, "core")
    weights, p2, p3 = lax.optimization_barrier((weights, p2, p3))
    pieces = (p0, p1, p2, p3)

    key_value, query = kernel_call(
        project_features,
        [jax.ShapeDtypeStruct((512, BLOCK), BF16)] * 2,
        [SMEM] + [VMEM] * 5,
        2 * 512 * 1024 * 256,
        2000000,
        (order, *pieces, weights),
    )
    arrived = shifted(key_value, 1)
    (both,) = kernel_call(
        project_cotangents,
        [jax.ShapeDtypeStruct((512, BLOCK), BF16)],
        [SMEM] + [VMEM] * 6,
        2 * 512 * 1024 * 128,
        2000000,
        (order, *pieces, weights, query),
    )
    spread = jnp.broadcast_to(weights[None], (Y, 1024, 256))
    group_weights = lax.all_to_all(spread, "y", 0, 0, tiled=False)

    mask = lax.all_gather(local_mask, "y", axis=0).reshape(Y, 1)
    usable = (mask > 0) | jnp.eye(1, dtype=bool)
    wrap = (xl * Z + z == 0).reshape(1)
    scalars = jnp.concatenate([wrap, usable.reshape(Y)]).astype(jnp.int32)
    shape = (Y, BLOCK, BLOCK)
    local, back, grad_query = kernel_call(
        attend,
        [
            jax.ShapeDtypeStruct(shape, F32),
            jax.ShapeDtypeStruct(shape, F32),
            jax.ShapeDtypeStruct(shape, BF16),
        ],
        [SMEM] + [VMEM] * 3,
        4 * 6 * 256 * 512 * 128,
        1000000,
        (scalars, both.reshape(shape), key_value.reshape(shape), arrived.reshape(shape)),
    )
    returned = shifted(back, -1)
    returned, group_weights = lax.optimization_barrier((returned, group_weights))

    term, grads = kernel_call(
        weight_terms,
        [
            jax.ShapeDtypeStruct((1024, 256), BF16),
            jax.ShapeDtypeStruct((Y, 192, BLOCK), BF16),
        ],
        [SMEM] + [VMEM] * 7,
        2 * 512 * 1024 * 256,
        2000000,
        (order, *pieces, local, returned, grad_query),
    )
    term = lax.all_to_all(term, DOM, 0, 0, tiled=True)

    grads = lax.all_gather(grads, "y", axis=0)
    ours, theirs = kernel_call(
        input_terms,
        [jax.ShapeDtypeStruct((2, BLOCK, 256), BF16)] * 2,
        [SMEM] + [VMEM] * 2,
        2 * 128 * 1024 * 1024,
        2500000,
        (place, grads, group_weights),
    )
    pair = ours.astype(F32) + swapped(theirs, "core").astype(F32)
    other = swapped(lax.dynamic_index_in_dim(pair, 1 - xh, 0, keepdims=False), "xh")
    pair = lax.dynamic_index_in_dim(pair, xh, 0, keepdims=False)
    input_grad = (pair + other).astype(BF16)

    (weight_grads,) = kernel_call(
        sum_weight_terms,
        [jax.ShapeDtypeStruct((3, 8, 256), F32)],
        [VMEM],
        1000000,
        600000,
        (term.reshape(128, 8, 256),),
    )
    return (input_grad, weight_grads.transpose(1, 0, 2))


def solution(mesh):
    fine = Mesh(mesh.devices.reshape(Y, XL, Z, XH, CORE), AXES)
    head = ("xh", "core")
    return jax.shard_map(
        shards,
        mesh=fine,
        in_specs=(
            P(DOM, head),
            P(DOM, head),
            P(DOM, None, head),
            P(DOM, None),
            P(None, DOM),
        ),
        out_specs=(P(DOM, head), P(DOM, None, head)),
        check_vma=False,
    )
```

```python
import jax
import jax.numpy as jnp
from jax import lax
from jax.experimental import pallas as pl
from jax.experimental.pallas import tpu as pltpu
from jax.sharding import Mesh
from jax.sharding import PartitionSpec as P

HEAD_DIM = 64
BLOCK = 128
ROUNDS = 3
Y, XL, Z, XH, CORE = 4, 2, 16, 2, 2
AXES = ("y", "xl", "z", "xh", "core")
DOM = ("y", "xl", "z")
RING = ("xl", "z")
RING_SIZE = XL * Z
F32 = jnp.float32
BF16 = jnp.bfloat16
SMEM = pl.BlockSpec(memory_space=pltpu.SMEM)
VMEM = pl.BlockSpec(memory_space=pltpu.VMEM)
ANY = pl.BlockSpec(memory_space=pl.ANY)


def swapped(block, axis):
    return lax.ppermute(block, axis, [(0, 1), (1, 0)])


def shifted(block, distance):
    route = [(i, (i + distance) % RING_SIZE) for i in range(RING_SIZE)]
    return lax.ppermute(block, RING, route)


def matmul(left, right, dims):
    return lax.dot_general(left, right, (dims, ((), ())), preferred_element_type=F32)


def low_lanes(shape):
    return lax.broadcasted_iota(jnp.int32, shape, len(shape) - 1) < HEAD_DIM


def kernel_call(kernel, shapes, specs, flops, size, args, scratch=()):
    return pl.pallas_call(
        kernel,
        out_shape=[jax.ShapeDtypeStruct(shape, dtype) for shape, dtype in shapes],
        in_specs=specs,
        out_specs=[VMEM] * len(shapes),
        scratch_shapes=list(scratch),
        compiler_params=pltpu.CompilerParams(vmem_limit_bytes=16 * 1024 * 1024),
        cost_estimate=pl.CostEstimate(flops=flops, bytes_accessed=size, transcendentals=0),
    )(*args)


FETCHED = (pltpu.VMEM((4, Y, BLOCK, 256), BF16), pltpu.SemaphoreType.DMA((4,)))


def fetch(pieces, lower, held, arrivals):
    copies = [
        pltpu.make_async_copy(
            piece.at[:, pl.ds(lower, BLOCK), :], held.at[index], arrivals.at[index]
        )
        for index, piece in enumerate(pieces)
    ]
    for copy in copies:
        copy.start()
    return copies


def pack(features, cotangents, weights, packed, rows):
    packed[:BLOCK] = features[...]
    packed[BLOCK:] = cotangents[...]
    for quarter in range(Y):
        lower = quarter * HEAD_DIM
        part = jnp.concatenate(
            [weights[:, t, lower : lower + HEAD_DIM] for t in (1, 2, 0, 3)], axis=1
        )
        rows[quarter] = jnp.broadcast_to(part[None], (Z, 8, 256))


def project_features(
    scalars, p0, p1, p2, p3, near, far, key_value, query, weights, held, arrivals
):
    copies = fetch((p0, p1, p2, p3), 0, held, arrivals)
    first = scalars[4] == 0
    weights[:, 0] = jnp.where(first, near[...], far[...])
    weights[:, 1] = jnp.where(first, far[...], near[...])
    total = jnp.zeros((Y * BLOCK, 256), F32)
    for index in range(4):
        copies[index].wait()
        rows = weights[scalars[index]].reshape(256, 256)
        total += matmul(held[index].reshape(Y * BLOCK, 256), rows, ((1,), (0,)))
    key_value[...] = total[:, :BLOCK].astype(BF16)
    query[...] = total[:, BLOCK:].astype(BF16)


def project_cotangents(scalars, p0, p1, p2, p3, weights, query, both, held, arrivals):
    copies = fetch((p0, p1, p2, p3), BLOCK, held, arrivals)
    total = jnp.zeros((Y * BLOCK, BLOCK), F32)
    for index in range(4):
        copies[index].wait()
        rows = weights[scalars[index]].reshape(256, 256)[:, BLOCK:]
        total += matmul(held[index].reshape(Y * BLOCK, 256), rows, ((1,), (0,)))
    low = low_lanes((Y * BLOCK, BLOCK))
    both[...] = jnp.where(low, query[...], total.astype(BF16))


def attend(scalars, both, own, arrived, local, back, grad_query):
    scale = HEAD_DIM ** (-0.5)
    low = low_lanes((BLOCK, BLOCK))
    zero = jnp.zeros((BLOCK, BLOCK), BF16)
    wrap = scalars[0]
    back[...] = jnp.zeros((Y, BLOCK, BLOCK), F32)
    for block in range(Y):
        pair = both[block]
        stacked = jnp.concatenate(
            [jnp.where(low, pair, zero), jnp.where(low, zero, pair)], axis=0
        )
        sources = [lax.rem(block + r + wrap, Y) for r in range(ROUNDS)]
        listed = jnp.concatenate([own[block]] + [arrived[s] for s in sources], axis=0)
        inner = matmul(stacked, listed, ((1,), (1,)))
        scores = inner[:BLOCK] * scale
        prob_grad = inner[BLOCK:]
        usable = scalars[1 + block] > 0
        local_scores = jnp.where(usable, scores[:, :BLOCK], -1e30)
        scores = jnp.concatenate([local_scores, scores[:, BLOCK:]], axis=1)
        exponent = jnp.exp(scores - jnp.max(scores, axis=1, keepdims=True))
        total = jnp.sum(exponent, axis=1, keepdims=True)
        probs = exponent * (1.0 / total)
        mean = jnp.sum(probs * prob_grad, axis=1, keepdims=True)
        score_grad = (probs * (prob_grad - mean) * scale).astype(BF16)
        query_side = matmul(score_grad, listed, ((1,), (0,)))
        grad_query[block] = jnp.where(low, query_side, 0.0).astype(BF16)
        terms = jnp.concatenate([score_grad, probs.astype(BF16)], axis=0)
        key_side = matmul(terms, stacked, ((0,), (0,)))
        local[block] = key_side[:BLOCK]
        for r in range(ROUNDS):
            lower = (1 + r) * BLOCK
            part = key_side[lower : lower + BLOCK].astype(BF16).astype(F32)
            back[sources[r]] += part


def weight_terms(
    scalars, p0, p1, p2, p3, local, returned, grad_query, kept, sent, grads, held, arrivals
):
    copies = fetch((p0, p1, p2, p3), 0, held, arrivals)
    sides = (local[...] + returned[...]).astype(BF16)
    both = jnp.concatenate([sides, grad_query[...]], axis=2)
    for slot in range(Y):
        block = lax.rem(scalars[5] + (Y - slot), Y)
        grads[block] = both[slot, :, : 3 * HEAD_DIM].T
    both = both.reshape(Y * BLOCK, 256)
    first = scalars[4] == 0
    for index in range(4):
        copies[index].wait()
        rows = held[index].reshape(Y * BLOCK, 256)
        product = matmul(rows, both, ((0,), (0,)))
        quarter = scalars[index]
        kept[quarter] = jnp.where(first, product[:BLOCK], product[BLOCK:])
        sent[quarter] = jnp.where(first, product[BLOCK:], product[:BLOCK]).astype(BF16)


def input_terms(scalars, grads, w0, w1, w2, w3, ours, theirs):
    core = scalars[6]
    for half in range(XH):
        for out, side in ((ours, core), (theirs, 1 - core)):
            total = jnp.zeros((BLOCK, 256), F32)
            for slot, weights in enumerate((w0, w1, w2, w3)):
                rows = weights[half * CORE + side].reshape(256, 256)[:, : 3 * HEAD_DIM]
                left = grads[lax.rem(scalars[5] + slot, Y)]
                total += matmul(left, rows, ((0,), (1,)))
            out[half] = total.astype(BF16)


def sum_weight_terms(terms, out):
    sums = [
        jnp.sum(terms[s * Z : (s + 1) * Z].astype(F32), axis=0)
        for s in range(Y)
    ]
    for place, lower in ((1, 0), (2, HEAD_DIM), (0, 2 * HEAD_DIM)):
        out[place] = jnp.concatenate(
            [part[:, lower : lower + HEAD_DIM] for part in sums], axis=1
        )


def shards(node_features, cotangent, proj_weights, local_mask, matching):
    y = lax.axis_index("y")
    xl = lax.axis_index("xl")
    z = lax.axis_index("z")
    xh = lax.axis_index("xh")
    core = lax.axis_index("core")
    head = xh * CORE + core
    scalars = jnp.stack([head, head ^ 2, head ^ 1, head ^ 3, xl, y, core]).astype(jnp.int32)

    packed, rows = kernel_call(
        pack,
        [((2 * BLOCK, 256), BF16), ((Y, Z, 8, 256), BF16)],
        [VMEM] * 3,
        1000,
        600000,
        (node_features, cotangent, proj_weights),
    )
    slots = [packed] + [
        lax.ppermute(packed, "y", [(i, (i + k) % Y) for i in range(Y)]) for k in range(1, Y)
    ]
    near = lax.all_to_all(rows.reshape(512, 256), ("y", "z"), 0, 0, tiled=True)
    near = near.reshape(Y, BLOCK, 256)

    p0 = jnp.stack(slots)
    p1 = swapped(p0, "xh")
    p2 = swapped(p0, "core")
    far = swapped(near, "xl")
    p3 = swapped(p1, "core")
    pieces = (p0, p1, p2, p3)

    shape = (Y, BLOCK, BLOCK)
    key_value, query, weights = kernel_call(
        project_features,
        [((512, BLOCK), BF16), ((512, BLOCK), BF16), ((4, XL, BLOCK, 256), BF16)],
        [SMEM] + [ANY] * 4 + [VMEM] * 2,
        2 * 512 * 1024 * 256,
        2000000,
        (scalars, *pieces, near, far),
        FETCHED,
    )
    arrived = shifted(key_value, 1)
    (both,) = kernel_call(
        project_cotangents,
        [((512, BLOCK), BF16)],
        [SMEM] + [ANY] * 4 + [VMEM] * 2,
        2 * 512 * 1024 * 128,
        2000000,
        (scalars, *pieces, weights, query),
        FETCHED,
    )
    group_weights = [weights] + [
        lax.ppermute(weights, "y", [(i, (i - k) % Y) for i in range(Y)]) for k in range(1, Y)
    ]

    mask = lax.all_gather(local_mask, "y", axis=0).reshape(Y, 1)
    usable = (mask > 0) | jnp.eye(1, dtype=bool)
    wrap = (xl * Z + z == 0).reshape(1)
    flags = jnp.concatenate([wrap, usable.reshape(Y)]).astype(jnp.int32)
    local, back, grad_query = kernel_call(
        attend,
        [(shape, F32), (shape, F32), (shape, BF16)],
        [SMEM] + [VMEM] * 3,
        4 * 6 * 256 * 512 * 128,
        1000000,
        (flags, both.reshape(shape), key_value.reshape(shape), arrived.reshape(shape)),
    )
    returned = shifted(back, -1)

    kept, sent, grads = kernel_call(
        weight_terms,
        [((Y, BLOCK, 256), F32), ((Y, BLOCK, 256), BF16), ((Y, 192, BLOCK), BF16)],
        [SMEM] + [ANY] * 4 + [VMEM] * 3,
        2 * 512 * 1024 * 256,
        2000000,
        (scalars, *pieces, local, returned, grad_query),
        FETCHED,
    )
    other = swapped(sent, "xl")
    grads = lax.all_to_all(grads, "y", 0, 0, tiled=False)
    grads, other = lax.optimization_barrier((grads, other))
    term = (kept + other.astype(F32)).astype(BF16)
    term = lax.all_to_all(term.reshape(512, 256), ("y", "z"), 0, 0, tiled=True)
    ours, theirs = kernel_call(
        input_terms,
        [((2, BLOCK, 256), BF16)] * 2,
        [SMEM] + [VMEM] * 5,
        2 * 128 * 1024 * 1024,
        2500000,
        (scalars, grads, *group_weights),
    )
    pair = ours.astype(F32) + swapped(theirs, "core").astype(F32)
    remote = swapped(lax.dynamic_index_in_dim(pair, 1 - xh, 0, keepdims=False), "xh")
    pair = lax.dynamic_index_in_dim(pair, xh, 0, keepdims=False)
    input_grad = (pair + remote).astype(BF16)

    (weight_grads,) = kernel_call(
        sum_weight_terms,
        [((3, 8, 256), F32)],
        [VMEM],
        1000000,
        600000,
        (term.reshape(Y * Z, 8, 256),),
    )
    return (input_grad, weight_grads.transpose(1, 0, 2))


def solution(mesh):
    fine = Mesh(mesh.devices.reshape(Y, XL, Z, XH, CORE), AXES)
    head = ("xh", "core")
    return jax.shard_map(
        shards,
        mesh=fine,
        in_specs=(
            P(DOM, head),
            P(DOM, head),
            P(DOM, None, head),
            P(DOM, None),
            P(None, DOM),
        ),
        out_specs=(P(DOM, head), P(DOM, None, head)),
        check_vma=False,
    )
```

```python
import jax
import jax.numpy as jnp
from jax import lax
from jax.experimental import pallas as pl
from jax.experimental.pallas import tpu as pltpu
from jax.sharding import Mesh
from jax.sharding import PartitionSpec as P

HEAD_DIM = 64
BLOCK = 128
ROUNDS = 3
Y, XL, Z, XH, CORE = 4, 2, 16, 2, 2
AXES = ("y", "xl", "z", "xh", "core")
DOM = ("y", "xl", "z")
RING = ("xl", "z")
RING_SIZE = XL * Z
F32 = jnp.float32
BF16 = jnp.bfloat16
SMEM = pl.BlockSpec(memory_space=pltpu.SMEM)
VMEM = pl.BlockSpec(memory_space=pltpu.VMEM)
HBM = pl.BlockSpec(memory_space=pltpu.HBM)


def swapped(block, axis):
    return lax.ppermute(block, axis, [(0, 1), (1, 0)])


def passed(block, distance):
    return lax.ppermute(block, "y", [(i, (i + distance) % Y) for i in range(Y)])


def shifted(block, distance):
    route = [(i, (i + distance) % RING_SIZE) for i in range(RING_SIZE)]
    return lax.ppermute(block, RING, route)


def matmul(left, right, dims):
    return lax.dot_general(left, right, (dims, ((), ())), preferred_element_type=F32)


def low_lanes(shape):
    return lax.broadcasted_iota(jnp.int32, shape, len(shape) - 1) < HEAD_DIM


def kernel_call(kernel, shapes, specs, flops, size, args, scratch=(), limit=16):
    return pl.pallas_call(
        kernel,
        out_shape=[jax.ShapeDtypeStruct(shape, dtype) for shape, dtype in shapes],
        in_specs=specs,
        out_specs=[VMEM] * len(shapes),
        scratch_shapes=list(scratch),
        compiler_params=pltpu.CompilerParams(vmem_limit_bytes=limit * 1024 * 1024),
        cost_estimate=pl.CostEstimate(flops=flops, bytes_accessed=size, transcendentals=0),
    )(*args)


def pack(features, cotangents, weights, packed, rows, held, arrivals):
    copies = [
        pltpu.make_async_copy(weights, held, arrivals.at[0]),
        pltpu.make_async_copy(features, packed.at[pl.ds(0, BLOCK)], arrivals.at[1]),
        pltpu.make_async_copy(cotangents, packed.at[pl.ds(BLOCK, BLOCK)], arrivals.at[2]),
    ]
    for copy in copies:
        copy.start()
    copies[0].wait()
    for quarter in range(Y):
        lower = quarter * HEAD_DIM
        part = jnp.concatenate(
            [held[:, t, lower : lower + HEAD_DIM] for t in (1, 2, 0, 3)], axis=1
        )
        rows[:, quarter] = jnp.broadcast_to(part[None], (Z, 8, 256))
    copies[1].wait()
    copies[2].wait()


def spread(gathered, rows):
    for quarter in range(Y):
        part = gathered[:, quarter].reshape(BLOCK, 256)
        rows[quarter, 0] = part
        rows[quarter, 1] = part


def features_of(piece):
    return piece[:, :BLOCK].reshape(Y * BLOCK, 256)


def cotangents_of(piece):
    return piece[:, BLOCK:].reshape(Y * BLOCK, 256)


def project_features(scalars, p0, p1, p2, p3, weights, key_value, query):
    total = jnp.zeros((Y * BLOCK, 256), F32)
    for index, piece in enumerate((p0, p1, p2, p3)):
        rows = weights[scalars[index]]
        total += matmul(features_of(piece), rows, ((1,), (0,)))
    key_value[...] = total[:, :BLOCK].astype(BF16)
    query[...] = total[:, BLOCK:].astype(BF16)


def project_cotangents(scalars, p0, p1, p2, p3, weights, query, both):
    total = jnp.zeros((Y * BLOCK, BLOCK), F32)
    for index, piece in enumerate((p0, p1, p2, p3)):
        rows = weights[scalars[index], :, BLOCK:]
        total += matmul(cotangents_of(piece), rows, ((1,), (0,)))
    low = low_lanes((Y * BLOCK, BLOCK))
    both[...] = jnp.where(low, query[...], total.astype(BF16))


def attend(scalars, both, own, arrived, local, back, grad_query):
    scale = HEAD_DIM ** (-0.5)
    low = low_lanes((BLOCK, BLOCK))
    zero = jnp.zeros((BLOCK, BLOCK), BF16)
    wrap = scalars[0]
    back[...] = jnp.zeros((Y, BLOCK, BLOCK), F32)
    for block in range(Y):
        pair = both[block]
        stacked = jnp.concatenate(
            [jnp.where(low, pair, zero), jnp.where(low, zero, pair)], axis=0
        )
        sources = [lax.rem(block + r + wrap, Y) for r in range(ROUNDS)]
        listed = jnp.concatenate([own[block]] + [arrived[s] for s in sources], axis=0)
        inner = matmul(stacked, listed, ((1,), (1,)))
        scores = inner[:BLOCK] * scale
        prob_grad = inner[BLOCK:]
        usable = scalars[1 + block] > 0
        local_scores = jnp.where(usable, scores[:, :BLOCK], -1e30)
        scores = jnp.concatenate([local_scores, scores[:, BLOCK:]], axis=1)
        exponent = jnp.exp(scores - jnp.max(scores, axis=1, keepdims=True))
        total = jnp.sum(exponent, axis=1, keepdims=True)
        probs = exponent * (1.0 / total)
        mean = jnp.sum(probs * prob_grad, axis=1, keepdims=True)
        score_grad = (probs * (prob_grad - mean) * scale).astype(BF16)
        query_side = matmul(score_grad, listed, ((1,), (0,)))
        grad_query[block] = jnp.where(low, query_side, 0.0).astype(BF16)
        terms = jnp.concatenate([score_grad, probs.astype(BF16)], axis=0)
        key_side = matmul(terms, stacked, ((0,), (0,)))
        local[block] = key_side[:BLOCK]
        for r in range(ROUNDS):
            lower = (1 + r) * BLOCK
            part = key_side[lower : lower + BLOCK].astype(BF16).astype(F32)
            back[sources[r]] += part


def weight_terms(scalars, p0, p1, p2, p3, local, returned, grad_query, term, g0, g1, g2, g3):
    sides = (local[...] + returned[...]).astype(BF16)
    both = jnp.concatenate([sides, grad_query[...]], axis=2)
    for slot, grads in enumerate((g0, g1, g2, g3)):
        grads[...] = both[slot, :, : 3 * HEAD_DIM].T
    both = both.reshape(Y * BLOCK, 256)
    for index, piece in enumerate((p0, p1, p2, p3)):
        product = matmul(features_of(piece), both, ((0,), (0,)))
        term[scalars[index]] = product.astype(BF16)


def add_terms(terms, out):
    for source in range(Y):
        total = terms[XL * source].astype(F32) + terms[XL * source + 1].astype(F32)
        total = total.astype(BF16)
        for place, lower in ((1, 0), (2, HEAD_DIM), (0, 2 * HEAD_DIM)):
            at = place * 256 + source * HEAD_DIM
            out[:, at : at + HEAD_DIM] = total[:, lower : lower + HEAD_DIM]


def input_terms(scalars, g0, g1, g2, g3, w0, w1, w2, w3, ours, theirs):
    core = scalars[4]
    for half in range(XH):
        for out, side in ((ours, core), (theirs, 1 - core)):
            total = jnp.zeros((BLOCK, 256), F32)
            for grads, weights in ((g0, w0), (g1, w1), (g2, w2), (g3, w3)):
                rows = weights[half * CORE + side, :, : 3 * HEAD_DIM]
                total += matmul(grads[...], rows, ((0,), (1,)))
            out[half] = total.astype(BF16)


def sum_terms(terms, out):
    out[...] = jnp.sum(terms[...].astype(F32), axis=0)


def shards(node_features, cotangent, proj_weights, local_mask, matching):
    xl = lax.axis_index("xl")
    z = lax.axis_index("z")
    xh = lax.axis_index("xh")
    core = lax.axis_index("core")
    head = xh * CORE + core
    scalars = jnp.stack([head, head ^ 2, head ^ 1, head ^ 3, core]).astype(jnp.int32)

    packed, rows = kernel_call(
        pack,
        [((2 * BLOCK, 256), BF16), ((Z, Y, 8, 256), BF16)],
        [HBM] * 3,
        1000,
        600000,
        (node_features, cotangent, proj_weights),
        (pltpu.VMEM((8, 4, 256), BF16), pltpu.SemaphoreType.DMA((3,))),
        60,
    )
    rows = lax.all_to_all(rows, "z", 0, 0, tiled=True)
    slots = [packed] + [passed(packed, k) for k in range(1, Y)]
    (rows,) = kernel_call(
        spread, [((Y, XL, BLOCK, 256), BF16)], [VMEM], 1000, 800000, (rows,)
    )
    p0 = jnp.stack(slots)
    p1 = swapped(p0, "xh")
    p2 = swapped(p0, "core")
    weights = lax.all_to_all(
        rows.reshape(Y * XL, BLOCK, 256), ("y", "xl"), 0, 0, tiled=True
    ).reshape(4, 256, 256)
    p1, weights = lax.optimization_barrier((p1, weights))
    p3 = swapped(p1, "core")
    pieces = (p0, p1, p2, p3)

    shape = (Y, BLOCK, BLOCK)
    key_value, query = kernel_call(
        project_features,
        [((512, BLOCK), BF16)] * 2,
        [SMEM] + [VMEM] * 5,
        2 * 512 * 1024 * 256,
        2000000,
        (scalars, *pieces, weights),
    )
    arrived = shifted(key_value, 1)
    (both,) = kernel_call(
        project_cotangents,
        [((512, BLOCK), BF16)],
        [SMEM] + [VMEM] * 6,
        2 * 512 * 1024 * 128,
        2000000,
        (scalars, *pieces, weights, query),
    )
    both, weights = lax.optimization_barrier((both, weights))
    group_weights = [weights] + [passed(weights, -k) for k in range(1, Y)]

    mask = lax.all_gather(local_mask, "y", axis=0).reshape(Y, 1)
    usable = (mask > 0) | jnp.eye(1, dtype=bool)
    wrap = (xl * Z + z == 0).reshape(1)
    flags = jnp.concatenate([wrap, usable.reshape(Y)]).astype(jnp.int32)
    local, back, grad_query = kernel_call(
        attend,
        [(shape, F32), (shape, F32), (shape, BF16)],
        [SMEM] + [VMEM] * 3,
        4 * 6 * 256 * 512 * 128,
        1000000,
        (flags, both.reshape(shape), key_value.reshape(shape), arrived.reshape(shape)),
    )
    returned = shifted(back, -1)

    term, *grads = kernel_call(
        weight_terms,
        [((4, 256, 256), BF16)] + [((3 * HEAD_DIM, BLOCK), BF16)] * 4,
        [SMEM] + [VMEM] * 7,
        2 * 512 * 1024 * 256,
        2000000,
        (scalars, *pieces, local, returned, grad_query),
    )
    term = lax.all_to_all(
        term.reshape(Y * XL, BLOCK, 256), ("y", "xl"), 0, 0, tiled=True
    )
    grads = [grads[0]] + [passed(grads[k], -k) for k in range(1, Y)]
    term, *grads = lax.optimization_barrier((term, *grads))
    (term,) = kernel_call(
        add_terms, [((BLOCK, 768), BF16)], [VMEM], 1000000, 800000, (term,)
    )
    term, grads[0] = lax.optimization_barrier((term, grads[0]))
    term = lax.all_to_all(term.reshape(Z, 8, 768), "z", 0, 0, tiled=True)
    ours, theirs = kernel_call(
        input_terms,
        [((2, BLOCK, 256), BF16)] * 2,
        [SMEM] + [VMEM] * 8,
        2 * 128 * 1024 * 1024,
        2500000,
        (scalars, *grads, *group_weights),
    )
    pair = ours.astype(F32) + swapped(theirs, "core").astype(F32)
    remote = swapped(lax.dynamic_index_in_dim(pair, 1 - xh, 0, keepdims=False), "xh")
    pair = lax.dynamic_index_in_dim(pair, xh, 0, keepdims=False)
    input_grad = (pair + remote).astype(BF16)

    (weight_grads,) = kernel_call(
        sum_terms, [((8, 768), F32)], [VMEM], 1000000, 300000, (term,)
    )
    return (input_grad, weight_grads.reshape(8, 3, 256))


def solution(mesh):
    fine = Mesh(mesh.devices.reshape(Y, XL, Z, XH, CORE), AXES)
    head = ("xh", "core")
    return jax.shard_map(
        shards,
        mesh=fine,
        in_specs=(
            P(DOM, head),
            P(DOM, head),
            P(DOM, None, head),
            P(DOM, None),
            P(None, DOM),
        ),
        out_specs=(P(DOM, head), P(DOM, None, head)),
        check_vma=False,
    )
```

```python
import jax
import jax.numpy as jnp
from jax import lax
from jax.experimental import pallas as pl
from jax.experimental.pallas import tpu as pltpu
from jax.sharding import Mesh
from jax.sharding import PartitionSpec as P

HEAD_DIM = 64
BLOCK = 128
ROUNDS = 3
Y, XL, Z, XH, CORE = 4, 2, 16, 2, 2
AXES = ("y", "xl", "z", "xh", "core")
DOM = ("y", "xl", "z")
RING = ("xl", "z")
RING_SIZE = XL * Z
F32 = jnp.float32
BF16 = jnp.bfloat16
SMEM = pl.BlockSpec(memory_space=pltpu.SMEM)
VMEM = pl.BlockSpec(memory_space=pltpu.VMEM)
HBM = pl.BlockSpec(memory_space=pltpu.HBM)


def swapped(block, axis):
    return lax.ppermute(block, axis, [(0, 1), (1, 0)])


def shifted(block, distance):
    route = [(i, (i + distance) % RING_SIZE) for i in range(RING_SIZE)]
    return lax.ppermute(block, RING, route)


def matmul(left, right, dims):
    return lax.dot_general(left, right, (dims, ((), ())), preferred_element_type=F32)


def low_lanes(shape):
    return lax.broadcasted_iota(jnp.int32, shape, len(shape) - 1) < HEAD_DIM


def kernel_call(kernel, shapes, specs, flops, size, args, scratch=(), limit=16):
    return pl.pallas_call(
        kernel,
        out_shape=[jax.ShapeDtypeStruct(shape, dtype) for shape, dtype in shapes],
        in_specs=specs,
        out_specs=[VMEM] * len(shapes),
        scratch_shapes=list(scratch),
        compiler_params=pltpu.CompilerParams(vmem_limit_bytes=limit * 1024 * 1024),
        cost_estimate=pl.CostEstimate(flops=flops, bytes_accessed=size, transcendentals=0),
    )(*args)


def pack(features, cotangents, weights, packed, held, arrivals):
    copies = [
        pltpu.make_async_copy(weights, held, arrivals.at[0]),
        pltpu.make_async_copy(features, packed.at[pl.ds(0, BLOCK)], arrivals.at[1]),
        pltpu.make_async_copy(cotangents, packed.at[pl.ds(BLOCK, BLOCK)], arrivals.at[2]),
    ]
    for copy in copies:
        copy.start()
    copies[0].wait()
    for index, t in enumerate((1, 2, 0, 3)):
        lower = 2 * BLOCK + 8 * index
        packed[lower : lower + 8, :] = held[:, t, :]
    copies[1].wait()
    copies[2].wait()


def spread(scalars, gathered, piece, rows):
    piece[...] = gathered[:, : 2 * BLOCK]
    y = scalars[5]
    for source in range(Y):
        whole = gathered[source, 2 * BLOCK :]
        part = whole[:, :HEAD_DIM]
        for quarter in range(1, Y):
            lower = quarter * HEAD_DIM
            part = jnp.where(y == quarter, whole[:, lower : lower + HEAD_DIM], part)
        part = jnp.concatenate([part[8 * t : 8 * t + 8] for t in range(4)], axis=1)
        rows[:, source] = jnp.broadcast_to(part[None], (Z, 8, 256))


def features_of(piece):
    return piece[:, :BLOCK].reshape(Y * BLOCK, 256)


def cotangents_of(piece):
    return piece[:, BLOCK:].reshape(Y * BLOCK, 256)


def project_features(scalars, p0, p1, p2, p3, near, far, key_value, query, weights):
    first = scalars[6] == 0
    for quarter in range(Y):
        own = near[:, quarter].reshape(BLOCK, 256)
        other = far[:, quarter].reshape(BLOCK, 256)
        weights[quarter, :BLOCK] = jnp.where(first, own, other)
        weights[quarter, BLOCK:] = jnp.where(first, other, own)
    total = jnp.zeros((Y * BLOCK, 256), F32)
    for index, piece in enumerate((p0, p1, p2, p3)):
        rows = weights[scalars[index]]
        total += matmul(features_of(piece), rows, ((1,), (0,)))
    key_value[...] = total[:, :BLOCK].astype(BF16)
    query[...] = total[:, BLOCK:].astype(BF16)


def project_cotangents(scalars, p0, p1, p2, p3, weights, query, both, turned):
    total = jnp.zeros((Y * BLOCK, BLOCK), F32)
    for index, piece in enumerate((p0, p1, p2, p3)):
        rows = weights[scalars[index], :, BLOCK:]
        total += matmul(cotangents_of(piece), rows, ((1,), (0,)))
    low = low_lanes((Y * BLOCK, BLOCK))
    both[...] = jnp.where(low, query[...], total.astype(BF16))
    for quarter in range(Y):
        part = weights[quarter, :, : 3 * HEAD_DIM].T
        turned[:, quarter * 256 : (quarter + 1) * 256] = part


def attend(scalars, both, own, arrived, local, back, grad_query):
    scale = HEAD_DIM ** (-0.5)
    low = low_lanes((BLOCK, BLOCK))
    zero = jnp.zeros((BLOCK, BLOCK), BF16)
    wrap = scalars[0]
    back[...] = jnp.zeros((Y, BLOCK, BLOCK), F32)
    for block in range(Y):
        pair = both[block]
        stacked = jnp.concatenate(
            [jnp.where(low, pair, zero), jnp.where(low, zero, pair)], axis=0
        )
        sources = [lax.rem(block - r - wrap + 2 * Y, Y) for r in range(ROUNDS)]
        listed = jnp.concatenate([own[block]] + [arrived[s] for s in sources], axis=0)
        inner = matmul(stacked, listed, ((1,), (1,)))
        scores = inner[:BLOCK] * scale
        prob_grad = inner[BLOCK:]
        usable = scalars[1 + block] > 0
        local_scores = jnp.where(usable, scores[:, :BLOCK], -1e30)
        scores = jnp.concatenate([local_scores, scores[:, BLOCK:]], axis=1)
        exponent = jnp.exp(scores - jnp.max(scores, axis=1, keepdims=True))
        total = jnp.sum(exponent, axis=1, keepdims=True)
        probs = exponent * (1.0 / total)
        mean = jnp.sum(probs * prob_grad, axis=1, keepdims=True)
        score_grad = (probs * (prob_grad - mean) * scale).astype(BF16)
        query_side = matmul(score_grad, listed, ((1,), (0,)))
        grad_query[block] = jnp.where(low, query_side, 0.0).astype(BF16)
        terms = jnp.concatenate([score_grad, probs.astype(BF16)], axis=0)
        key_side = matmul(terms, stacked, ((0,), (0,)))
        local[block] = key_side[:BLOCK]
        for r in range(ROUNDS):
            lower = (1 + r) * BLOCK
            part = key_side[lower : lower + BLOCK].astype(BF16).astype(F32)
            back[sources[r]] += part


def weight_terms(scalars, p0, p1, p2, p3, local, returned, grad_query, kept, sent, grads):
    sides = (local[...] + returned[...]).astype(BF16)
    both = jnp.concatenate([sides, grad_query[...]], axis=2)
    for block in range(Y):
        grads[block] = both[block, :, : 3 * HEAD_DIM].T
    both = both.reshape(Y * BLOCK, 256)
    first = scalars[6] == 0
    for index, piece in enumerate((p0, p1, p2, p3)):
        product = matmul(features_of(piece), both, ((0,), (0,)))
        quarter = scalars[index]
        kept[quarter] = jnp.where(first, product[:BLOCK], product[BLOCK:])
        sent[quarter] = jnp.where(first, product[BLOCK:], product[:BLOCK]).astype(BF16)


def input_terms(scalars, grads, w0, w1, w2, w3, ours, theirs):
    core = scalars[4]
    for half in range(XH):
        for out, side in ((ours, core), (theirs, 1 - core)):
            total = jnp.zeros((BLOCK, 256), F32)
            lower = (half * CORE + side) * 256
            for slot, weights in enumerate((w0, w1, w2, w3)):
                columns = weights[:, pl.ds(pl.multiple_of(lower, 256), 256)]
                left = grads[lax.rem(scalars[5] + slot, Y)]
                total += matmul(left, columns, ((0,), (0,)))
            out[half] = total.astype(BF16)


def sum_terms(terms, out):
    for source in range(Y):
        total = jnp.sum(terms[source * Z : (source + 1) * Z].astype(F32), axis=0)
        for place, lower in ((1, 0), (2, HEAD_DIM), (0, 2 * HEAD_DIM)):
            at = place * 256 + source * HEAD_DIM
            out[:, at : at + HEAD_DIM] = total[:, lower : lower + HEAD_DIM]


def shards(node_features, cotangent, proj_weights, local_mask, matching):
    xl = lax.axis_index("xl")
    z = lax.axis_index("z")
    xh = lax.axis_index("xh")
    core = lax.axis_index("core")
    head = xh * CORE + core
    y = lax.axis_index("y")
    scalars = jnp.stack([head, head ^ 2, head ^ 1, head ^ 3, core, y, xl]).astype(jnp.int32)

    (packed,) = kernel_call(
        pack,
        [((2 * BLOCK + 32, 256), BF16)],
        [HBM] * 3,
        1000,
        300000,
        (node_features, cotangent, proj_weights),
        (pltpu.VMEM((8, 4, 256), BF16), pltpu.SemaphoreType.DMA((3,))),
        60,
    )
    gathered = lax.all_gather(packed, "y", axis=0)
    p0, rows = kernel_call(
        spread,
        [((Y, 2 * BLOCK, 256), BF16), ((Z, Y, 8, 256), BF16)],
        [SMEM, VMEM],
        1000,
        1500000,
        (scalars, gathered),
    )
    near = lax.all_to_all(rows, "z", 0, 0, tiled=True)
    p1 = swapped(p0, "xh")
    p2 = swapped(p0, "core")
    far = swapped(near, "xl")
    p3 = swapped(p1, "core")
    pieces = (p0, p1, p2, p3)

    shape = (Y, BLOCK, BLOCK)
    key_value, query, weights = kernel_call(
        project_features,
        [((512, BLOCK), BF16), ((512, BLOCK), BF16), ((4, 256, 256), BF16)],
        [SMEM] + [VMEM] * 6,
        2 * 512 * 1024 * 256,
        2000000,
        (scalars, *pieces, near, far),
    )
    arrived = shifted(key_value, 1)
    both, turned = kernel_call(
        project_cotangents,
        [((512, BLOCK), BF16), ((192, 1024), BF16)],
        [SMEM] + [VMEM] * 6,
        2 * 512 * 1024 * 128,
        3500000,
        (scalars, *pieces, weights, query),
    )
    group_weights = [turned] + [
        lax.ppermute(turned, "y", [(i, (i - k) % Y) for i in range(Y)]) for k in range(1, Y)
    ]

    mask = lax.all_gather(local_mask, "y", axis=0).reshape(Y, 1)
    usable = (mask > 0) | jnp.eye(1, dtype=bool)
    wrap = (xl * Z + z == 0).reshape(1)
    flags = jnp.concatenate([wrap, usable.reshape(Y)]).astype(jnp.int32)
    local, back, grad_query = kernel_call(
        attend,
        [(shape, F32), (shape, F32), (shape, BF16)],
        [SMEM] + [VMEM] * 3,
        4 * 6 * 256 * 512 * 128,
        1000000,
        (flags, both.reshape(shape), key_value.reshape(shape), arrived.reshape(shape)),
    )
    returned = shifted(back, -1)
    returned, *group_weights[1:3] = lax.optimization_barrier((returned, *group_weights[1:3]))

    kept, sent, grads = kernel_call(
        weight_terms,
        [((Y, BLOCK, 256), F32), ((Y, BLOCK, 256), BF16), ((Y, 192, BLOCK), BF16)],
        [SMEM] + [VMEM] * 7,
        2 * 512 * 1024 * 256,
        2000000,
        (scalars, *pieces, local, returned, grad_query),
    )
    grads, group_weights[3] = lax.optimization_barrier((grads, group_weights[3]))
    other = swapped(sent, "xl")
    grads = lax.all_to_all(grads, "y", 0, 0, tiled=True)
    grads, other = lax.optimization_barrier((grads, other))
    term = (kept + other.astype(F32)).astype(BF16)
    term, grads = lax.optimization_barrier((term, grads))
    term = lax.all_to_all(term.reshape(Y * Z, 8, 256), ("y", "z"), 0, 0, tiled=True)
    ours, theirs = kernel_call(
        input_terms,
        [((2, BLOCK, 256), BF16)] * 2,
        [SMEM] + [VMEM] * 5,
        2 * 128 * 1024 * 1024,
        2500000,
        (scalars, grads, *group_weights),
    )
    pair = ours.astype(F32) + swapped(theirs, "core").astype(F32)
    remote = swapped(lax.dynamic_index_in_dim(pair, 1 - xh, 0, keepdims=False), "xh")
    pair = lax.dynamic_index_in_dim(pair, xh, 0, keepdims=False)
    input_grad = (pair + remote).astype(BF16)

    (weight_grads,) = kernel_call(
        sum_terms, [((8, 768), F32)], [VMEM], 1000000, 300000, (term,)
    )
    return (input_grad, weight_grads.reshape(8, 3, 256))


def solution(mesh):
    fine = Mesh(mesh.devices.reshape(Y, XL, Z, XH, CORE), AXES)
    head = ("xh", "core")
    return jax.shard_map(
        shards,
        mesh=fine,
        in_specs=(
            P(DOM, head),
            P(DOM, head),
            P(DOM, None, head),
            P(DOM, None),
            P(None, DOM),
        ),
        out_specs=(P(DOM, head), P(DOM, None, head)),
        check_vma=False,
    )
```

```python
import jax
import jax.numpy as jnp
from jax import lax
from jax.experimental import pallas as pl
from jax.experimental.pallas import tpu as pltpu
from jax.sharding import Mesh
from jax.sharding import PartitionSpec as P

HEAD_DIM = 64
BLOCK = 128
ROUNDS = 3
Y, XL, Z, XH, CORE = 4, 2, 16, 2, 2
AXES = ("y", "xl", "z", "xh", "core")
DOM = ("y", "xl", "z")
RING = ("xl", "z")
RING_SIZE = XL * Z
F32 = jnp.float32
BF16 = jnp.bfloat16
SMEM = pl.BlockSpec(memory_space=pltpu.SMEM)
VMEM = pl.BlockSpec(memory_space=pltpu.VMEM)
HBM = pl.BlockSpec(memory_space=pltpu.HBM)


def swapped(block, axis):
    return lax.ppermute(block, axis, [(0, 1), (1, 0)])


def shifted(block, distance):
    route = [(i, (i + distance) % RING_SIZE) for i in range(RING_SIZE)]
    return lax.ppermute(block, RING, route)


def matmul(left, right, dims):
    return lax.dot_general(left, right, (dims, ((), ())), preferred_element_type=F32)


def low_lanes(shape):
    return lax.broadcasted_iota(jnp.int32, shape, len(shape) - 1) < HEAD_DIM


def kernel_call(kernel, shapes, specs, flops, size, args, scratch=(), limit=16):
    return pl.pallas_call(
        kernel,
        out_shape=[jax.ShapeDtypeStruct(shape, dtype) for shape, dtype in shapes],
        in_specs=specs,
        out_specs=[VMEM] * len(shapes),
        scratch_shapes=list(scratch),
        compiler_params=pltpu.CompilerParams(vmem_limit_bytes=limit * 1024 * 1024),
        cost_estimate=pl.CostEstimate(flops=flops, bytes_accessed=size, transcendentals=0),
    )(*args)


def pack(features, cotangents, weights, packed, rows, held, arrivals):
    copies = [
        pltpu.make_async_copy(weights, held, arrivals.at[0]),
        pltpu.make_async_copy(features, packed.at[pl.ds(0, BLOCK)], arrivals.at[1]),
        pltpu.make_async_copy(cotangents, packed.at[pl.ds(BLOCK, BLOCK)], arrivals.at[2]),
    ]
    for copy in copies:
        copy.start()
    copies[0].wait()
    for quarter in range(Y):
        lower = quarter * HEAD_DIM
        part = jnp.concatenate(
            [held[:, t, lower : lower + HEAD_DIM] for t in (1, 2, 0, 3)], axis=1
        )
        rows[:, quarter] = jnp.broadcast_to(part[None], (Z, 8, 256))
    copies[1].wait()
    copies[2].wait()


def spread(gathered, rows):
    for quarter in range(Y):
        part = gathered[:, quarter].reshape(BLOCK, 256)
        rows[quarter, 0] = part
        rows[quarter, 1] = part


def features_of(piece):
    return piece[:, :BLOCK].reshape(Y * BLOCK, 256)


def cotangents_of(piece):
    return piece[:, BLOCK:].reshape(Y * BLOCK, 256)


def project_features(scalars, p0, p1, p2, p3, weights, key_value, query):
    total = jnp.zeros((Y * BLOCK, 256), F32)
    for index, piece in enumerate((p0, p1, p2, p3)):
        rows = weights[scalars[index]]
        total += matmul(features_of(piece), rows, ((1,), (0,)))
    key_value[...] = total[:, :BLOCK].astype(BF16)
    query[...] = total[:, BLOCK:].astype(BF16)


def project_cotangents(scalars, p0, p1, p2, p3, weights, query, both, turned):
    total = jnp.zeros((Y * BLOCK, BLOCK), F32)
    for index, piece in enumerate((p0, p1, p2, p3)):
        rows = weights[scalars[index], :, BLOCK:]
        total += matmul(cotangents_of(piece), rows, ((1,), (0,)))
    low = low_lanes((Y * BLOCK, BLOCK))
    both[...] = jnp.where(low, query[...], total.astype(BF16))
    for quarter in range(Y):
        part = weights[quarter, :, : 3 * HEAD_DIM].T
        turned[:, quarter * 256 : (quarter + 1) * 256] = part


def attend(scalars, both, own, arrived, local, back, grad_query):
    scale = HEAD_DIM ** (-0.5)
    low = low_lanes((BLOCK, BLOCK))
    zero = jnp.zeros((BLOCK, BLOCK), BF16)
    wrap = scalars[0]
    back[...] = jnp.zeros((Y, BLOCK, BLOCK), F32)
    for block in range(Y):
        pair = both[block]
        stacked = jnp.concatenate(
            [jnp.where(low, pair, zero), jnp.where(low, zero, pair)], axis=0
        )
        sources = [lax.rem(block - r - wrap + 2 * Y, Y) for r in range(ROUNDS)]
        listed = jnp.concatenate([own[block]] + [arrived[s] for s in sources], axis=0)
        inner = matmul(stacked, listed, ((1,), (1,)))
        scores = inner[:BLOCK] * scale
        prob_grad = inner[BLOCK:]
        usable = scalars[1 + block] > 0
        local_scores = jnp.where(usable, scores[:, :BLOCK], -1e30)
        scores = jnp.concatenate([local_scores, scores[:, BLOCK:]], axis=1)
        exponent = jnp.exp(scores - jnp.max(scores, axis=1, keepdims=True))
        total = jnp.sum(exponent, axis=1, keepdims=True)
        probs = exponent * (1.0 / total)
        mean = jnp.sum(probs * prob_grad, axis=1, keepdims=True)
        score_grad = (probs * (prob_grad - mean) * scale).astype(BF16)
        query_side = matmul(score_grad, listed, ((1,), (0,)))
        grad_query[block] = jnp.where(low, query_side, 0.0).astype(BF16)
        terms = jnp.concatenate([score_grad, probs.astype(BF16)], axis=0)
        key_side = matmul(terms, stacked, ((0,), (0,)))
        local[block] = key_side[:BLOCK]
        for r in range(ROUNDS):
            lower = (1 + r) * BLOCK
            part = key_side[lower : lower + BLOCK].astype(BF16).astype(F32)
            back[sources[r]] += part


def weight_terms(scalars, p0, p1, p2, p3, local, returned, grad_query, kept, sent, grads):
    sides = (local[...] + returned[...]).astype(BF16)
    both = jnp.concatenate([sides, grad_query[...]], axis=2)
    for block in range(Y):
        grads[block] = both[block, :, : 3 * HEAD_DIM].T
    both = both.reshape(Y * BLOCK, 256)
    first = scalars[6] == 0
    for index, piece in enumerate((p0, p1, p2, p3)):
        product = matmul(features_of(piece), both, ((0,), (0,)))
        quarter = scalars[index]
        kept[quarter] = jnp.where(first, product[:BLOCK], product[BLOCK:])
        sent[quarter] = jnp.where(first, product[BLOCK:], product[:BLOCK]).astype(BF16)


def input_terms(scalars, grads, w0, w1, w2, w3, *out):
    for index in range(4):
        total = jnp.zeros((BLOCK, 256), F32)
        lower = pl.multiple_of(scalars[index] * 256, 256)
        for slot, weights in enumerate((w0, w1, w2, w3)):
            columns = weights[:, pl.ds(lower, 256)]
            left = grads[lax.rem(scalars[5] + slot, Y)]
            total += matmul(left, columns, ((0,), (0,)))
        out[index][...] = total.astype(BF16)


def sum_terms(terms, out):
    for source in range(Y):
        total = jnp.sum(terms[source * Z : (source + 1) * Z].astype(F32), axis=0)
        for place, lower in ((1, 0), (2, HEAD_DIM), (0, 2 * HEAD_DIM)):
            at = place * 256 + source * HEAD_DIM
            out[:, at : at + HEAD_DIM] = total[:, lower : lower + HEAD_DIM]


def shards(node_features, cotangent, proj_weights, local_mask, matching):
    xl = lax.axis_index("xl")
    z = lax.axis_index("z")
    xh = lax.axis_index("xh")
    core = lax.axis_index("core")
    head = xh * CORE + core
    y = lax.axis_index("y")
    scalars = jnp.stack([head, head ^ 2, head ^ 1, head ^ 3, core, y, xl]).astype(jnp.int32)

    packed, rows = kernel_call(
        pack,
        [((2 * BLOCK, 256), BF16), ((Z, Y, 8, 256), BF16)],
        [HBM] * 3,
        1000,
        600000,
        (node_features, cotangent, proj_weights),
        (pltpu.VMEM((8, 4, 256), BF16), pltpu.SemaphoreType.DMA((3,))),
        60,
    )
    near = lax.all_to_all(rows, "z", 0, 0, tiled=True)
    p0 = lax.all_gather(packed, "y", axis=0)
    p1 = swapped(p0, "xh")
    p2 = swapped(p0, "core")
    (rows,) = kernel_call(
        spread, [((Y, XL, BLOCK, 256), BF16)], [VMEM], 1000, 800000, (near,)
    )
    weights = lax.all_to_all(
        rows.reshape(Y * XL, BLOCK, 256), ("y", "xl"), 0, 0, tiled=True
    ).reshape(4, 256, 256)
    p1, weights = lax.optimization_barrier((p1, weights))
    p3 = swapped(p1, "core")
    pieces = (p0, p1, p2, p3)

    shape = (Y, BLOCK, BLOCK)
    key_value, query = kernel_call(
        project_features,
        [((512, BLOCK), BF16), ((512, BLOCK), BF16)],
        [SMEM] + [VMEM] * 5,
        2 * 512 * 1024 * 256,
        2000000,
        (scalars, *pieces, weights),
    )
    arrived = shifted(key_value, 1)
    both, turned = kernel_call(
        project_cotangents,
        [((512, BLOCK), BF16), ((192, 1024), BF16)],
        [SMEM] + [VMEM] * 6,
        2 * 512 * 1024 * 128,
        3500000,
        (scalars, *pieces, weights, query),
    )
    group_weights = [turned] + [
        lax.ppermute(turned, "y", [(i, (i - k) % Y) for i in range(Y)]) for k in range(1, Y)
    ]

    mask = lax.all_gather(local_mask, "y", axis=0).reshape(Y, 1)
    usable = (mask > 0) | jnp.eye(1, dtype=bool)
    wrap = (xl * Z + z == 0).reshape(1)
    flags = jnp.concatenate([wrap, usable.reshape(Y)]).astype(jnp.int32)
    local, back, grad_query = kernel_call(
        attend,
        [(shape, F32), (shape, F32), (shape, BF16)],
        [SMEM] + [VMEM] * 3,
        4 * 6 * 256 * 512 * 128,
        1000000,
        (flags, both.reshape(shape), key_value.reshape(shape), arrived.reshape(shape)),
    )
    returned = shifted(back, -1)
    returned, *group_weights[1:3] = lax.optimization_barrier((returned, *group_weights[1:3]))

    kept, sent, grads = kernel_call(
        weight_terms,
        [((Y, BLOCK, 256), F32), ((Y, BLOCK, 256), BF16), ((Y, 192, BLOCK), BF16)],
        [SMEM] + [VMEM] * 7,
        2 * 512 * 1024 * 256,
        2000000,
        (scalars, *pieces, local, returned, grad_query),
    )
    grads, group_weights[3] = lax.optimization_barrier((grads, group_weights[3]))
    other = swapped(sent, "xl")
    grads = lax.all_to_all(grads, "y", 0, 0, tiled=True)
    grads, other = lax.optimization_barrier((grads, other))
    term = (kept + other.astype(F32)).astype(BF16)
    term, grads = lax.optimization_barrier((term, grads))
    term = lax.all_to_all(term.reshape(Y * Z, 8, 256), ("y", "z"), 0, 0, tiled=True)
    mine, half, side, far = kernel_call(
        input_terms,
        [((BLOCK, 256), BF16)] * 4,
        [SMEM] + [VMEM] * 5,
        2 * 128 * 1024 * 1024,
        2500000,
        (scalars, grads, *group_weights),
    )
    route = [(i, i ^ 3) for i in range(4)]
    parts = [mine, swapped(half, "xh"), swapped(side, "core")]
    parts.append(lax.ppermute(far, ("xh", "core"), route))
    input_grad = sum(part.astype(F32) for part in parts).astype(BF16)

    (weight_grads,) = kernel_call(
        sum_terms, [((8, 768), F32)], [VMEM], 1000000, 300000, (term,)
    )
    return (input_grad, weight_grads.reshape(8, 3, 256))


def solution(mesh):
    fine = Mesh(mesh.devices.reshape(Y, XL, Z, XH, CORE), AXES)
    head = ("xh", "core")
    return jax.shard_map(
        shards,
        mesh=fine,
        in_specs=(
            P(DOM, head),
            P(DOM, head),
            P(DOM, None, head),
            P(DOM, None),
            P(None, DOM),
        ),
        out_specs=(P(DOM, head), P(DOM, None, head)),
        check_vma=False,
    )
```

```python
import jax
import jax.numpy as jnp
from jax import lax
from jax.experimental import pallas as pl
from jax.experimental.pallas import tpu as pltpu
from jax.sharding import Mesh
from jax.sharding import PartitionSpec as P

HEAD_DIM = 64
BLOCK = 128
ROUNDS = 3
Y, XL, Z, XH, CORE = 4, 2, 16, 2, 2
AXES = ("y", "xl", "z", "xh", "core")
DOM = ("y", "xl", "z")
RING = ("xl", "z")
RING_SIZE = XL * Z
F32 = jnp.float32
BF16 = jnp.bfloat16
SMEM = pl.BlockSpec(memory_space=pltpu.SMEM)
VMEM = pl.BlockSpec(memory_space=pltpu.VMEM)
HBM = pl.BlockSpec(memory_space=pltpu.HBM)


def swapped(block, axis):
    return lax.ppermute(block, axis, [(0, 1), (1, 0)])


def shifted(block, distance):
    route = [(i, (i + distance) % RING_SIZE) for i in range(RING_SIZE)]
    return lax.ppermute(block, RING, route)


def matmul(left, right, dims):
    return lax.dot_general(left, right, (dims, ((), ())), preferred_element_type=F32)


def low_lanes(shape):
    return lax.broadcasted_iota(jnp.int32, shape, len(shape) - 1) < HEAD_DIM


def kernel_call(kernel, shapes, specs, flops, size, args, scratch=(), limit=16):
    return pl.pallas_call(
        kernel,
        out_shape=[jax.ShapeDtypeStruct(shape, dtype) for shape, dtype in shapes],
        in_specs=specs,
        out_specs=[VMEM] * len(shapes),
        scratch_shapes=list(scratch),
        compiler_params=pltpu.CompilerParams(vmem_limit_bytes=limit * 1024 * 1024),
        cost_estimate=pl.CostEstimate(flops=flops, bytes_accessed=size, transcendentals=0),
    )(*args)


def pack(features, cotangents, weights, packed, rows, held, arrivals):
    copies = [
        pltpu.make_async_copy(weights, held, arrivals.at[0]),
        pltpu.make_async_copy(features, packed.at[pl.ds(0, BLOCK)], arrivals.at[1]),
        pltpu.make_async_copy(cotangents, packed.at[pl.ds(BLOCK, BLOCK)], arrivals.at[2]),
    ]
    for copy in copies:
        copy.start()
    copies[0].wait()
    for quarter in range(Y):
        lower = quarter * HEAD_DIM
        part = jnp.concatenate(
            [held[:, t, lower : lower + HEAD_DIM] for t in (1, 2, 0, 3)], axis=1
        )
        rows[:, quarter] = jnp.broadcast_to(part[None], (Z, 8, 256))
    copies[1].wait()
    copies[2].wait()


def spread(gathered, rows):
    for quarter in range(Y):
        part = gathered[:, quarter].reshape(BLOCK, 256)
        rows[quarter, 0] = part
        rows[quarter, 1] = part


def features_of(piece):
    return piece[:, :BLOCK].reshape(Y * BLOCK, 256)


def cotangents_of(piece):
    return piece[:, BLOCK:].reshape(Y * BLOCK, 256)


def project_features(scalars, p0, p1, p2, p3, weights, key_value, query):
    total = jnp.zeros((Y * BLOCK, 256), F32)
    for index, piece in enumerate((p0, p1, p2, p3)):
        rows = weights[scalars[index]]
        total += matmul(features_of(piece), rows, ((1,), (0,)))
    key_value[...] = total[:, :BLOCK].astype(BF16)
    query[...] = total[:, BLOCK:].astype(BF16)


def project_cotangents(scalars, p0, p1, p2, p3, weights, query, both, turned):
    total = jnp.zeros((Y * BLOCK, BLOCK), F32)
    for index, piece in enumerate((p0, p1, p2, p3)):
        rows = weights[scalars[index], :, BLOCK:]
        total += matmul(cotangents_of(piece), rows, ((1,), (0,)))
    low = low_lanes((Y * BLOCK, BLOCK))
    both[...] = jnp.where(low, query[...], total.astype(BF16))
    for quarter in range(Y):
        part = weights[quarter, :, : 3 * HEAD_DIM].T
        turned[:, quarter * 256 : (quarter + 1) * 256] = part


def attend(scalars, both, own, arrived, local, back, grad_query):
    scale = HEAD_DIM ** (-0.5)
    low = low_lanes((BLOCK, BLOCK))
    zero = jnp.zeros((BLOCK, BLOCK), BF16)
    wrap = scalars[0]
    back[...] = jnp.zeros((Y, BLOCK, BLOCK), F32)
    for block in range(Y):
        pair = both[block]
        stacked = jnp.concatenate(
            [jnp.where(low, pair, zero), jnp.where(low, zero, pair)], axis=0
        )
        sources = [lax.rem(block - r - wrap + 2 * Y, Y) for r in range(ROUNDS)]
        listed = jnp.concatenate([own[block]] + [arrived[s] for s in sources], axis=0)
        inner = matmul(stacked, listed, ((1,), (1,)))
        scores = inner[:BLOCK] * scale
        prob_grad = inner[BLOCK:]
        usable = scalars[1 + block] > 0
        local_scores = jnp.where(usable, scores[:, :BLOCK], -1e30)
        scores = jnp.concatenate([local_scores, scores[:, BLOCK:]], axis=1)
        exponent = jnp.exp(scores - jnp.max(scores, axis=1, keepdims=True))
        total = jnp.sum(exponent, axis=1, keepdims=True)
        probs = exponent * (1.0 / total)
        mean = jnp.sum(probs * prob_grad, axis=1, keepdims=True)
        score_grad = (probs * (prob_grad - mean) * scale).astype(BF16)
        query_side = matmul(score_grad, listed, ((1,), (0,)))
        grad_query[block] = jnp.where(low, query_side, 0.0).astype(BF16)
        terms = jnp.concatenate([score_grad, probs.astype(BF16)], axis=0)
        key_side = matmul(terms, stacked, ((0,), (0,)))
        local[block] = key_side[:BLOCK]
        for r in range(ROUNDS):
            lower = (1 + r) * BLOCK
            part = key_side[lower : lower + BLOCK].astype(BF16).astype(F32)
            back[sources[r]] += part


def weight_terms(scalars, p0, p1, p2, p3, local, returned, grad_query, bundle):
    sides = (local[...] + returned[...]).astype(BF16)
    both = jnp.concatenate([sides, grad_query[...]], axis=2)
    for block in range(Y):
        turned = both[block, :, : 3 * HEAD_DIM].T
        bundle[block, 256:] = jnp.concatenate([turned[:96], turned[96:]], axis=1)
    both = both.reshape(Y * BLOCK, 256)
    for index, piece in enumerate((p0, p1, p2, p3)):
        product = matmul(features_of(piece), both, ((0,), (0,)))
        bundle[scalars[index], :256] = product.astype(BF16)


def input_terms(scalars, bundle, w0, w1, w2, w3, sent, ours, theirs):
    other = pl.multiple_of((1 - scalars[6]) * BLOCK, BLOCK)
    sent[...] = bundle[:, pl.ds(other, BLOCK), :]
    core = scalars[4]
    grads = []
    for slot in range(Y):
        folded = bundle[lax.rem(scalars[5] + slot, Y), 256:]
        grads.append(jnp.concatenate([folded[:, :BLOCK], folded[:, BLOCK:]], axis=0))
    for half in range(XH):
        for out, side in ((ours, core), (theirs, 1 - core)):
            total = jnp.zeros((BLOCK, 256), F32)
            lower = pl.multiple_of((half * CORE + side) * 256, 256)
            for left, weights in zip(grads, (w0, w1, w2, w3)):
                columns = weights[:, pl.ds(lower, 256)]
                total += matmul(left, columns, ((0,), (0,)))
            out[half] = total.astype(BF16)


def add_terms(scalars, bundle, other, out):
    own = pl.multiple_of(scalars[6] * BLOCK, BLOCK)
    for source in range(Y):
        total = bundle[source, pl.ds(own, BLOCK), :].astype(F32) + other[source].astype(F32)
        total = total.astype(BF16)
        for place, lower in ((1, 0), (2, HEAD_DIM), (0, 2 * HEAD_DIM)):
            at = place * 256 + source * HEAD_DIM
            out[:, at : at + HEAD_DIM] = total[:, lower : lower + HEAD_DIM]


def sum_terms(terms, out):
    out[...] = jnp.sum(terms[...].astype(F32), axis=0)


def shards(node_features, cotangent, proj_weights, local_mask, matching):
    xl = lax.axis_index("xl")
    z = lax.axis_index("z")
    xh = lax.axis_index("xh")
    core = lax.axis_index("core")
    head = xh * CORE + core
    y = lax.axis_index("y")
    scalars = jnp.stack([head, head ^ 2, head ^ 1, head ^ 3, core, y, xl]).astype(jnp.int32)

    packed, rows = kernel_call(
        pack,
        [((2 * BLOCK, 256), BF16), ((Z, Y, 8, 256), BF16)],
        [HBM] * 3,
        1000,
        600000,
        (node_features, cotangent, proj_weights),
        (pltpu.VMEM((8, 4, 256), BF16), pltpu.SemaphoreType.DMA((3,))),
        60,
    )
    near = lax.all_to_all(rows, "z", 0, 0, tiled=True)
    p0 = lax.all_gather(packed, "y", axis=0)
    p1 = swapped(p0, "xh")
    p2 = swapped(p0, "core")
    (rows,) = kernel_call(
        spread, [((Y, XL, BLOCK, 256), BF16)], [VMEM], 1000, 800000, (near,)
    )
    weights = lax.all_to_all(
        rows.reshape(Y * XL, BLOCK, 256), ("y", "xl"), 0, 0, tiled=True
    ).reshape(4, 256, 256)
    p1, weights = lax.optimization_barrier((p1, weights))
    p3 = swapped(p1, "core")
    pieces = (p0, p1, p2, p3)

    shape = (Y, BLOCK, BLOCK)
    key_value, query = kernel_call(
        project_features,
        [((512, BLOCK), BF16), ((512, BLOCK), BF16)],
        [SMEM] + [VMEM] * 5,
        2 * 512 * 1024 * 256,
        2000000,
        (scalars, *pieces, weights),
    )
    arrived = shifted(key_value, 1)
    both, turned = kernel_call(
        project_cotangents,
        [((512, BLOCK), BF16), ((192, 1024), BF16)],
        [SMEM] + [VMEM] * 6,
        2 * 512 * 1024 * 128,
        3500000,
        (scalars, *pieces, weights, query),
    )
    group_weights = [turned] + [
        lax.ppermute(turned, "y", [(i, (i - k) % Y) for i in range(Y)]) for k in range(1, Y)
    ]

    mask = lax.all_gather(local_mask, "y", axis=0).reshape(Y, 1)
    usable = (mask > 0) | jnp.eye(1, dtype=bool)
    wrap = (xl * Z + z == 0).reshape(1)
    flags = jnp.concatenate([wrap, usable.reshape(Y)]).astype(jnp.int32)
    local, back, grad_query = kernel_call(
        attend,
        [(shape, F32), (shape, F32), (shape, BF16)],
        [SMEM] + [VMEM] * 3,
        4 * 6 * 256 * 512 * 128,
        1000000,
        (flags, both.reshape(shape), key_value.reshape(shape), arrived.reshape(shape)),
    )
    returned = shifted(back, -1)
    returned, *group_weights[1:3] = lax.optimization_barrier((returned, *group_weights[1:3]))

    (bundle,) = kernel_call(
        weight_terms,
        [((Y, 352, 256), BF16)],
        [SMEM] + [VMEM] * 7,
        2 * 512 * 1024 * 256,
        2000000,
        (scalars, *pieces, local, returned, grad_query),
    )
    bundle = lax.all_to_all(bundle, "y", 0, 0, tiled=True)
    bundle, group_weights[3] = lax.optimization_barrier((bundle, group_weights[3]))
    sent, ours, theirs = kernel_call(
        input_terms,
        [((Y, BLOCK, 256), BF16)] + [((XH, BLOCK, 256), BF16)] * 2,
        [SMEM] + [VMEM] * 5,
        2 * 128 * 1024 * 1024,
        2500000,
        (scalars, bundle, *group_weights),
    )
    other = swapped(sent, "xl")
    theirs = swapped(theirs, "core")
    other, theirs = lax.optimization_barrier((other, theirs))
    (term,) = kernel_call(
        add_terms,
        [((BLOCK, 768), BF16)],
        [SMEM] + [VMEM] * 2,
        1000000,
        800000,
        (scalars, bundle, other),
    )
    term, theirs, ours = lax.optimization_barrier((term, theirs, ours))
    term = lax.all_to_all(term.reshape(Z, 8, 768), "z", 0, 0, tiled=True)
    pair = ours.astype(F32) + theirs.astype(F32)
    remote = swapped(lax.dynamic_index_in_dim(pair, 1 - xh, 0, keepdims=False), "xh")
    pair = lax.dynamic_index_in_dim(pair, xh, 0, keepdims=False)
    input_grad = (pair + remote).astype(BF16)

    (weight_grads,) = kernel_call(
        sum_terms, [((8, 768), F32)], [VMEM], 1000000, 300000, (term,)
    )
    return (input_grad, weight_grads.reshape(8, 3, 256))


def solution(mesh):
    fine = Mesh(mesh.devices.reshape(Y, XL, Z, XH, CORE), AXES)
    head = ("xh", "core")
    return jax.shard_map(
        shards,
        mesh=fine,
        in_specs=(
            P(DOM, head),
            P(DOM, head),
            P(DOM, None, head),
            P(DOM, None),
            P(None, DOM),
        ),
        out_specs=(P(DOM, head), P(DOM, None, head)),
        check_vma=False,
    )
```

```python
import jax
import jax.numpy as jnp
from jax import lax
from jax.experimental import pallas as pl
from jax.experimental.pallas import tpu as pltpu
from jax.sharding import Mesh
from jax.sharding import PartitionSpec as P

HEAD_DIM = 64
BLOCK = 128
ROUNDS = 3
Y, XL, Z, XH, CORE = 4, 2, 16, 2, 2
AXES = ("y", "xl", "z", "xh", "core")
DOM = ("y", "xl", "z")
RING = ("xl", "z")
RING_SIZE = XL * Z
F32 = jnp.float32
BF16 = jnp.bfloat16
SMEM = pl.BlockSpec(memory_space=pltpu.SMEM)
VMEM = pl.BlockSpec(memory_space=pltpu.VMEM)
HBM = pl.BlockSpec(memory_space=pltpu.HBM)


def swapped(block, axis):
    return lax.ppermute(block, axis, [(0, 1), (1, 0)])


def shifted(block, distance):
    route = [(i, (i + distance) % RING_SIZE) for i in range(RING_SIZE)]
    return lax.ppermute(block, RING, route)


def matmul(left, right, dims):
    return lax.dot_general(left, right, (dims, ((), ())), preferred_element_type=F32)


def low_lanes(shape):
    return lax.broadcasted_iota(jnp.int32, shape, len(shape) - 1) < HEAD_DIM


def kernel_call(kernel, shapes, specs, flops, size, args, scratch=(), limit=16):
    return pl.pallas_call(
        kernel,
        out_shape=[jax.ShapeDtypeStruct(shape, dtype) for shape, dtype in shapes],
        in_specs=specs,
        out_specs=[VMEM] * len(shapes),
        scratch_shapes=list(scratch),
        compiler_params=pltpu.CompilerParams(vmem_limit_bytes=limit * 1024 * 1024),
        cost_estimate=pl.CostEstimate(flops=flops, bytes_accessed=size, transcendentals=0),
    )(*args)


def pack(features, cotangents, weights, packed, rows, held, arrivals):
    copies = [
        pltpu.make_async_copy(weights, held, arrivals.at[0]),
        pltpu.make_async_copy(features, packed.at[pl.ds(0, BLOCK)], arrivals.at[1]),
        pltpu.make_async_copy(cotangents, packed.at[pl.ds(BLOCK, BLOCK)], arrivals.at[2]),
    ]
    for copy in copies:
        copy.start()
    copies[0].wait()
    for quarter in range(Y):
        lower = quarter * HEAD_DIM
        part = jnp.concatenate(
            [held[:, t, lower : lower + HEAD_DIM] for t in (1, 2, 0, 3)], axis=1
        )
        rows[:, quarter] = jnp.broadcast_to(part[None], (Z, 8, 256))
    copies[1].wait()
    copies[2].wait()


def spread(gathered, rows):
    for quarter in range(Y):
        part = gathered[:, quarter].reshape(BLOCK, 256)
        rows[quarter, 0] = part
        rows[quarter, 1] = part


def project_features(scalars, x0, x1, weights, key_value, query):
    total = jnp.zeros((Y * BLOCK, 256), F32)
    for half, pair in enumerate((x0, x1)):
        for core in range(CORE):
            rows = weights[CORE * scalars[half] + core]
            total += matmul(pair[core].reshape(Y * BLOCK, 256), rows, ((1,), (0,)))
    key_value[...] = total[:, :BLOCK].astype(BF16)
    query[...] = total[:, BLOCK:].astype(BF16)


def project_cotangents(scalars, c0, c1, weights, query, both, turned):
    total = jnp.zeros((Y * BLOCK, BLOCK), F32)
    for half, pair in enumerate((c0, c1)):
        for core in range(CORE):
            rows = weights[CORE * scalars[half] + core, :, BLOCK:]
            total += matmul(pair[core].reshape(Y * BLOCK, 256), rows, ((1,), (0,)))
    low = low_lanes((Y * BLOCK, BLOCK))
    both[...] = jnp.where(low, query[...], total.astype(BF16))
    for quarter in range(Y):
        part = weights[quarter, :, : 3 * HEAD_DIM].T
        turned[:, quarter * 256 : (quarter + 1) * 256] = part


def attend(scalars, both, own, arrived, local, back, grad_query):
    scale = HEAD_DIM ** (-0.5)
    low = low_lanes((BLOCK, BLOCK))
    zero = jnp.zeros((BLOCK, BLOCK), BF16)
    wrap = scalars[0]
    back[...] = jnp.zeros((Y, BLOCK, BLOCK), F32)
    for block in range(Y):
        pair = both[block]
        stacked = jnp.concatenate(
            [jnp.where(low, pair, zero), jnp.where(low, zero, pair)], axis=0
        )
        sources = [lax.rem(block - r - wrap + 2 * Y, Y) for r in range(ROUNDS)]
        listed = jnp.concatenate([own[block]] + [arrived[s] for s in sources], axis=0)
        inner = matmul(stacked, listed, ((1,), (1,)))
        scores = inner[:BLOCK] * scale
        prob_grad = inner[BLOCK:]
        usable = scalars[1 + block] > 0
        local_scores = jnp.where(usable, scores[:, :BLOCK], -1e30)
        scores = jnp.concatenate([local_scores, scores[:, BLOCK:]], axis=1)
        exponent = jnp.exp(scores - jnp.max(scores, axis=1, keepdims=True))
        total = jnp.sum(exponent, axis=1, keepdims=True)
        probs = exponent * (1.0 / total)
        mean = jnp.sum(probs * prob_grad, axis=1, keepdims=True)
        score_grad = (probs * (prob_grad - mean) * scale).astype(BF16)
        query_side = matmul(score_grad, listed, ((1,), (0,)))
        grad_query[block] = jnp.where(low, query_side, 0.0).astype(BF16)
        terms = jnp.concatenate([score_grad, probs.astype(BF16)], axis=0)
        key_side = matmul(terms, stacked, ((0,), (0,)))
        local[block] = key_side[:BLOCK]
        for r in range(ROUNDS):
            lower = (1 + r) * BLOCK
            part = key_side[lower : lower + BLOCK].astype(BF16).astype(F32)
            back[sources[r]] += part


def weight_terms(scalars, x0, x1, local, returned, grad_query, kept, sent, grads):
    sides = (local[...] + returned[...]).astype(BF16)
    both = jnp.concatenate([sides, grad_query[...]], axis=2)
    for block in range(Y):
        grads[block] = both[block, :, : 3 * HEAD_DIM].T
    both = both.reshape(Y * BLOCK, 256)
    first = scalars[3] == 0
    for half, pair in enumerate((x0, x1)):
        for core in range(CORE):
            product = matmul(pair[core].reshape(Y * BLOCK, 256), both, ((0,), (0,)))
            quarter = CORE * scalars[half] + core
            kept[quarter] = jnp.where(first, product[:BLOCK], product[BLOCK:])
            sent[quarter] = jnp.where(first, product[BLOCK:], product[:BLOCK]).astype(BF16)


def input_terms(scalars, grads, w0, w1, w2, w3, out):
    for quarter in range(4):
        total = jnp.zeros((BLOCK, 256), F32)
        for slot, weights in enumerate((w0, w1, w2, w3)):
            columns = weights[:, quarter * 256 : (quarter + 1) * 256]
            left = grads[lax.rem(scalars[2] + slot, Y)]
            total += matmul(left, columns, ((0,), (0,)))
        out[quarter] = total.astype(BF16)


def sum_terms(terms, out):
    for source in range(Y):
        total = jnp.sum(terms[source * Z : (source + 1) * Z].astype(F32), axis=0)
        for place, lower in ((1, 0), (2, HEAD_DIM), (0, 2 * HEAD_DIM)):
            at = place * 256 + source * HEAD_DIM
            out[:, at : at + HEAD_DIM] = total[:, lower : lower + HEAD_DIM]


def shards(node_features, cotangent, proj_weights, local_mask, matching):
    xl = lax.axis_index("xl")
    z = lax.axis_index("z")
    xh = lax.axis_index("xh")
    core = lax.axis_index("core")
    y = lax.axis_index("y")
    scalars = jnp.stack([xh, 1 - xh, y, xl]).astype(jnp.int32)

    packed, rows = kernel_call(
        pack,
        [((2 * BLOCK, 256), BF16), ((Z, Y, 8, 256), BF16)],
        [HBM] * 3,
        1000,
        600000,
        (node_features, cotangent, proj_weights),
        (pltpu.VMEM((8, 4, 256), BF16), pltpu.SemaphoreType.DMA((3,))),
        60,
    )
    near = lax.all_to_all(rows, "z", 0, 0, tiled=True)
    p0 = lax.all_gather(packed, "y", axis=0)
    p1 = swapped(p0, "xh")
    (rows,) = kernel_call(
        spread, [((Y, XL, BLOCK, 256), BF16)], [VMEM], 1000, 800000, (near,)
    )
    weights = lax.all_to_all(
        rows.reshape(Y * XL, BLOCK, 256), ("y", "xl"), 0, 0, tiled=True
    ).reshape(4, 256, 256)
    x0 = lax.all_gather(p0[:, :BLOCK], "core", axis=0)
    c0 = lax.all_gather(p0[:, BLOCK:], "core", axis=0)
    x1 = lax.all_gather(p1[:, :BLOCK], "core", axis=0)

    shape = (Y, BLOCK, BLOCK)
    key_value, query = kernel_call(
        project_features,
        [((512, BLOCK), BF16), ((512, BLOCK), BF16)],
        [SMEM] + [VMEM] * 3,
        2 * 512 * 1024 * 256,
        2000000,
        (scalars, x0, x1, weights),
    )
    arrived = shifted(key_value, 1)
    p1, query = lax.optimization_barrier((p1, query))
    c1 = lax.all_gather(p1[:, BLOCK:], "core", axis=0)
    both, turned = kernel_call(
        project_cotangents,
        [((512, BLOCK), BF16), ((192, 1024), BF16)],
        [SMEM] + [VMEM] * 4,
        2 * 512 * 1024 * 128,
        3500000,
        (scalars, c0, c1, weights, query),
    )
    group_weights = [turned] + [
        lax.ppermute(turned, "y", [(i, (i - k) % Y) for i in range(Y)]) for k in range(1, Y)
    ]

    mask = lax.all_gather(local_mask, "y", axis=0).reshape(Y, 1)
    usable = (mask > 0) | jnp.eye(1, dtype=bool)
    wrap = (xl * Z + z == 0).reshape(1)
    flags = jnp.concatenate([wrap, usable.reshape(Y)]).astype(jnp.int32)
    local, back, grad_query = kernel_call(
        attend,
        [(shape, F32), (shape, F32), (shape, BF16)],
        [SMEM] + [VMEM] * 3,
        4 * 6 * 256 * 512 * 128,
        1000000,
        (flags, both.reshape(shape), key_value.reshape(shape), arrived.reshape(shape)),
    )
    returned = shifted(back, -1)
    returned, *group_weights[1:3] = lax.optimization_barrier((returned, *group_weights[1:3]))

    kept, sent, grads = kernel_call(
        weight_terms,
        [((Y, BLOCK, 256), F32), ((Y, BLOCK, 256), BF16), ((Y, 192, BLOCK), BF16)],
        [SMEM] + [VMEM] * 5,
        2 * 512 * 1024 * 256,
        2000000,
        (scalars, x0, x1, local, returned, grad_query),
    )
    grads, group_weights[3] = lax.optimization_barrier((grads, group_weights[3]))
    other = swapped(sent, "xl")
    grads = lax.all_to_all(grads, "y", 0, 0, tiled=True)
    grads, other = lax.optimization_barrier((grads, other))
    term = (kept + other.astype(F32)).astype(BF16)
    term, grads = lax.optimization_barrier((term, grads))
    term = lax.all_to_all(term.reshape(Y * Z, 8, 256), ("y", "z"), 0, 0, tiled=True)
    (partial,) = kernel_call(
        input_terms,
        [((4, BLOCK, 256), BF16)],
        [SMEM] + [VMEM] * 5,
        2 * 128 * 1024 * 1024,
        2500000,
        (scalars, grads, *group_weights),
    )
    partial = lax.all_gather(partial, "core", axis=0).reshape(CORE, XH, CORE, BLOCK, 256)
    partial = lax.dynamic_index_in_dim(partial, core, 2, keepdims=False)
    pair = jnp.sum(partial.astype(F32), axis=0)
    remote = lax.dynamic_index_in_dim(pair, 1 - xh, 0, keepdims=False)
    remote = lax.all_gather(remote, "xh", axis=0)
    remote = lax.dynamic_index_in_dim(remote, 1 - xh, 0, keepdims=False)
    pair = lax.dynamic_index_in_dim(pair, xh, 0, keepdims=False)
    input_grad = (pair + remote).astype(BF16)

    (weight_grads,) = kernel_call(
        sum_terms, [((8, 768), F32)], [VMEM], 1000000, 300000, (term,)
    )
    return (input_grad, weight_grads.reshape(8, 3, 256))


def solution(mesh):
    fine = Mesh(mesh.devices.reshape(Y, XL, Z, XH, CORE), AXES)
    head = ("xh", "core")
    return jax.shard_map(
        shards,
        mesh=fine,
        in_specs=(
            P(DOM, head),
            P(DOM, head),
            P(DOM, None, head),
            P(DOM, None),
            P(None, DOM),
        ),
        out_specs=(P(DOM, head), P(DOM, None, head)),
        check_vma=False,
    )
```

```python
import jax
import jax.numpy as jnp
from jax import lax
from jax.experimental import pallas as pl
from jax.experimental.pallas import tpu as pltpu
from jax.sharding import Mesh
from jax.sharding import PartitionSpec as P

HEAD_DIM = 64
BLOCK = 128
ROUNDS = 3
Y, XL, Z, XH, CORE = 4, 2, 16, 2, 2
AXES = ("y", "xl", "z", "xh", "core")
DOM = ("y", "xl", "z")
RING = ("xl", "z")
RING_SIZE = XL * Z
F32 = jnp.float32
BF16 = jnp.bfloat16
SMEM = pl.BlockSpec(memory_space=pltpu.SMEM)
VMEM = pl.BlockSpec(memory_space=pltpu.VMEM)
HBM = pl.BlockSpec(memory_space=pltpu.HBM)


def swapped(block, axis):
    return lax.ppermute(block, axis, [(0, 1), (1, 0)])


def shifted(block, distance):
    route = [(i, (i + distance) % RING_SIZE) for i in range(RING_SIZE)]
    return lax.ppermute(block, RING, route)


def matmul(left, right, dims):
    return lax.dot_general(left, right, (dims, ((), ())), preferred_element_type=F32)


def low_lanes(shape):
    return lax.broadcasted_iota(jnp.int32, shape, len(shape) - 1) < HEAD_DIM


def kernel_call(kernel, shapes, specs, flops, size, args, scratch=(), limit=16):
    return pl.pallas_call(
        kernel,
        out_shape=[jax.ShapeDtypeStruct(shape, dtype) for shape, dtype in shapes],
        in_specs=specs,
        out_specs=[VMEM] * len(shapes),
        scratch_shapes=list(scratch),
        compiler_params=pltpu.CompilerParams(vmem_limit_bytes=limit * 1024 * 1024),
        cost_estimate=pl.CostEstimate(flops=flops, bytes_accessed=size, transcendentals=0),
    )(*args)


def pack(features, cotangents, weights, packed, rows, held, arrivals):
    copies = [
        pltpu.make_async_copy(weights, held, arrivals.at[0]),
        pltpu.make_async_copy(features, packed.at[pl.ds(0, BLOCK)], arrivals.at[1]),
        pltpu.make_async_copy(cotangents, packed.at[pl.ds(BLOCK, BLOCK)], arrivals.at[2]),
    ]
    for copy in copies:
        copy.start()
    copies[0].wait()
    for quarter in range(Y):
        lower = quarter * HEAD_DIM
        part = jnp.concatenate(
            [held[:, t, lower : lower + HEAD_DIM] for t in (1, 2, 0, 3)], axis=1
        )
        rows[:, quarter] = jnp.broadcast_to(part[None], (Z, 8, 256))
    copies[1].wait()
    copies[2].wait()


def spread(gathered, rows):
    for quarter in range(Y):
        part = gathered[:, quarter].reshape(BLOCK, 256)
        rows[quarter, 0] = part
        rows[quarter, 1] = part


def project_features(scalars, x0, x1, weights, key_value, query):
    total = jnp.zeros((Y * BLOCK, 256), F32)
    for half, pair in enumerate((x0, x1)):
        for core in range(CORE):
            rows = weights[CORE * scalars[half] + core]
            total += matmul(pair[core].reshape(Y * BLOCK, 256), rows, ((1,), (0,)))
    key_value[...] = total[:, :BLOCK].astype(BF16)
    query[...] = total[:, BLOCK:].astype(BF16)


def project_cotangents(scalars, c0, c1, weights, query, both, turned):
    total = jnp.zeros((Y * BLOCK, BLOCK), F32)
    for half, pair in enumerate((c0, c1)):
        for core in range(CORE):
            rows = weights[CORE * scalars[half] + core, :, BLOCK:]
            total += matmul(pair[core].reshape(Y * BLOCK, 256), rows, ((1,), (0,)))
    low = low_lanes((Y * BLOCK, BLOCK))
    both[...] = jnp.where(low, query[...], total.astype(BF16))
    for quarter in range(Y):
        part = weights[quarter, :, : 3 * HEAD_DIM].T
        turned[:, quarter * 256 : (quarter + 1) * 256] = part


def attend(scalars, both, own, arrived, local, back, grad_query):
    scale = HEAD_DIM ** (-0.5)
    low = low_lanes((BLOCK, BLOCK))
    zero = jnp.zeros((BLOCK, BLOCK), BF16)
    wrap = scalars[0]
    back[...] = jnp.zeros((Y, BLOCK, BLOCK), F32)
    for block in range(Y):
        pair = both[block]
        stacked = jnp.concatenate(
            [jnp.where(low, pair, zero), jnp.where(low, zero, pair)], axis=0
        )
        sources = [lax.rem(block - r - wrap + 2 * Y, Y) for r in range(ROUNDS)]
        listed = jnp.concatenate([own[block]] + [arrived[s] for s in sources], axis=0)
        inner = matmul(stacked, listed, ((1,), (1,)))
        scores = inner[:BLOCK] * scale
        prob_grad = inner[BLOCK:]
        usable = scalars[1 + block] > 0
        local_scores = jnp.where(usable, scores[:, :BLOCK], -1e30)
        scores = jnp.concatenate([local_scores, scores[:, BLOCK:]], axis=1)
        exponent = jnp.exp(scores - jnp.max(scores, axis=1, keepdims=True))
        total = jnp.sum(exponent, axis=1, keepdims=True)
        probs = exponent * (1.0 / total)
        mean = jnp.sum(probs * prob_grad, axis=1, keepdims=True)
        score_grad = (probs * (prob_grad - mean) * scale).astype(BF16)
        query_side = matmul(score_grad, listed, ((1,), (0,)))
        query_side = jnp.where(low, query_side, pltpu.roll(query_side, HEAD_DIM, 1))
        grad_query[block] = query_side.astype(BF16)
        terms = jnp.concatenate([score_grad, probs.astype(BF16)], axis=0)
        key_side = matmul(terms, stacked, ((0,), (0,)))
        local[block] = key_side[:BLOCK]
        for r in range(ROUNDS):
            lower = (1 + r) * BLOCK
            part = key_side[lower : lower + BLOCK].astype(BF16).astype(F32)
            back[sources[r]] += part


def weight_terms(scalars, x0, x1, local, returned, grad_query, bundle, both):
    sides = (local[...] + returned[...]).astype(BF16)
    both[...] = jnp.concatenate([sides, grad_query[...]], axis=2)
    for block in range(Y):
        turned = sides[block].T
        turned = jnp.concatenate([turned[:HEAD_DIM], turned[HEAD_DIM:]], axis=1)
        for part in range(XL):
            bundle[block, part, BLOCK:] = turned
    right = both[...].reshape(Y * BLOCK, 256)
    terms = lax.broadcasted_iota(jnp.int32, (BLOCK, 256), 1) < 3 * HEAD_DIM
    for half, pair in enumerate((x0, x1)):
        for core in range(CORE):
            product = matmul(pair[core].reshape(Y * BLOCK, 256), right, ((0,), (0,)))
            product = product.astype(BF16)
            quarter = CORE * scalars[half] + core
            for part in range(XL):
                rows = product[part * BLOCK : (part + 1) * BLOCK]
                bundle[quarter, part, :BLOCK] = jnp.where(terms, rows, both[quarter])


def add_terms(bundle, out):
    for source in range(Y):
        near, far = bundle[XL * source, :BLOCK], bundle[XL * source + 1, :BLOCK]
        total = (near.astype(F32) + far.astype(F32)).astype(BF16)
        for place, lower in ((1, 0), (2, HEAD_DIM), (0, 2 * HEAD_DIM)):
            at = place * 256 + source * HEAD_DIM
            out[:, at : at + HEAD_DIM] = total[:, lower : lower + HEAD_DIM]


def input_terms(scalars, bundle, w0, w1, w2, w3, out):
    sides, queries = [], []
    for slot in range(Y):
        entry = XL * lax.rem(scalars[2] + slot, Y) + scalars[3]
        folded = bundle[entry, BLOCK:]
        sides.append(jnp.concatenate([folded[:, :BLOCK], folded[:, BLOCK:]], axis=0))
        queries.append(bundle[entry, :BLOCK, 3 * HEAD_DIM :])
    for quarter in range(4):
        total = jnp.zeros((BLOCK, 256), F32)
        lower = quarter * 256
        for side, query, weights in zip(sides, queries, (w0, w1, w2, w3)):
            columns = weights[:, lower : lower + 256]
            total += matmul(side, columns[: 2 * HEAD_DIM], ((0,), (0,)))
            total += matmul(query, columns[2 * HEAD_DIM :], ((1,), (0,)))
        out[quarter] = total.astype(BF16)


def sum_terms(terms, out):
    out[...] = jnp.sum(terms[...].astype(F32), axis=0)


def shards(node_features, cotangent, proj_weights, local_mask, matching):
    xl = lax.axis_index("xl")
    z = lax.axis_index("z")
    xh = lax.axis_index("xh")
    core = lax.axis_index("core")
    y = lax.axis_index("y")
    scalars = jnp.stack([xh, 1 - xh, y, xl]).astype(jnp.int32)

    packed, rows = kernel_call(
        pack,
        [((2 * BLOCK, 256), BF16), ((Z, Y, 8, 256), BF16)],
        [HBM] * 3,
        1000,
        600000,
        (node_features, cotangent, proj_weights),
        (pltpu.VMEM((8, 4, 256), BF16), pltpu.SemaphoreType.DMA((3,))),
        60,
    )
    near = lax.all_to_all(rows, "z", 0, 0, tiled=True)
    p0 = lax.all_gather(packed, "y", axis=0)
    p1 = swapped(p0, "xh")
    (rows,) = kernel_call(
        spread, [((Y, XL, BLOCK, 256), BF16)], [VMEM], 1000, 800000, (near,)
    )
    weights = lax.all_to_all(
        rows.reshape(Y * XL, BLOCK, 256), ("y", "xl"), 0, 0, tiled=True
    ).reshape(4, 256, 256)
    x0 = lax.all_gather(p0[:, :BLOCK], "core", axis=0)
    c0 = lax.all_gather(p0[:, BLOCK:], "core", axis=0)
    x1 = lax.all_gather(p1[:, :BLOCK], "core", axis=0)

    shape = (Y, BLOCK, BLOCK)
    key_value, query = kernel_call(
        project_features,
        [((512, BLOCK), BF16), ((512, BLOCK), BF16)],
        [SMEM] + [VMEM] * 3,
        2 * 512 * 1024 * 256,
        2000000,
        (scalars, x0, x1, weights),
    )
    arrived = shifted(key_value, 1)
    p1, query = lax.optimization_barrier((p1, query))
    c1 = lax.all_gather(p1[:, BLOCK:], "core", axis=0)
    both, turned = kernel_call(
        project_cotangents,
        [((512, BLOCK), BF16), ((192, 1024), BF16)],
        [SMEM] + [VMEM] * 4,
        2 * 512 * 1024 * 128,
        3500000,
        (scalars, c0, c1, weights, query),
    )
    group_weights = [turned] + [
        lax.ppermute(turned, "y", [(i, (i - k) % Y) for i in range(Y)]) for k in range(1, Y)
    ]

    mask = lax.all_gather(local_mask, "y", axis=0).reshape(Y, 1)
    usable = (mask > 0) | jnp.eye(1, dtype=bool)
    wrap = (xl * Z + z == 0).reshape(1)
    flags = jnp.concatenate([wrap, usable.reshape(Y)]).astype(jnp.int32)
    local, back, grad_query = kernel_call(
        attend,
        [(shape, F32), (shape, F32), (shape, BF16)],
        [SMEM] + [VMEM] * 3,
        4 * 6 * 256 * 512 * 128,
        1000000,
        (flags, both.reshape(shape), key_value.reshape(shape), arrived.reshape(shape)),
    )
    returned = shifted(back, -1)
    returned, group_weights[2] = lax.optimization_barrier((returned, group_weights[2]))

    (bundle,) = kernel_call(
        weight_terms,
        [((Y, XL, 192, 256), BF16)],
        [SMEM] + [VMEM] * 5,
        1500 * 1000000,
        2000000,
        (scalars, x0, x1, local, returned, grad_query),
        (pltpu.VMEM((Y, BLOCK, 256), BF16),),
    )
    bundle, group_weights[1], group_weights[3] = lax.optimization_barrier(
        (bundle, group_weights[1], group_weights[3])
    )
    bundle = lax.all_to_all(
        bundle.reshape(Y * XL, 192, 256), ("y", "xl"), 0, 0, tiled=True
    )
    (term,) = kernel_call(
        add_terms, [((BLOCK, 768), BF16)], [VMEM], 1000000, 800000, (bundle,)
    )
    term, bundle = lax.optimization_barrier((term, bundle))
    term = lax.all_to_all(term.reshape(Z, 8, 768), "z", 0, 0, tiled=True)
    (partial,) = kernel_call(
        input_terms,
        [((4, BLOCK, 256), BF16)],
        [SMEM] + [VMEM] * 5,
        2 * 128 * 1024 * 1024,
        2500000,
        (scalars, bundle, *group_weights),
    )
    partial = lax.all_gather(partial, "core", axis=0).reshape(CORE, XH, CORE, BLOCK, 256)
    partial = lax.dynamic_index_in_dim(partial, core, 2, keepdims=False)
    pair = jnp.sum(partial.astype(F32), axis=0)
    remote = lax.dynamic_index_in_dim(pair, 1 - xh, 0, keepdims=False)
    remote = lax.all_gather(remote, "xh", axis=0)
    remote = lax.dynamic_index_in_dim(remote, 1 - xh, 0, keepdims=False)
    pair = lax.dynamic_index_in_dim(pair, xh, 0, keepdims=False)
    input_grad = (pair + remote).astype(BF16)

    (weight_grads,) = kernel_call(
        sum_terms, [((8, 768), F32)], [VMEM], 1000000, 300000, (term,)
    )
    return (input_grad, weight_grads.reshape(8, 3, 256))


def solution(mesh):
    fine = Mesh(mesh.devices.reshape(Y, XL, Z, XH, CORE), AXES)
    head = ("xh", "core")
    return jax.shard_map(
        shards,
        mesh=fine,
        in_specs=(
            P(DOM, head),
            P(DOM, head),
            P(DOM, None, head),
            P(DOM, None),
            P(None, DOM),
        ),
        out_specs=(P(DOM, head), P(DOM, None, head)),
        check_vma=False,
    )
```

```python
import jax
import jax.numpy as jnp
from jax import lax
from jax.experimental import pallas as pl
from jax.experimental.pallas import tpu as pltpu
from jax.sharding import Mesh
from jax.sharding import PartitionSpec as P

HEAD_DIM = 64
BLOCK = 128
ROUNDS = 3
Y, XL, Z, XH, CORE = 4, 2, 16, 2, 2
AXES = ("y", "xl", "z", "xh", "core")
DOM = ("y", "xl", "z")
RING = ("xl", "z")
RING_SIZE = XL * Z
F32 = jnp.float32
BF16 = jnp.bfloat16
SMEM = pl.BlockSpec(memory_space=pltpu.SMEM)
VMEM = pl.BlockSpec(memory_space=pltpu.VMEM)
HBM = pl.BlockSpec(memory_space=pltpu.HBM)


def swapped(block, axis):
    return lax.ppermute(block, axis, [(0, 1), (1, 0)])


def shifted(block, distance):
    route = [(i, (i + distance) % RING_SIZE) for i in range(RING_SIZE)]
    return lax.ppermute(block, RING, route)


def matmul(left, right, dims):
    return lax.dot_general(left, right, (dims, ((), ())), preferred_element_type=F32)


def low_lanes(shape):
    return lax.broadcasted_iota(jnp.int32, shape, len(shape) - 1) < HEAD_DIM


def kernel_call(kernel, shapes, specs, flops, size, args, scratch=(), limit=16):
    return pl.pallas_call(
        kernel,
        out_shape=[jax.ShapeDtypeStruct(shape, dtype) for shape, dtype in shapes],
        in_specs=specs,
        out_specs=[VMEM] * len(shapes),
        scratch_shapes=list(scratch),
        compiler_params=pltpu.CompilerParams(vmem_limit_bytes=limit * 1024 * 1024),
        cost_estimate=pl.CostEstimate(flops=flops, bytes_accessed=size, transcendentals=0),
    )(*args)


def pack(features, cotangents, weights, packed, rows, held, arrivals):
    copies = [
        pltpu.make_async_copy(weights, held, arrivals.at[0]),
        pltpu.make_async_copy(features, packed.at[pl.ds(0, BLOCK)], arrivals.at[1]),
        pltpu.make_async_copy(cotangents, packed.at[pl.ds(BLOCK, BLOCK)], arrivals.at[2]),
    ]
    for copy in copies:
        copy.start()
    copies[0].wait()
    for quarter in range(Y):
        lower = quarter * HEAD_DIM
        part = jnp.concatenate(
            [held[:, t, lower : lower + HEAD_DIM] for t in (1, 2, 0, 3)], axis=1
        )
        rows[:, quarter] = jnp.broadcast_to(part[None], (Z, 8, 256))
    copies[1].wait()
    copies[2].wait()


def spread(gathered, rows):
    for quarter in range(Y):
        part = gathered[:, quarter].reshape(BLOCK, 256)
        rows[quarter, 0] = part
        rows[quarter, 1] = part


def project_features(scalars, x0, x1, weights, key_value, query):
    total = jnp.zeros((Y * BLOCK, 256), F32)
    for half, pair in enumerate((x0, x1)):
        for core in range(CORE):
            rows = weights[CORE * scalars[half] + core]
            total += matmul(pair[core].reshape(Y * BLOCK, 256), rows, ((1,), (0,)))
    key_value[...] = total[:, :BLOCK].astype(BF16)
    query[...] = total[:, BLOCK:].astype(BF16)


def project_cotangents(scalars, c0, c1, weights, query, both, turned):
    total = jnp.zeros((Y * BLOCK, BLOCK), F32)
    for half, pair in enumerate((c0, c1)):
        for core in range(CORE):
            rows = weights[CORE * scalars[half] + core, :, BLOCK:]
            total += matmul(pair[core].reshape(Y * BLOCK, 256), rows, ((1,), (0,)))
    low = low_lanes((Y * BLOCK, BLOCK))
    both[...] = jnp.where(low, query[...], total.astype(BF16))
    for quarter in range(Y):
        part = weights[quarter, :, : 3 * HEAD_DIM].T
        turned[:, quarter * 256 : (quarter + 1) * 256] = part


def attend(scalars, both, own, arrived, local, back, grad_query):
    scale = HEAD_DIM ** (-0.5)
    low = low_lanes((BLOCK, BLOCK))
    zero = jnp.zeros((BLOCK, BLOCK), BF16)
    wrap = scalars[0]
    back[...] = jnp.zeros((Y, BLOCK, BLOCK), F32)
    for block in range(Y):
        pair = both[block]
        stacked = jnp.concatenate(
            [jnp.where(low, pair, zero), jnp.where(low, zero, pair)], axis=0
        )
        sources = [lax.rem(block - r - wrap + 2 * Y, Y) for r in range(ROUNDS)]
        listed = jnp.concatenate([own[block]] + [arrived[s] for s in sources], axis=0)
        inner = matmul(stacked, listed, ((1,), (1,)))
        scores = inner[:BLOCK] * scale
        prob_grad = inner[BLOCK:]
        usable = scalars[1 + block] > 0
        local_scores = jnp.where(usable, scores[:, :BLOCK], -1e30)
        scores = jnp.concatenate([local_scores, scores[:, BLOCK:]], axis=1)
        exponent = jnp.exp(scores - jnp.max(scores, axis=1, keepdims=True))
        total = jnp.sum(exponent, axis=1, keepdims=True)
        probs = exponent * (1.0 / total)
        mean = jnp.sum(probs * prob_grad, axis=1, keepdims=True)
        score_grad = (probs * (prob_grad - mean) * scale).astype(BF16)
        query_side = matmul(score_grad, listed, ((1,), (0,)))
        query_side = jnp.where(low, query_side, pltpu.roll(query_side, HEAD_DIM, 1))
        grad_query[block] = query_side.astype(BF16)
        terms = jnp.concatenate([score_grad, probs.astype(BF16)], axis=0)
        key_side = matmul(terms, stacked, ((0,), (0,)))
        local[block] = key_side[:BLOCK]
        for r in range(ROUNDS):
            lower = (1 + r) * BLOCK
            part = key_side[lower : lower + BLOCK].astype(BF16).astype(F32)
            back[sources[r]] += part


def weight_terms(scalars, x0, x1, local, returned, grad_query, bundle, both):
    sides = (local[...] + returned[...]).astype(BF16)
    both[...] = jnp.concatenate([sides, grad_query[...]], axis=2)
    for block in range(Y):
        turned = sides[block].T
        turned = jnp.concatenate([turned[:HEAD_DIM], turned[HEAD_DIM:]], axis=1)
        for part in range(XL):
            bundle[block, part, BLOCK:] = turned
    right = both[...].reshape(Y * BLOCK, 256)
    terms = lax.broadcasted_iota(jnp.int32, (BLOCK, 256), 1) < 3 * HEAD_DIM
    for half, pair in enumerate((x0, x1)):
        for core in range(CORE):
            product = matmul(pair[core].reshape(Y * BLOCK, 256), right, ((0,), (0,)))
            product = product.astype(BF16)
            quarter = CORE * scalars[half] + core
            for part in range(XL):
                rows = product[part * BLOCK : (part + 1) * BLOCK]
                bundle[quarter, part, :BLOCK] = jnp.where(terms, rows, both[quarter])


def add_terms(bundle, out):
    for source in range(Y):
        near, far = bundle[XL * source, :BLOCK], bundle[XL * source + 1, :BLOCK]
        total = (near.astype(F32) + far.astype(F32)).astype(BF16)
        for place, lower in ((1, 0), (2, HEAD_DIM), (0, 2 * HEAD_DIM)):
            at = place * 256 + source * HEAD_DIM
            out[:, at : at + HEAD_DIM] = total[:, lower : lower + HEAD_DIM]


def input_terms(scalars, bundle, w0, w1, w2, w3, out):
    sides, queries = [], []
    for slot in range(Y):
        entry = XL * lax.rem(scalars[2] + slot, Y) + scalars[3]
        folded = bundle[entry, BLOCK:]
        sides.append(jnp.concatenate([folded[:, :BLOCK], folded[:, BLOCK:]], axis=0))
        queries.append(bundle[entry, :BLOCK, 3 * HEAD_DIM :])
    for quarter in range(4):
        total = jnp.zeros((BLOCK, 256), F32)
        lower = quarter * 256
        for side, query, weights in zip(sides, queries, (w0, w1, w2, w3)):
            columns = weights[:, lower : lower + 256]
            total += matmul(side, columns[: 2 * HEAD_DIM], ((0,), (0,)))
            total += matmul(query, columns[2 * HEAD_DIM :], ((1,), (0,)))
        out[quarter] = total.astype(BF16)


def sum_terms(terms, out):
    out[...] = jnp.sum(terms[...].astype(F32), axis=0)


def shards(node_features, cotangent, proj_weights, local_mask, matching):
    xl = lax.axis_index("xl")
    z = lax.axis_index("z")
    xh = lax.axis_index("xh")
    core = lax.axis_index("core")
    y = lax.axis_index("y")
    scalars = jnp.stack([xh, 1 - xh, y, xl]).astype(jnp.int32)

    packed, rows = kernel_call(
        pack,
        [((2 * BLOCK, 256), BF16), ((Z, Y, 8, 256), BF16)],
        [HBM] * 3,
        1000,
        600000,
        (node_features, cotangent, proj_weights),
        (pltpu.VMEM((8, 4, 256), BF16), pltpu.SemaphoreType.DMA((3,))),
        60,
    )
    near = lax.all_to_all(rows, "z", 0, 0, tiled=True)
    p0 = lax.all_gather(packed, "y", axis=0)
    p1 = swapped(p0, "xh")
    (rows,) = kernel_call(
        spread, [((Y, XL, BLOCK, 256), BF16)], [VMEM], 1000, 800000, (near,)
    )
    weights = lax.all_to_all(
        rows.reshape(Y * XL, BLOCK, 256), ("y", "xl"), 0, 0, tiled=True
    ).reshape(4, 256, 256)
    x0 = lax.all_gather(p0[:, :BLOCK], "core", axis=0)
    c0 = lax.all_gather(p0[:, BLOCK:], "core", axis=0)
    x1 = lax.all_gather(p1[:, :BLOCK], "core", axis=0)

    shape = (Y, BLOCK, BLOCK)
    key_value, query = kernel_call(
        project_features,
        [((512, BLOCK), BF16), ((512, BLOCK), BF16)],
        [SMEM] + [VMEM] * 3,
        2 * 512 * 1024 * 256,
        2000000,
        (scalars, x0, x1, weights),
    )
    arrived = shifted(key_value, 1)
    p1, query = lax.optimization_barrier((p1, query))
    c1 = lax.all_gather(p1[:, BLOCK:], "core", axis=0)
    both, turned = kernel_call(
        project_cotangents,
        [((512, BLOCK), BF16), ((192, 1024), BF16)],
        [SMEM] + [VMEM] * 4,
        2 * 512 * 1024 * 128,
        3500000,
        (scalars, c0, c1, weights, query),
    )
    group_weights = [turned] + [
        lax.ppermute(turned, "y", [(i, (i - k) % Y) for i in range(Y)]) for k in range(1, Y)
    ]

    mask = lax.all_gather(local_mask, "y", axis=0).reshape(Y, 1)
    usable = (mask > 0) | jnp.eye(1, dtype=bool)
    wrap = (xl * Z + z == 0).reshape(1)
    flags = jnp.concatenate([wrap, usable.reshape(Y)]).astype(jnp.int32)
    local, back, grad_query = kernel_call(
        attend,
        [(shape, F32), (shape, F32), (shape, BF16)],
        [SMEM] + [VMEM] * 3,
        4 * 6 * 256 * 512 * 128,
        1000000,
        (flags, both.reshape(shape), key_value.reshape(shape), arrived.reshape(shape)),
    )
    returned = shifted(back, -1)
    returned, group_weights[2] = lax.optimization_barrier((returned, group_weights[2]))

    (bundle,) = kernel_call(
        weight_terms,
        [((Y, XL, 192, 256), BF16)],
        [SMEM] + [VMEM] * 5,
        2 * 512 * 1024 * 256,
        2000000,
        (scalars, x0, x1, local, returned, grad_query),
        (pltpu.VMEM((Y, BLOCK, 256), BF16),),
    )
    bundle, group_weights[1], group_weights[3] = lax.optimization_barrier(
        (bundle, group_weights[1], group_weights[3])
    )
    bundle = lax.all_to_all(
        bundle.reshape(Y * XL, 192, 256), ("y", "xl"), 0, 0, tiled=True
    )
    (term,) = kernel_call(
        add_terms, [((BLOCK, 768), BF16)], [VMEM], 1000000, 800000, (bundle,)
    )
    term, bundle = lax.optimization_barrier((term, bundle))
    term = lax.all_to_all(term.reshape(Z, 8, 768), "z", 0, 0, tiled=True)
    (partial,) = kernel_call(
        input_terms,
        [((4, BLOCK, 256), BF16)],
        [SMEM] + [VMEM] * 5,
        2 * 128 * 1024 * 1024,
        2500000,
        (scalars, bundle, *group_weights),
    )
    partial = lax.all_gather(partial, "core", axis=0).reshape(CORE, XH, CORE, BLOCK, 256)
    partial = lax.dynamic_index_in_dim(partial, core, 2, keepdims=False)
    pair = jnp.sum(partial.astype(F32), axis=0)
    remote = lax.dynamic_index_in_dim(pair, 1 - xh, 0, keepdims=False)
    remote = lax.all_gather(remote, "xh", axis=0)
    remote = lax.dynamic_index_in_dim(remote, 1 - xh, 0, keepdims=False)
    pair = lax.dynamic_index_in_dim(pair, xh, 0, keepdims=False)
    input_grad = (pair + remote).astype(BF16)

    (weight_grads,) = kernel_call(
        sum_terms, [((8, 768), F32)], [VMEM], 1000000, 300000, (term,)
    )
    return (input_grad, weight_grads.reshape(8, 3, 256))


def solution(mesh):
    fine = Mesh(mesh.devices.reshape(Y, XL, Z, XH, CORE), AXES)
    head = ("xh", "core")
    return jax.shard_map(
        shards,
        mesh=fine,
        in_specs=(
            P(DOM, head),
            P(DOM, head),
            P(DOM, None, head),
            P(DOM, None),
            P(None, DOM),
        ),
        out_specs=(P(DOM, head), P(DOM, None, head)),
        check_vma=False,
    )
```

```python
import jax
import jax.numpy as jnp
from jax import lax
from jax.experimental import pallas as pl
from jax.experimental.pallas import tpu as pltpu
from jax.sharding import Mesh
from jax.sharding import PartitionSpec as P

HEAD_DIM = 64
BLOCK = 128
ROUNDS = 3
Y, XL, Z, XH, CORE = 4, 2, 16, 2, 2
AXES = ("y", "xl", "z", "xh", "core")
DOM = ("y", "xl", "z")
RING = ("xl", "z")
RING_SIZE = XL * Z
F32 = jnp.float32
BF16 = jnp.bfloat16
SMEM = pl.BlockSpec(memory_space=pltpu.SMEM)
VMEM = pl.BlockSpec(memory_space=pltpu.VMEM)
HBM = pl.BlockSpec(memory_space=pltpu.HBM)


def swapped(block, axis):
    return lax.ppermute(block, axis, [(0, 1), (1, 0)])


def shifted(block, distance):
    route = [(i, (i + distance) % RING_SIZE) for i in range(RING_SIZE)]
    return lax.ppermute(block, RING, route)


def matmul(left, right, dims):
    return lax.dot_general(left, right, (dims, ((), ())), preferred_element_type=F32)


def low_lanes(shape):
    return lax.broadcasted_iota(jnp.int32, shape, len(shape) - 1) < HEAD_DIM


def kernel_call(kernel, shapes, specs, flops, size, args, scratch=(), limit=16):
    return pl.pallas_call(
        kernel,
        out_shape=[jax.ShapeDtypeStruct(shape, dtype) for shape, dtype in shapes],
        in_specs=specs,
        out_specs=[VMEM] * len(shapes),
        scratch_shapes=list(scratch),
        compiler_params=pltpu.CompilerParams(vmem_limit_bytes=limit * 1024 * 1024),
        cost_estimate=pl.CostEstimate(flops=flops, bytes_accessed=size, transcendentals=0),
    )(*args)


def pack(features, cotangents, weights, packed, rows, held, arrivals):
    copies = [
        pltpu.make_async_copy(weights, held, arrivals.at[0]),
        pltpu.make_async_copy(features, packed.at[pl.ds(0, BLOCK)], arrivals.at[1]),
        pltpu.make_async_copy(cotangents, packed.at[pl.ds(BLOCK, BLOCK)], arrivals.at[2]),
    ]
    for copy in copies:
        copy.start()
    copies[0].wait()
    for quarter in range(Y):
        lower = quarter * HEAD_DIM
        part = jnp.concatenate(
            [held[:, t, lower : lower + HEAD_DIM] for t in (1, 2, 0, 3)], axis=1
        )
        rows[:, quarter] = jnp.broadcast_to(part[None], (Z, 8, 256))
    copies[1].wait()
    copies[2].wait()


def spread(gathered, rows):
    for quarter in range(Y):
        part = gathered[:, quarter].reshape(BLOCK, 256)
        rows[quarter, 0] = part
        rows[quarter, 1] = part


def project_features(scalars, x0, x1, weights, key_value, query):
    total = jnp.zeros((Y * BLOCK, 256), F32)
    for half, pair in enumerate((x0, x1)):
        for core in range(CORE):
            rows = weights[CORE * scalars[half] + core]
            total += matmul(pair[core].reshape(Y * BLOCK, 256), rows, ((1,), (0,)))
    key_value[...] = total[:, :BLOCK].astype(BF16)
    query[...] = total[:, BLOCK:].astype(BF16)


def project_cotangents(scalars, c0, c1, weights, key_value, query, both, turned):
    total = jnp.zeros((Y * BLOCK, BLOCK), F32)
    for half, pair in enumerate((c0, c1)):
        for core in range(CORE):
            rows = weights[CORE * scalars[half] + core, :, BLOCK:]
            total += matmul(pair[core].reshape(Y * BLOCK, 256), rows, ((1,), (0,)))
    low = low_lanes((Y * BLOCK, BLOCK))
    both[:, :BLOCK] = key_value[...]
    both[:, BLOCK:] = jnp.where(low, query[...], total.astype(BF16))
    for quarter in range(Y):
        part = weights[quarter, :, : 3 * HEAD_DIM].T
        turned[:, quarter * 256 : (quarter + 1) * 256] = part


def attention(pair, listed, usable):
    scale = HEAD_DIM ** (-0.5)
    low = low_lanes((BLOCK, BLOCK))
    zero = jnp.zeros((BLOCK, BLOCK), BF16)
    stacked = jnp.concatenate(
        [jnp.where(low, pair, zero), jnp.where(low, zero, pair)], axis=0
    )
    inner = matmul(stacked, listed, ((1,), (1,)))
    scores = inner[:BLOCK] * scale
    prob_grad = inner[BLOCK:]
    local_scores = jnp.where(usable, scores[:, :BLOCK], -1e30)
    scores = jnp.concatenate([local_scores, scores[:, BLOCK:]], axis=1)
    exponent = jnp.exp(scores - jnp.max(scores, axis=1, keepdims=True))
    total = jnp.sum(exponent, axis=1, keepdims=True)
    probs = exponent * (1.0 / total)
    mean = jnp.sum(probs * prob_grad, axis=1, keepdims=True)
    score_grad = (probs * (prob_grad - mean) * scale).astype(BF16)
    return stacked, score_grad, probs.astype(BF16)


def matched(block, wrap):
    return [lax.rem(block - r - wrap + 2 * Y, Y) for r in range(ROUNDS)]


def gradients(scalars, flags, mine, ahead, arrived, x0, x1, bundle, total, both):
    low = low_lanes((BLOCK, BLOCK))
    for block in range(Y):
        listed = [mine[block, :, :BLOCK]] + [arrived[s] for s in matched(block, flags[0])]
        listed = jnp.concatenate(listed, axis=0)
        stacked, score_grad, probs = attention(
            mine[block, :, BLOCK:], listed, flags[2 + block] > 0
        )
        query_side = matmul(score_grad, listed, ((1,), (0,)))
        query_side = jnp.where(low, query_side, pltpu.roll(query_side, HEAD_DIM, 1))
        both[block, :, BLOCK:] = query_side.astype(BF16)
        terms = jnp.concatenate([score_grad[:, :BLOCK], probs[:, :BLOCK]], axis=0)
        total[block] = matmul(terms, stacked, ((0,), (0,)))
    for block in range(Y):
        sources = matched(block, flags[1])
        listed = [ahead[block, :, :BLOCK]] + [mine[s, :, :BLOCK] for s in sources]
        listed = jnp.concatenate(listed, axis=0)
        stacked, score_grad, probs = attention(
            ahead[block, :, BLOCK:], listed, flags[2 + Y + block] > 0
        )
        terms = jnp.concatenate([score_grad[:, BLOCK:], probs[:, BLOCK:]], axis=0)
        side = matmul(terms, stacked, ((0,), (0,)))
        for r in range(ROUNDS):
            part = side[r * BLOCK : (r + 1) * BLOCK].astype(BF16).astype(F32)
            total[sources[r]] += part
    for block in range(Y):
        side = total[block].astype(BF16)
        both[block, :, :BLOCK] = side
        turned = side.T
        turned = jnp.concatenate([turned[:HEAD_DIM], turned[HEAD_DIM:]], axis=1)
        for part in range(XL):
            bundle[block, part, BLOCK:] = turned
    right = both[...].reshape(Y * BLOCK, 256)
    terms = lax.broadcasted_iota(jnp.int32, (BLOCK, 256), 1) < 3 * HEAD_DIM
    for half, pair in enumerate((x0, x1)):
        for core in range(CORE):
            product = matmul(pair[core].reshape(Y * BLOCK, 256), right, ((0,), (0,)))
            product = product.astype(BF16)
            quarter = CORE * scalars[half] + core
            for part in range(XL):
                rows = product[part * BLOCK : (part + 1) * BLOCK]
                bundle[quarter, part, :BLOCK] = jnp.where(terms, rows, both[quarter])


def add_terms(bundle, out):
    for source in range(Y):
        near, far = bundle[XL * source, :BLOCK], bundle[XL * source + 1, :BLOCK]
        total = (near.astype(F32) + far.astype(F32)).astype(BF16)
        for place, lower in ((1, 0), (2, HEAD_DIM), (0, 2 * HEAD_DIM)):
            at = place * 256 + source * HEAD_DIM
            out[:, at : at + HEAD_DIM] = total[:, lower : lower + HEAD_DIM]


def input_terms(scalars, bundle, w0, w1, w2, w3, out):
    sides, queries = [], []
    for slot in range(Y):
        entry = XL * lax.rem(scalars[2] + slot, Y) + scalars[3]
        folded = bundle[entry, BLOCK:]
        sides.append(jnp.concatenate([folded[:, :BLOCK], folded[:, BLOCK:]], axis=0))
        queries.append(bundle[entry, :BLOCK, 3 * HEAD_DIM :])
    for quarter in range(4):
        total = jnp.zeros((BLOCK, 256), F32)
        lower = quarter * 256
        for side, query, weights in zip(sides, queries, (w0, w1, w2, w3)):
            columns = weights[:, lower : lower + 256]
            total += matmul(side, columns[: 2 * HEAD_DIM], ((0,), (0,)))
            total += matmul(query, columns[2 * HEAD_DIM :], ((1,), (0,)))
        out[quarter] = total.astype(BF16)


def sum_terms(terms, out):
    out[...] = jnp.sum(terms[...].astype(F32), axis=0)


def shards(node_features, cotangent, proj_weights, local_mask, matching):
    xl = lax.axis_index("xl")
    z = lax.axis_index("z")
    xh = lax.axis_index("xh")
    core = lax.axis_index("core")
    y = lax.axis_index("y")
    scalars = jnp.stack([xh, 1 - xh, y, xl]).astype(jnp.int32)

    packed, rows = kernel_call(
        pack,
        [((2 * BLOCK, 256), BF16), ((Z, Y, 8, 256), BF16)],
        [HBM] * 3,
        1000,
        600000,
        (node_features, cotangent, proj_weights),
        (pltpu.VMEM((8, 4, 256), BF16), pltpu.SemaphoreType.DMA((3,))),
        60,
    )
    near = lax.all_to_all(rows, "z", 0, 0, tiled=True)
    p0 = lax.all_gather(packed, "y", axis=0)
    p1 = swapped(p0, "xh")
    (rows,) = kernel_call(
        spread, [((Y, XL, BLOCK, 256), BF16)], [VMEM], 1000, 800000, (near,)
    )
    weights = lax.all_to_all(
        rows.reshape(Y * XL, BLOCK, 256), ("y", "xl"), 0, 0, tiled=True
    ).reshape(4, 256, 256)
    x0 = lax.all_gather(p0[:, :BLOCK], "core", axis=0)
    c0 = lax.all_gather(p0[:, BLOCK:], "core", axis=0)
    x1 = lax.all_gather(p1[:, :BLOCK], "core", axis=0)

    key_value, query = kernel_call(
        project_features,
        [((512, BLOCK), BF16), ((512, BLOCK), BF16)],
        [SMEM] + [VMEM] * 3,
        2 * 512 * 1024 * 256,
        2000000,
        (scalars, x0, x1, weights),
    )
    arrived = shifted(key_value, 1)
    p1, query = lax.optimization_barrier((p1, query))
    c1 = lax.all_gather(p1[:, BLOCK:], "core", axis=0)
    both, turned = kernel_call(
        project_cotangents,
        [((512, 256), BF16), ((192, 1024), BF16)],
        [SMEM] + [VMEM] * 5,
        2 * 512 * 1024 * 128,
        3500000,
        (scalars, c0, c1, weights, key_value, query),
    )
    ahead = shifted(both, -1)
    group_weights = [turned] + [
        lax.ppermute(turned, "y", [(i, (i - k) % Y) for i in range(Y)]) for k in range(1, Y)
    ]

    mask = lax.all_gather(local_mask, "y", axis=0).reshape(Y, 1)
    usable = (mask > 0) | jnp.eye(1, dtype=bool)
    next_usable = (shifted(mask, -1) > 0) | jnp.eye(1, dtype=bool)
    at = xl * Z + z
    wraps = jnp.stack([at == 0, at == RING_SIZE - 1])
    flags = jnp.concatenate([wraps, usable.reshape(Y), next_usable.reshape(Y)])
    (bundle,) = kernel_call(
        gradients,
        [((Y, XL, 192, 256), BF16)],
        [SMEM] * 2 + [VMEM] * 5,
        7 * 1000 * 1000 * 1000,
        3000000,
        (
            scalars,
            flags.astype(jnp.int32),
            both.reshape(Y, BLOCK, 256),
            ahead.reshape(Y, BLOCK, 256),
            arrived.reshape(Y, BLOCK, BLOCK),
            x0,
            x1,
        ),
        (pltpu.VMEM((Y, BLOCK, BLOCK), F32), pltpu.VMEM((Y, BLOCK, 256), BF16)),
    )
    bundle, *group_weights[1:] = lax.optimization_barrier((bundle, *group_weights[1:]))
    bundle = lax.all_to_all(
        bundle.reshape(Y * XL, 192, 256), ("y", "xl"), 0, 0, tiled=True
    )
    (term,) = kernel_call(
        add_terms, [((BLOCK, 768), BF16)], [VMEM], 1000000, 800000, (bundle,)
    )
    term, bundle = lax.optimization_barrier((term, bundle))
    term = lax.all_to_all(term.reshape(Z, 8, 768), "z", 0, 0, tiled=True)
    (partial,) = kernel_call(
        input_terms,
        [((4, BLOCK, 256), BF16)],
        [SMEM] + [VMEM] * 5,
        2 * 128 * 1024 * 1024,
        2500000,
        (scalars, bundle, *group_weights),
    )
    partial = lax.all_gather(partial, "core", axis=0).reshape(CORE, XH, CORE, BLOCK, 256)
    partial = lax.dynamic_index_in_dim(partial, core, 2, keepdims=False)
    pair = jnp.sum(partial.astype(F32), axis=0)
    remote = lax.dynamic_index_in_dim(pair, 1 - xh, 0, keepdims=False)
    remote = lax.all_gather(remote, "xh", axis=0)
    remote = lax.dynamic_index_in_dim(remote, 1 - xh, 0, keepdims=False)
    pair = lax.dynamic_index_in_dim(pair, xh, 0, keepdims=False)
    input_grad = (pair + remote).astype(BF16)

    (weight_grads,) = kernel_call(
        sum_terms, [((8, 768), F32)], [VMEM], 1000000, 300000, (term,)
    )
    return (input_grad, weight_grads.reshape(8, 3, 256))


def solution(mesh):
    fine = Mesh(mesh.devices.reshape(Y, XL, Z, XH, CORE), AXES)
    head = ("xh", "core")
    return jax.shard_map(
        shards,
        mesh=fine,
        in_specs=(
            P(DOM, head),
            P(DOM, head),
            P(DOM, None, head),
            P(DOM, None),
            P(None, DOM),
        ),
        out_specs=(P(DOM, head), P(DOM, None, head)),
        check_vma=False,
    )
```

```python
import jax
import jax.numpy as jnp
from jax import lax
from jax.experimental import pallas as pl
from jax.experimental.pallas import tpu as pltpu
from jax.sharding import Mesh
from jax.sharding import PartitionSpec as P

HEAD_DIM = 64
BLOCK = 128
ROUNDS = 3
Y, XL, Z, XH, CORE = 4, 2, 16, 2, 2
AXES = ("y", "xl", "z", "xh", "core")
DOM = ("y", "xl", "z")
RING = ("xl", "z")
RING_SIZE = XL * Z
F32 = jnp.float32
BF16 = jnp.bfloat16
SMEM = pl.BlockSpec(memory_space=pltpu.SMEM)
VMEM = pl.BlockSpec(memory_space=pltpu.VMEM)
HBM = pl.BlockSpec(memory_space=pltpu.HBM)


def swapped(block, axis):
    return lax.ppermute(block, axis, [(0, 1), (1, 0)])


def shifted(block, distance):
    route = [(i, (i + distance) % RING_SIZE) for i in range(RING_SIZE)]
    return lax.ppermute(block, RING, route)


def matmul(left, right, dims):
    return lax.dot_general(left, right, (dims, ((), ())), preferred_element_type=F32)


def low_lanes(shape):
    return lax.broadcasted_iota(jnp.int32, shape, len(shape) - 1) < HEAD_DIM


def kernel_call(kernel, shapes, specs, flops, size, args, scratch=(), limit=16):
    return pl.pallas_call(
        kernel,
        out_shape=[jax.ShapeDtypeStruct(shape, dtype) for shape, dtype in shapes],
        in_specs=specs,
        out_specs=[VMEM] * len(shapes),
        scratch_shapes=list(scratch),
        compiler_params=pltpu.CompilerParams(vmem_limit_bytes=limit * 1024 * 1024),
        cost_estimate=pl.CostEstimate(flops=flops, bytes_accessed=size, transcendentals=0),
    )(*args)


def pack(features, cotangents, weights, packed, rows, held, arrivals):
    copies = [
        pltpu.make_async_copy(weights, held, arrivals.at[0]),
        pltpu.make_async_copy(features, packed.at[pl.ds(0, BLOCK)], arrivals.at[1]),
        pltpu.make_async_copy(cotangents, packed.at[pl.ds(BLOCK, BLOCK)], arrivals.at[2]),
    ]
    for copy in copies:
        copy.start()
    copies[0].wait()
    for quarter in range(Y):
        lower = quarter * HEAD_DIM
        part = jnp.concatenate(
            [held[:, t, lower : lower + HEAD_DIM] for t in (1, 2, 0, 3)], axis=1
        )
        rows[:, quarter] = jnp.broadcast_to(part[None], (Z, 8, 256))
    copies[1].wait()
    copies[2].wait()


def spread(gathered, rows):
    for quarter in range(Y):
        part = gathered[:, quarter].reshape(BLOCK, 256)
        rows[quarter, 0] = part
        rows[quarter, 1] = part


def project_features(scalars, x0, x1, weights, key_value, query):
    total = jnp.zeros((Y * BLOCK, 256), F32)
    for half, pair in enumerate((x0, x1)):
        for core in range(CORE):
            rows = weights[CORE * scalars[half] + core]
            total += matmul(pair[core].reshape(Y * BLOCK, 256), rows, ((1,), (0,)))
    key_value[...] = total[:, :BLOCK].astype(BF16)
    query[...] = total[:, BLOCK:].astype(BF16)


def project_cotangents(scalars, c0, c1, weights, key_value, query, both, turned):
    total = jnp.zeros((Y * BLOCK, BLOCK), F32)
    for half, pair in enumerate((c0, c1)):
        for core in range(CORE):
            rows = weights[CORE * scalars[half] + core, :, BLOCK:]
            total += matmul(pair[core].reshape(Y * BLOCK, 256), rows, ((1,), (0,)))
    low = low_lanes((Y * BLOCK, BLOCK))
    both[:, :BLOCK] = key_value[...]
    both[:, BLOCK:] = jnp.where(low, query[...], total.astype(BF16))
    for quarter in range(Y):
        part = weights[quarter, :, : 3 * HEAD_DIM].T
        turned[:, quarter * 256 : (quarter + 1) * 256] = part


def attention(pair, listed, usable):
    scale = HEAD_DIM ** (-0.5)
    low = low_lanes((BLOCK, BLOCK))
    zero = jnp.zeros((BLOCK, BLOCK), BF16)
    stacked = jnp.concatenate(
        [jnp.where(low, pair, zero), jnp.where(low, zero, pair)], axis=0
    )
    inner = matmul(stacked, listed, ((1,), (1,)))
    scores = inner[:BLOCK] * scale
    prob_grad = inner[BLOCK:]
    local_scores = jnp.where(usable, scores[:, :BLOCK], -1e30)
    scores = jnp.concatenate([local_scores, scores[:, BLOCK:]], axis=1)
    exponent = jnp.exp(scores - jnp.max(scores, axis=1, keepdims=True))
    total = jnp.sum(exponent, axis=1, keepdims=True)
    probs = exponent * (1.0 / total)
    mean = jnp.sum(probs * prob_grad, axis=1, keepdims=True)
    score_grad = (probs * (prob_grad - mean) * scale).astype(BF16)
    return stacked, score_grad, probs.astype(BF16)


def matched(block, wrap):
    return [lax.rem(block - r - wrap + 2 * Y, Y) for r in range(ROUNDS)]


def gradients(scalars, flags, mine, ahead, arrived, x0, x1, bundle, total, both):
    low = low_lanes((BLOCK, BLOCK))
    for block in range(Y):
        listed = [mine[block, :, :BLOCK]] + [arrived[s] for s in matched(block, flags[0])]
        listed = jnp.concatenate(listed, axis=0)
        stacked, score_grad, probs = attention(
            mine[block, :, BLOCK:], listed, flags[2 + block] > 0
        )
        query_side = matmul(score_grad, listed, ((1,), (0,)))
        query_side = jnp.where(low, query_side, pltpu.roll(query_side, HEAD_DIM, 1))
        both[block, :, BLOCK:] = query_side.astype(BF16)
        terms = jnp.concatenate([score_grad[:, :BLOCK], probs[:, :BLOCK]], axis=0)
        total[block] = matmul(terms, stacked, ((0,), (0,)))
    for block in range(Y):
        sources = matched(block, flags[1])
        listed = [ahead[block, :, :BLOCK]] + [mine[s, :, :BLOCK] for s in sources]
        listed = jnp.concatenate(listed, axis=0)
        stacked, score_grad, probs = attention(
            ahead[block, :, BLOCK:], listed, flags[2 + Y + block] > 0
        )
        terms = jnp.concatenate([score_grad[:, BLOCK:], probs[:, BLOCK:]], axis=0)
        side = matmul(terms, stacked, ((0,), (0,)))
        for r in range(ROUNDS):
            part = side[r * BLOCK : (r + 1) * BLOCK].astype(BF16).astype(F32)
            total[sources[r]] += part
    for block in range(Y):
        side = total[block].astype(BF16)
        both[block, :, :BLOCK] = side
        turned = side.T
        turned = jnp.concatenate([turned[:HEAD_DIM], turned[HEAD_DIM:]], axis=1)
        for part in range(XL):
            bundle[block, part, BLOCK:] = turned
    right = both[...].reshape(Y * BLOCK, 256)
    terms = lax.broadcasted_iota(jnp.int32, (BLOCK, 256), 1) < 3 * HEAD_DIM
    for half, pair in enumerate((x0, x1)):
        for core in range(CORE):
            product = matmul(pair[core].reshape(Y * BLOCK, 256), right, ((0,), (0,)))
            product = product.astype(BF16)
            quarter = CORE * scalars[half] + core
            for part in range(XL):
                rows = product[part * BLOCK : (part + 1) * BLOCK]
                bundle[quarter, part, :BLOCK] = jnp.where(terms, rows, both[quarter])


def add_terms(bundle, out):
    for source in range(Y):
        near, far = bundle[XL * source, :BLOCK], bundle[XL * source + 1, :BLOCK]
        total = (near.astype(F32) + far.astype(F32)).astype(BF16)
        for place, lower in ((1, 0), (2, HEAD_DIM), (0, 2 * HEAD_DIM)):
            at = place * 256 + source * HEAD_DIM
            out[:, at : at + HEAD_DIM] = total[:, lower : lower + HEAD_DIM]


def input_terms(scalars, bundle, w0, w1, w2, w3, out):
    sides, queries = [], []
    for slot in range(Y):
        entry = XL * lax.rem(scalars[2] + slot, Y) + scalars[3]
        folded = bundle[entry, BLOCK:]
        sides.append(jnp.concatenate([folded[:, :BLOCK], folded[:, BLOCK:]], axis=0))
        queries.append(bundle[entry, :BLOCK, 3 * HEAD_DIM :])
    for quarter in range(4):
        total = jnp.zeros((BLOCK, 256), F32)
        lower = quarter * 256
        for side, query, weights in zip(sides, queries, (w0, w1, w2, w3)):
            columns = weights[:, lower : lower + 256]
            total += matmul(side, columns[: 2 * HEAD_DIM], ((0,), (0,)))
            total += matmul(query, columns[2 * HEAD_DIM :], ((1,), (0,)))
        out[quarter] = total.astype(BF16)


def sum_terms(terms, out):
    out[...] = jnp.sum(terms[...].astype(F32), axis=0)


def shards(node_features, cotangent, proj_weights, local_mask, matching):
    xl = lax.axis_index("xl")
    z = lax.axis_index("z")
    xh = lax.axis_index("xh")
    core = lax.axis_index("core")
    y = lax.axis_index("y")
    scalars = jnp.stack([xh, 1 - xh, y, xl]).astype(jnp.int32)

    packed, rows = kernel_call(
        pack,
        [((2 * BLOCK, 256), BF16), ((Z, Y, 8, 256), BF16)],
        [HBM] * 3,
        1000,
        600000,
        (node_features, cotangent, proj_weights),
        (pltpu.VMEM((8, 4, 256), BF16), pltpu.SemaphoreType.DMA((3,))),
        60,
    )
    near = lax.all_to_all(rows, "z", 0, 0, tiled=True)
    p0 = lax.all_gather(packed, "y", axis=0)
    p1 = swapped(p0, "xh")
    (rows,) = kernel_call(
        spread, [((Y, XL, BLOCK, 256), BF16)], [VMEM], 1000, 800000, (near,)
    )
    weights = lax.all_to_all(
        rows.reshape(Y * XL, BLOCK, 256), ("y", "xl"), 0, 0, tiled=True
    ).reshape(4, 256, 256)
    x0 = lax.all_gather(p0[:, :BLOCK], "core", axis=0)
    c0 = lax.all_gather(p0[:, BLOCK:], "core", axis=0)
    x1 = lax.all_gather(p1[:, :BLOCK], "core", axis=0)

    key_value, query = kernel_call(
        project_features,
        [((512, BLOCK), BF16), ((512, BLOCK), BF16)],
        [SMEM] + [VMEM] * 3,
        2 * 512 * 1024 * 256,
        2000000,
        (scalars, x0, x1, weights),
    )
    arrived = shifted(key_value, 1)
    p1, query = lax.optimization_barrier((p1, query))
    c1 = lax.all_gather(p1[:, BLOCK:], "core", axis=0)
    both, turned = kernel_call(
        project_cotangents,
        [((512, 256), BF16), ((192, 1024), BF16)],
        [SMEM] + [VMEM] * 5,
        2 * 512 * 1024 * 128,
        3500000,
        (scalars, c0, c1, weights, key_value, query),
    )
    ahead = shifted(both, -1)
    group_weights = [turned] + [
        lax.ppermute(turned, "y", [(i, (i - k) % Y) for i in range(Y)]) for k in range(1, Y)
    ]

    mask = lax.all_gather(local_mask, "y", axis=0).reshape(Y, 1)
    usable = (mask > 0) | jnp.eye(1, dtype=bool)
    next_usable = (shifted(mask, -1) > 0) | jnp.eye(1, dtype=bool)
    at = xl * Z + z
    wraps = jnp.stack([at == 0, at == RING_SIZE - 1])
    flags = jnp.concatenate([wraps, usable.reshape(Y), next_usable.reshape(Y)])
    (bundle,) = kernel_call(
        gradients,
        [((Y, XL, 192, 256), BF16)],
        [SMEM] * 2 + [VMEM] * 5,
        7 * 1000 * 1000 * 1000,
        3000000,
        (
            scalars,
            flags.astype(jnp.int32),
            both.reshape(Y, BLOCK, 256),
            ahead.reshape(Y, BLOCK, 256),
            arrived.reshape(Y, BLOCK, BLOCK),
            x0,
            x1,
        ),
        (pltpu.VMEM((Y, BLOCK, BLOCK), F32), pltpu.VMEM((Y, BLOCK, 256), BF16)),
    )
    bundle, group_weights[2] = lax.optimization_barrier((bundle, group_weights[2]))
    bundle = lax.all_to_all(
        bundle.reshape(Y * XL, 192, 256), ("y", "xl"), 0, 0, tiled=True
    )
    (term,) = kernel_call(
        add_terms, [((BLOCK, 768), BF16)], [VMEM], 1000000, 800000, (bundle,)
    )
    term, bundle = lax.optimization_barrier((term, bundle))
    term = lax.all_to_all(term.reshape(Z, 8, 768), "z", 0, 0, tiled=True)
    (partial,) = kernel_call(
        input_terms,
        [((4, BLOCK, 256), BF16)],
        [SMEM] + [VMEM] * 5,
        2 * 128 * 1024 * 1024,
        2500000,
        (scalars, bundle, *group_weights),
    )
    partial = lax.all_gather(partial, "core", axis=0).reshape(CORE, XH, CORE, BLOCK, 256)
    partial = lax.dynamic_index_in_dim(partial, core, 2, keepdims=False)
    pair = jnp.sum(partial.astype(F32), axis=0)
    remote = lax.dynamic_index_in_dim(pair, 1 - xh, 0, keepdims=False)
    remote = lax.all_gather(remote, "xh", axis=0)
    remote = lax.dynamic_index_in_dim(remote, 1 - xh, 0, keepdims=False)
    pair = lax.dynamic_index_in_dim(pair, xh, 0, keepdims=False)
    input_grad = (pair + remote).astype(BF16)

    (weight_grads,) = kernel_call(
        sum_terms, [((8, 768), F32)], [VMEM], 1000000, 300000, (term,)
    )
    return (input_grad, weight_grads.reshape(8, 3, 256))


def solution(mesh):
    fine = Mesh(mesh.devices.reshape(Y, XL, Z, XH, CORE), AXES)
    head = ("xh", "core")
    return jax.shard_map(
        shards,
        mesh=fine,
        in_specs=(
            P(DOM, head),
            P(DOM, head),
            P(DOM, None, head),
            P(DOM, None),
            P(None, DOM),
        ),
        out_specs=(P(DOM, head), P(DOM, None, head)),
        check_vma=False,
    )
```

```python
import jax
import jax.numpy as jnp
from jax import lax
from jax.experimental import pallas as pl
from jax.experimental.pallas import tpu as pltpu
from jax.sharding import Mesh
from jax.sharding import PartitionSpec as P

HEAD_DIM = 64
BLOCK = 128
ROUNDS = 3
Y, XL, Z, XH, CORE = 4, 2, 16, 2, 2
AXES = ("y", "xl", "z", "xh", "core")
DOM = ("y", "xl", "z")
RING = ("xl", "z")
RING_SIZE = XL * Z
F32 = jnp.float32
BF16 = jnp.bfloat16
SMEM = pl.BlockSpec(memory_space=pltpu.SMEM)
VMEM = pl.BlockSpec(memory_space=pltpu.VMEM)
HBM = pl.BlockSpec(memory_space=pltpu.HBM)


def swapped(block, axis):
    return lax.ppermute(block, axis, [(0, 1), (1, 0)])


def shifted(block, distance):
    route = [(i, (i + distance) % RING_SIZE) for i in range(RING_SIZE)]
    return lax.ppermute(block, RING, route)


def matmul(left, right, dims):
    return lax.dot_general(left, right, (dims, ((), ())), preferred_element_type=F32)


def low_lanes(shape):
    return lax.broadcasted_iota(jnp.int32, shape, len(shape) - 1) < HEAD_DIM


def kernel_call(kernel, shapes, specs, flops, size, args, scratch=(), limit=16):
    return pl.pallas_call(
        kernel,
        out_shape=[jax.ShapeDtypeStruct(shape, dtype) for shape, dtype in shapes],
        in_specs=specs,
        out_specs=[VMEM] * len(shapes),
        scratch_shapes=list(scratch),
        compiler_params=pltpu.CompilerParams(vmem_limit_bytes=limit * 1024 * 1024),
        cost_estimate=pl.CostEstimate(flops=flops, bytes_accessed=size, transcendentals=0),
    )(*args)


def pack(features, cotangents, weights, packed, rows, held, arrivals):
    copies = [
        pltpu.make_async_copy(weights, held, arrivals.at[0]),
        pltpu.make_async_copy(features, packed.at[pl.ds(0, BLOCK)], arrivals.at[1]),
        pltpu.make_async_copy(cotangents, packed.at[pl.ds(BLOCK, BLOCK)], arrivals.at[2]),
    ]
    for copy in copies:
        copy.start()
    copies[0].wait()
    for quarter in range(Y):
        lower = quarter * HEAD_DIM
        part = jnp.concatenate(
            [held[:, t, lower : lower + HEAD_DIM] for t in (1, 2, 0, 3)], axis=1
        )
        rows[:, quarter] = jnp.broadcast_to(part[None], (Z, 8, 256))
    copies[1].wait()
    copies[2].wait()


def spread(gathered, rows):
    for quarter in range(Y):
        part = gathered[:, quarter].reshape(BLOCK, 256)
        rows[quarter, 0] = part
        rows[quarter, 1] = part


def project_features(scalars, x0, x1, weights, key_value, query):
    total = jnp.zeros((Y * BLOCK, 256), F32)
    for half, pair in enumerate((x0, x1)):
        for core in range(CORE):
            rows = weights[CORE * scalars[half] + core]
            total += matmul(pair[core].reshape(Y * BLOCK, 256), rows, ((1,), (0,)))
    key_value[...] = total[:, :BLOCK].astype(BF16)
    query[...] = total[:, BLOCK:].astype(BF16)


def project_cotangents(scalars, c0, c1, weights, key_value, query, both, turned):
    total = jnp.zeros((Y * BLOCK, BLOCK), F32)
    for half, pair in enumerate((c0, c1)):
        for core in range(CORE):
            rows = weights[CORE * scalars[half] + core, :, BLOCK:]
            total += matmul(pair[core].reshape(Y * BLOCK, 256), rows, ((1,), (0,)))
    low = low_lanes((Y * BLOCK, BLOCK))
    both[:, :BLOCK] = key_value[...]
    both[:, BLOCK:] = jnp.where(low, query[...], total.astype(BF16))
    for quarter in range(Y):
        part = weights[quarter, :, : 3 * HEAD_DIM].T
        turned[:, quarter * 256 : (quarter + 1) * 256] = part


def attention(pair, listed, usable):
    scale = HEAD_DIM ** (-0.5)
    low = low_lanes((BLOCK, BLOCK))
    zero = jnp.zeros((BLOCK, BLOCK), BF16)
    stacked = jnp.concatenate(
        [jnp.where(low, pair, zero), jnp.where(low, zero, pair)], axis=0
    )
    inner = matmul(stacked, listed, ((1,), (1,)))
    scores = inner[:BLOCK] * scale
    prob_grad = inner[BLOCK:]
    local_scores = jnp.where(usable, scores[:, :BLOCK], -1e30)
    scores = jnp.concatenate([local_scores, scores[:, BLOCK:]], axis=1)
    exponent = jnp.exp(scores - jnp.max(scores, axis=1, keepdims=True))
    total = jnp.sum(exponent, axis=1, keepdims=True)
    probs = exponent * (1.0 / total)
    mean = jnp.sum(probs * prob_grad, axis=1, keepdims=True)
    score_grad = (probs * (prob_grad - mean) * scale).astype(BF16)
    return stacked, score_grad, probs.astype(BF16)


def matched(block, wrap):
    return [lax.rem(block - r - wrap + 2 * Y, Y) for r in range(ROUNDS)]


def own_rows(flags, mine, arrived, local, grad_query):
    low = low_lanes((BLOCK, BLOCK))
    for block in range(Y):
        listed = [mine[block, :, :BLOCK]] + [arrived[s] for s in matched(block, flags[0])]
        listed = jnp.concatenate(listed, axis=0)
        stacked, score_grad, probs = attention(
            mine[block, :, BLOCK:], listed, flags[2 + block] > 0
        )
        query_side = matmul(score_grad, listed, ((1,), (0,)))
        query_side = jnp.where(low, query_side, pltpu.roll(query_side, HEAD_DIM, 1))
        grad_query[block] = query_side.astype(BF16)
        terms = jnp.concatenate([score_grad[:, :BLOCK], probs[:, :BLOCK]], axis=0)
        local[block] = matmul(terms, stacked, ((0,), (0,)))


def gradients(scalars, flags, mine, ahead, local, grad_query, x0, x1, bundle, total, both):
    total[...] = local[...]
    for block in range(Y):
        sources = matched(block, flags[1])
        listed = [ahead[block, :, :BLOCK]] + [mine[s, :, :BLOCK] for s in sources]
        listed = jnp.concatenate(listed, axis=0)
        stacked, score_grad, probs = attention(
            ahead[block, :, BLOCK:], listed, flags[2 + Y + block] > 0
        )
        terms = jnp.concatenate([score_grad[:, BLOCK:], probs[:, BLOCK:]], axis=0)
        side = matmul(terms, stacked, ((0,), (0,)))
        for r in range(ROUNDS):
            part = side[r * BLOCK : (r + 1) * BLOCK].astype(BF16).astype(F32)
            total[sources[r]] += part
    for block in range(Y):
        side = total[block].astype(BF16)
        both[block, :, :BLOCK] = side
        both[block, :, BLOCK:] = grad_query[block]
        turned = side.T
        turned = jnp.concatenate([turned[:HEAD_DIM], turned[HEAD_DIM:]], axis=1)
        for part in range(XL):
            bundle[block, part, BLOCK:] = turned
    right = both[...].reshape(Y * BLOCK, 256)
    terms = lax.broadcasted_iota(jnp.int32, (BLOCK, 256), 1) < 3 * HEAD_DIM
    for half, pair in enumerate((x0, x1)):
        for core in range(CORE):
            product = matmul(pair[core].reshape(Y * BLOCK, 256), right, ((0,), (0,)))
            product = product.astype(BF16)
            quarter = CORE * scalars[half] + core
            for part in range(XL):
                rows = product[part * BLOCK : (part + 1) * BLOCK]
                bundle[quarter, part, :BLOCK] = jnp.where(terms, rows, both[quarter])


def add_terms(bundle, out):
    for source in range(Y):
        near, far = bundle[XL * source, :BLOCK], bundle[XL * source + 1, :BLOCK]
        total = (near.astype(F32) + far.astype(F32)).astype(BF16)
        for place, lower in ((1, 0), (2, HEAD_DIM), (0, 2 * HEAD_DIM)):
            at = place * 256 + source * HEAD_DIM
            out[:, at : at + HEAD_DIM] = total[:, lower : lower + HEAD_DIM]


def input_terms(scalars, bundle, w2, w1, w3, w0, out):
    sides, queries = [], []
    for slot in (2, 1, 3, 0):
        entry = XL * lax.rem(scalars[2] + slot, Y) + scalars[3]
        folded = bundle[entry, BLOCK:]
        sides.append(jnp.concatenate([folded[:, :BLOCK], folded[:, BLOCK:]], axis=0))
        queries.append(bundle[entry, :BLOCK, 3 * HEAD_DIM :])
    for quarter in range(4):
        total = jnp.zeros((BLOCK, 256), F32)
        lower = quarter * 256
        for side, query, weights in zip(sides, queries, (w2, w1, w3, w0)):
            columns = weights[:, lower : lower + 256]
            total += matmul(side, columns[: 2 * HEAD_DIM], ((0,), (0,)))
            total += matmul(query, columns[2 * HEAD_DIM :], ((1,), (0,)))
        out[quarter] = total.astype(BF16)


def sum_terms(terms, out):
    out[...] = jnp.sum(terms[...].astype(F32), axis=0)


def shards(node_features, cotangent, proj_weights, local_mask, matching):
    xl = lax.axis_index("xl")
    z = lax.axis_index("z")
    xh = lax.axis_index("xh")
    core = lax.axis_index("core")
    y = lax.axis_index("y")
    scalars = jnp.stack([xh, 1 - xh, y, xl]).astype(jnp.int32)

    packed, rows = kernel_call(
        pack,
        [((2 * BLOCK, 256), BF16), ((Z, Y, 8, 256), BF16)],
        [HBM] * 3,
        1000,
        600000,
        (node_features, cotangent, proj_weights),
        (pltpu.VMEM((8, 4, 256), BF16), pltpu.SemaphoreType.DMA((3,))),
        60,
    )
    near = lax.all_to_all(rows, "z", 0, 0, tiled=True)
    p0 = lax.all_gather(packed, "y", axis=0)
    p1 = swapped(p0, "xh")
    (rows,) = kernel_call(
        spread, [((Y, XL, BLOCK, 256), BF16)], [VMEM], 1000, 800000, (near,)
    )
    weights = lax.all_to_all(
        rows.reshape(Y * XL, BLOCK, 256), ("y", "xl"), 0, 0, tiled=True
    ).reshape(4, 256, 256)
    x0 = lax.all_gather(p0[:, :BLOCK], "core", axis=0)
    c0 = lax.all_gather(p0[:, BLOCK:], "core", axis=0)
    x1 = lax.all_gather(p1[:, :BLOCK], "core", axis=0)

    key_value, query = kernel_call(
        project_features,
        [((512, BLOCK), BF16), ((512, BLOCK), BF16)],
        [SMEM] + [VMEM] * 3,
        2 * 512 * 1024 * 256,
        2000000,
        (scalars, x0, x1, weights),
    )
    arrived = shifted(key_value, 1)
    p1, query = lax.optimization_barrier((p1, query))
    c1 = lax.all_gather(p1[:, BLOCK:], "core", axis=0)
    both, turned = kernel_call(
        project_cotangents,
        [((512, 256), BF16), ((192, 1024), BF16)],
        [SMEM] + [VMEM] * 5,
        2 * 512 * 1024 * 128,
        3500000,
        (scalars, c0, c1, weights, key_value, query),
    )
    ahead = shifted(both, -1)
    group_weights = [
        lax.ppermute(turned, "y", [(i, (i - k) % Y) for i in range(Y)]) for k in (2, 1, 3)
    ]
    group_weights.append(turned)

    mask = lax.all_gather(local_mask, "y", axis=0).reshape(Y, 1)
    usable = (mask > 0) | jnp.eye(1, dtype=bool)
    next_usable = (shifted(mask, -1) > 0) | jnp.eye(1, dtype=bool)
    at = xl * Z + z
    wraps = jnp.stack([at == 0, at == RING_SIZE - 1])
    flags = jnp.concatenate([wraps, usable.reshape(Y), next_usable.reshape(Y)])
    flags = flags.astype(jnp.int32)
    both = both.reshape(Y, BLOCK, 256)
    local, grad_query = kernel_call(
        own_rows,
        [((Y, BLOCK, BLOCK), F32), ((Y, BLOCK, BLOCK), BF16)],
        [SMEM] + [VMEM] * 2,
        3 * 1000 * 1000 * 1000,
        1000000,
        (flags, both, arrived.reshape(Y, BLOCK, BLOCK)),
    )
    (bundle,) = kernel_call(
        gradients,
        [((Y, XL, 192, 256), BF16)],
        [SMEM] * 2 + [VMEM] * 6,
        4 * 1000 * 1000 * 1000,
        3000000,
        (scalars, flags, both, ahead.reshape(Y, BLOCK, 256), local, grad_query, x0, x1),
        (pltpu.VMEM((Y, BLOCK, BLOCK), F32), pltpu.VMEM((Y, BLOCK, 256), BF16)),
    )
    bundle = lax.all_to_all(
        bundle.reshape(Y * XL, 192, 256), ("y", "xl"), 0, 0, tiled=True
    )
    (term,) = kernel_call(
        add_terms, [((BLOCK, 768), BF16)], [VMEM], 1000000, 800000, (bundle,)
    )
    term, bundle = lax.optimization_barrier((term, bundle))
    term = lax.all_to_all(term.reshape(Z, 8, 768), "z", 0, 0, tiled=True)
    (partial,) = kernel_call(
        input_terms,
        [((4, BLOCK, 256), BF16)],
        [SMEM] + [VMEM] * 5,
        2 * 128 * 1024 * 1024,
        2500000,
        (scalars, bundle, *group_weights),
    )
    partial = lax.all_gather(partial, "core", axis=0).reshape(CORE, XH, CORE, BLOCK, 256)
    partial = lax.dynamic_index_in_dim(partial, core, 2, keepdims=False)
    pair = jnp.sum(partial.astype(F32), axis=0)
    remote = lax.dynamic_index_in_dim(pair, 1 - xh, 0, keepdims=False)
    remote = lax.all_gather(remote, "xh", axis=0)
    remote = lax.dynamic_index_in_dim(remote, 1 - xh, 0, keepdims=False)
    pair = lax.dynamic_index_in_dim(pair, xh, 0, keepdims=False)
    input_grad = (pair + remote).astype(BF16)

    (weight_grads,) = kernel_call(
        sum_terms, [((8, 768), F32)], [VMEM], 1000000, 300000, (term,)
    )
    return (input_grad, weight_grads.reshape(8, 3, 256))


def solution(mesh):
    fine = Mesh(mesh.devices.reshape(Y, XL, Z, XH, CORE), AXES)
    head = ("xh", "core")
    return jax.shard_map(
        shards,
        mesh=fine,
        in_specs=(
            P(DOM, head),
            P(DOM, head),
            P(DOM, None, head),
            P(DOM, None),
            P(None, DOM),
        ),
        out_specs=(P(DOM, head), P(DOM, None, head)),
        check_vma=False,
    )
```

```python
import jax
import jax.numpy as jnp
from jax import lax
from jax.experimental import pallas as pl
from jax.experimental.pallas import tpu as pltpu
from jax.sharding import Mesh
from jax.sharding import PartitionSpec as P

HEAD_DIM = 64
BLOCK = 128
ROUNDS = 3
Y, XL, Z, XH, CORE = 4, 2, 16, 2, 2
AXES = ("y", "xl", "z", "xh", "core")
DOM = ("y", "xl", "z")
RING = ("xl", "z")
RING_SIZE = XL * Z
F32 = jnp.float32
BF16 = jnp.bfloat16
SMEM = pl.BlockSpec(memory_space=pltpu.SMEM)
VMEM = pl.BlockSpec(memory_space=pltpu.VMEM)
HBM = pl.BlockSpec(memory_space=pltpu.HBM)


def swapped(block, axis):
    return lax.ppermute(block, axis, [(0, 1), (1, 0)])


def shifted(block, distance):
    route = [(i, (i + distance) % RING_SIZE) for i in range(RING_SIZE)]
    return lax.ppermute(block, RING, route)


def matmul(left, right, dims):
    return lax.dot_general(left, right, (dims, ((), ())), preferred_element_type=F32)


def low_lanes(shape):
    return lax.broadcasted_iota(jnp.int32, shape, len(shape) - 1) < HEAD_DIM


def kernel_call(kernel, shapes, specs, flops, size, args, scratch=(), limit=16):
    return pl.pallas_call(
        kernel,
        out_shape=[jax.ShapeDtypeStruct(shape, dtype) for shape, dtype in shapes],
        in_specs=specs,
        out_specs=[VMEM] * len(shapes),
        scratch_shapes=list(scratch),
        compiler_params=pltpu.CompilerParams(vmem_limit_bytes=limit * 1024 * 1024),
        cost_estimate=pl.CostEstimate(flops=flops, bytes_accessed=size, transcendentals=0),
    )(*args)


def pack(features, cotangents, weights, packed, rows, held, arrivals):
    copies = [
        pltpu.make_async_copy(weights, held, arrivals.at[0]),
        pltpu.make_async_copy(features, packed.at[pl.ds(0, BLOCK)], arrivals.at[1]),
        pltpu.make_async_copy(cotangents, packed.at[pl.ds(BLOCK, BLOCK)], arrivals.at[2]),
    ]
    for copy in copies:
        copy.start()
    copies[0].wait()
    for quarter in range(Y):
        lower = quarter * HEAD_DIM
        part = jnp.concatenate(
            [held[:, t, lower : lower + HEAD_DIM] for t in (1, 2, 0, 3)], axis=1
        )
        rows[:, quarter] = jnp.broadcast_to(part[None], (Z, 8, 256))
    copies[1].wait()
    copies[2].wait()


def spread(gathered, rows):
    for quarter in range(Y):
        part = gathered[:, quarter].reshape(BLOCK, 256)
        rows[quarter, 0] = part
        rows[quarter, 1] = part


def project_features(scalars, x0, x1, weights, key_value, query):
    total = jnp.zeros((Y * BLOCK, 256), F32)
    for half, pair in enumerate((x0, x1)):
        for core in range(CORE):
            rows = weights[CORE * scalars[half] + core]
            total += matmul(pair[core].reshape(Y * BLOCK, 256), rows, ((1,), (0,)))
    key_value[...] = total[:, :BLOCK].astype(BF16)
    query[...] = total[:, BLOCK:].astype(BF16)


def project_cotangents(scalars, c0, c1, weights, key_value, query, both, turned):
    total = jnp.zeros((Y * BLOCK, BLOCK), F32)
    for half, pair in enumerate((c0, c1)):
        for core in range(CORE):
            rows = weights[CORE * scalars[half] + core, :, BLOCK:]
            total += matmul(pair[core].reshape(Y * BLOCK, 256), rows, ((1,), (0,)))
    low = low_lanes((Y * BLOCK, BLOCK))
    both[:, :BLOCK] = key_value[...]
    both[:, BLOCK:] = jnp.where(low, query[...], total.astype(BF16))
    for quarter in range(Y):
        part = weights[quarter, :, : 3 * HEAD_DIM].T
        turned[:, quarter * 256 : (quarter + 1) * 256] = part


def attention(pair, listed, usable):
    scale = HEAD_DIM ** (-0.5)
    low = low_lanes((BLOCK, BLOCK))
    zero = jnp.zeros((BLOCK, BLOCK), BF16)
    stacked = jnp.concatenate(
        [jnp.where(low, pair, zero), jnp.where(low, zero, pair)], axis=0
    )
    inner = matmul(stacked, listed, ((1,), (1,)))
    scores = inner[:BLOCK] * scale
    prob_grad = inner[BLOCK:]
    local_scores = jnp.where(usable, scores[:, :BLOCK], -1e30)
    scores = jnp.concatenate([local_scores, scores[:, BLOCK:]], axis=1)
    exponent = jnp.exp(scores - jnp.max(scores, axis=1, keepdims=True))
    total = jnp.sum(exponent, axis=1, keepdims=True)
    probs = exponent * (1.0 / total)
    mean = jnp.sum(probs * prob_grad, axis=1, keepdims=True)
    score_grad = (probs * (prob_grad - mean) * scale).astype(BF16)
    return stacked, score_grad, probs.astype(BF16)


def matched(block, wrap):
    return [lax.rem(block - r - wrap + 2 * Y, Y) for r in range(ROUNDS)]


def own_rows(flags, mine, arrived, local, grad_query):
    low = low_lanes((BLOCK, BLOCK))
    for block in range(Y):
        listed = [mine[block, :, :BLOCK]] + [arrived[s] for s in matched(block, flags[0])]
        listed = jnp.concatenate(listed, axis=0)
        stacked, score_grad, probs = attention(
            mine[block, :, BLOCK:], listed, flags[2 + block] > 0
        )
        query_side = matmul(score_grad, listed, ((1,), (0,)))
        query_side = jnp.where(low, query_side, pltpu.roll(query_side, HEAD_DIM, 1))
        grad_query[block] = query_side.astype(BF16)
        terms = jnp.concatenate([score_grad[:, :BLOCK], probs[:, :BLOCK]], axis=0)
        local[block] = matmul(terms, stacked, ((0,), (0,)))


def gradients(scalars, flags, mine, ahead, local, grad_query, x0, x1, bundle, total, both):
    total[...] = local[...]
    for block in range(Y):
        sources = matched(block, flags[1])
        listed = [ahead[block, :, :BLOCK]] + [mine[s, :, :BLOCK] for s in sources]
        listed = jnp.concatenate(listed, axis=0)
        stacked, score_grad, probs = attention(
            ahead[block, :, BLOCK:], listed, flags[2 + Y + block] > 0
        )
        terms = jnp.concatenate([score_grad[:, BLOCK:], probs[:, BLOCK:]], axis=0)
        side = matmul(terms, stacked, ((0,), (0,)))
        for r in range(ROUNDS):
            part = side[r * BLOCK : (r + 1) * BLOCK].astype(BF16).astype(F32)
            total[sources[r]] += part
    for block in range(Y):
        side = total[block].astype(BF16)
        both[block, :, :BLOCK] = side
        both[block, :, BLOCK:] = grad_query[block]
        turned = side.T
        turned = jnp.concatenate([turned[:HEAD_DIM], turned[HEAD_DIM:]], axis=1)
        for part in range(XL):
            bundle[block, part, BLOCK:] = turned
    right = both[...].reshape(Y * BLOCK, 256)
    terms = lax.broadcasted_iota(jnp.int32, (BLOCK, 256), 1) < 3 * HEAD_DIM
    for half, pair in enumerate((x0, x1)):
        for core in range(CORE):
            product = matmul(pair[core].reshape(Y * BLOCK, 256), right, ((0,), (0,)))
            product = product.astype(BF16)
            quarter = CORE * scalars[half] + core
            for part in range(XL):
                rows = product[part * BLOCK : (part + 1) * BLOCK]
                bundle[quarter, part, :BLOCK] = jnp.where(terms, rows, both[quarter])


def add_terms(bundle, out):
    for source in range(Y):
        near, far = bundle[XL * source, :BLOCK], bundle[XL * source + 1, :BLOCK]
        total = (near.astype(F32) + far.astype(F32)).astype(BF16)
        for place, lower in ((1, 0), (2, HEAD_DIM), (0, 2 * HEAD_DIM)):
            at = place * 256 + source * HEAD_DIM
            out[:, at : at + HEAD_DIM] = total[:, lower : lower + HEAD_DIM]


def input_terms(scalars, bundle, w2, w1, w3, w0, out):
    sides, queries = [], []
    for slot in (2, 1, 3, 0):
        entry = XL * lax.rem(scalars[2] + slot, Y) + scalars[3]
        folded = bundle[entry, BLOCK:]
        sides.append(jnp.concatenate([folded[:, :BLOCK], folded[:, BLOCK:]], axis=0))
        queries.append(bundle[entry, :BLOCK, 3 * HEAD_DIM :])
    for quarter in range(4):
        total = jnp.zeros((BLOCK, 256), F32)
        lower = quarter * 256
        for side, query, weights in zip(sides, queries, (w2, w1, w3, w0)):
            columns = weights[:, lower : lower + 256]
            total += matmul(side, columns[: 2 * HEAD_DIM], ((0,), (0,)))
            total += matmul(query, columns[2 * HEAD_DIM :], ((1,), (0,)))
        out[quarter] = total.astype(BF16)


def sum_terms(terms, out):
    out[...] = jnp.sum(terms[...].astype(F32), axis=0)


def shards(node_features, cotangent, proj_weights, local_mask, matching):
    xl = lax.axis_index("xl")
    z = lax.axis_index("z")
    xh = lax.axis_index("xh")
    core = lax.axis_index("core")
    y = lax.axis_index("y")
    scalars = jnp.stack([xh, 1 - xh, y, xl]).astype(jnp.int32)

    packed, rows = kernel_call(
        pack,
        [((2 * BLOCK, 256), BF16), ((Z, Y, 8, 256), BF16)],
        [HBM] * 3,
        1000,
        600000,
        (node_features, cotangent, proj_weights),
        (pltpu.VMEM((8, 4, 256), BF16), pltpu.SemaphoreType.DMA((3,))),
        60,
    )
    near = lax.all_to_all(rows, "z", 0, 0, tiled=True)
    p0 = lax.all_gather(packed, "y", axis=0)
    p1 = swapped(p0, "xh")
    (rows,) = kernel_call(
        spread, [((Y, XL, BLOCK, 256), BF16)], [VMEM], 1000, 800000, (near,)
    )
    weights = lax.all_to_all(
        rows.reshape(Y * XL, BLOCK, 256), ("y", "xl"), 0, 0, tiled=True
    ).reshape(4, 256, 256)
    x0 = lax.all_gather(p0[:, :BLOCK], "core", axis=0)
    c0 = lax.all_gather(p0[:, BLOCK:], "core", axis=0)
    x1 = lax.all_gather(p1[:, :BLOCK], "core", axis=0)

    key_value, query = kernel_call(
        project_features,
        [((512, BLOCK), BF16), ((512, BLOCK), BF16)],
        [SMEM] + [VMEM] * 3,
        2 * 512 * 1024 * 256,
        2000000,
        (scalars, x0, x1, weights),
    )
    arrived = shifted(key_value, 1)
    p1, query = lax.optimization_barrier((p1, query))
    c1 = lax.all_gather(p1[:, BLOCK:], "core", axis=0)
    both, turned = kernel_call(
        project_cotangents,
        [((512, 256), BF16), ((192, 1024), BF16)],
        [SMEM] + [VMEM] * 5,
        2 * 512 * 1024 * 128,
        3500000,
        (scalars, c0, c1, weights, key_value, query),
    )
    ahead = shifted(both, -1)
    group_weights = [
        lax.ppermute(turned, "y", [(i, (i - k) % Y) for i in range(Y)]) for k in (2, 1, 3)
    ]
    group_weights.append(turned)

    mask = lax.all_gather(local_mask, "y", axis=0).reshape(Y, 1)
    usable = (mask > 0) | jnp.eye(1, dtype=bool)
    next_usable = (shifted(mask, -1) > 0) | jnp.eye(1, dtype=bool)
    at = xl * Z + z
    wraps = jnp.stack([at == 0, at == RING_SIZE - 1])
    flags = jnp.concatenate([wraps, usable.reshape(Y), next_usable.reshape(Y)])
    flags = flags.astype(jnp.int32)
    both = both.reshape(Y, BLOCK, 256)
    local, grad_query = kernel_call(
        own_rows,
        [((Y, BLOCK, BLOCK), F32), ((Y, BLOCK, BLOCK), BF16)],
        [SMEM] + [VMEM] * 2,
        3 * 1000 * 1000 * 1000,
        1000000,
        (flags, both, arrived.reshape(Y, BLOCK, BLOCK)),
    )
    (bundle,) = kernel_call(
        gradients,
        [((Y, XL, 192, 256), BF16)],
        [SMEM] * 2 + [VMEM] * 6,
        1 * 1000 * 1000 * 1000,
        3000000,
        (scalars, flags, both, ahead.reshape(Y, BLOCK, 256), local, grad_query, x0, x1),
        (pltpu.VMEM((Y, BLOCK, BLOCK), F32), pltpu.VMEM((Y, BLOCK, 256), BF16)),
    )
    bundle, group_weights[0] = lax.optimization_barrier((bundle, group_weights[0]))
    bundle = lax.all_to_all(
        bundle.reshape(Y * XL, 192, 256), ("y", "xl"), 0, 0, tiled=True
    )
    (term,) = kernel_call(
        add_terms, [((BLOCK, 768), BF16)], [VMEM], 1000000, 800000, (bundle,)
    )
    term, bundle = lax.optimization_barrier((term, bundle))
    term = lax.all_to_all(term.reshape(Z, 8, 768), "z", 0, 0, tiled=True)
    (partial,) = kernel_call(
        input_terms,
        [((4, BLOCK, 256), BF16)],
        [SMEM] + [VMEM] * 5,
        2 * 128 * 1024 * 1024,
        2500000,
        (scalars, bundle, *group_weights),
    )
    partial = lax.all_gather(partial, "core", axis=0).reshape(CORE, XH, CORE, BLOCK, 256)
    partial = lax.dynamic_index_in_dim(partial, core, 2, keepdims=False)
    pair = jnp.sum(partial.astype(F32), axis=0)
    remote = lax.dynamic_index_in_dim(pair, 1 - xh, 0, keepdims=False)
    remote = lax.all_gather(remote, "xh", axis=0)
    remote = lax.dynamic_index_in_dim(remote, 1 - xh, 0, keepdims=False)
    pair = lax.dynamic_index_in_dim(pair, xh, 0, keepdims=False)
    input_grad = (pair + remote).astype(BF16)

    (weight_grads,) = kernel_call(
        sum_terms, [((8, 768), F32)], [VMEM], 1000000, 300000, (term,)
    )
    return (input_grad, weight_grads.reshape(8, 3, 256))


def solution(mesh):
    fine = Mesh(mesh.devices.reshape(Y, XL, Z, XH, CORE), AXES)
    head = ("xh", "core")
    return jax.shard_map(
        shards,
        mesh=fine,
        in_specs=(
            P(DOM, head),
            P(DOM, head),
            P(DOM, None, head),
            P(DOM, None),
            P(None, DOM),
        ),
        out_specs=(P(DOM, head), P(DOM, None, head)),
        check_vma=False,
    )
```

```python
import jax
import jax.numpy as jnp
from jax import lax
from jax.experimental import pallas as pl
from jax.experimental.pallas import tpu as pltpu
from jax.sharding import Mesh
from jax.sharding import PartitionSpec as P

HEAD_DIM = 64
BLOCK = 128
ROUNDS = 3
Y, XL, Z, XH, CORE = 4, 2, 16, 2, 2
AXES = ("y", "xl", "z", "xh", "core")
DOM = ("y", "xl", "z")
RING = ("xl", "z")
RING_SIZE = XL * Z
F32 = jnp.float32
BF16 = jnp.bfloat16
SMEM = pl.BlockSpec(memory_space=pltpu.SMEM)
VMEM = pl.BlockSpec(memory_space=pltpu.VMEM)
HBM = pl.BlockSpec(memory_space=pltpu.HBM)


def swapped(block, axis):
    return lax.ppermute(block, axis, [(0, 1), (1, 0)])


def shifted(block, distance):
    route = [(i, (i + distance) % RING_SIZE) for i in range(RING_SIZE)]
    return lax.ppermute(block, RING, route)


def matmul(left, right, dims):
    return lax.dot_general(left, right, (dims, ((), ())), preferred_element_type=F32)


def low_lanes(shape):
    return lax.broadcasted_iota(jnp.int32, shape, len(shape) - 1) < HEAD_DIM


def kernel_call(kernel, shapes, specs, flops, size, args, scratch=(), limit=16):
    return pl.pallas_call(
        kernel,
        out_shape=[jax.ShapeDtypeStruct(shape, dtype) for shape, dtype in shapes],
        in_specs=specs,
        out_specs=[VMEM] * len(shapes),
        scratch_shapes=list(scratch),
        compiler_params=pltpu.CompilerParams(vmem_limit_bytes=limit * 1024 * 1024),
        cost_estimate=pl.CostEstimate(flops=flops, bytes_accessed=size, transcendentals=0),
    )(*args)


def pack(features, cotangents, weights, packed, rows, held, arrivals):
    copies = [
        pltpu.make_async_copy(weights, held, arrivals.at[0]),
        pltpu.make_async_copy(features, packed.at[pl.ds(0, BLOCK)], arrivals.at[1]),
        pltpu.make_async_copy(cotangents, packed.at[pl.ds(BLOCK, BLOCK)], arrivals.at[2]),
    ]
    for copy in copies:
        copy.start()
    copies[0].wait()
    for quarter in range(Y):
        lower = quarter * HEAD_DIM
        part = jnp.concatenate(
            [held[:, t, lower : lower + HEAD_DIM] for t in (1, 2, 0, 3)], axis=1
        )
        rows[:, quarter] = jnp.broadcast_to(part[None], (Z, 8, 256))
    copies[1].wait()
    copies[2].wait()


def spread(gathered, rows):
    for quarter in range(Y):
        part = gathered[:, quarter].reshape(BLOCK, 256)
        rows[quarter, 0] = part
        rows[quarter, 1] = part


def project_features(scalars, x0, x1, weights, key_value, query):
    total = jnp.zeros((Y * BLOCK, 256), F32)
    for half, pair in enumerate((x0, x1)):
        for core in range(CORE):
            rows = weights[CORE * scalars[half] + core]
            total += matmul(pair[core].reshape(Y * BLOCK, 256), rows, ((1,), (0,)))
    key_value[...] = total[:, :BLOCK].astype(BF16)
    query[...] = total[:, BLOCK:].astype(BF16)


def project_cotangents(scalars, c0, c1, weights, key_value, query, both, turned):
    total = jnp.zeros((Y * BLOCK, BLOCK), F32)
    for half, pair in enumerate((c0, c1)):
        for core in range(CORE):
            rows = weights[CORE * scalars[half] + core, :, BLOCK:]
            total += matmul(pair[core].reshape(Y * BLOCK, 256), rows, ((1,), (0,)))
    low = low_lanes((Y * BLOCK, BLOCK))
    both[:, :BLOCK] = key_value[...]
    both[:, BLOCK:] = jnp.where(low, query[...], total.astype(BF16))
    for quarter in range(Y):
        part = weights[quarter, :, : 3 * HEAD_DIM].T
        turned[:, quarter * 256 : (quarter + 1) * 256] = part


def attention(pair, listed, usable):
    scale = HEAD_DIM ** (-0.5)
    low = low_lanes((BLOCK, BLOCK))
    zero = jnp.zeros((BLOCK, BLOCK), BF16)
    stacked = jnp.concatenate(
        [jnp.where(low, pair, zero), jnp.where(low, zero, pair)], axis=0
    )
    inner = matmul(listed, stacked, ((1,), (1,)))
    scores = inner[:, :BLOCK] * scale
    prob_grad = inner[:, BLOCK:]
    local_scores = jnp.where(usable, scores[:BLOCK], -1e30)
    scores = jnp.concatenate([local_scores, scores[BLOCK:]], axis=0)
    exponent = jnp.exp(scores - jnp.max(scores, axis=0, keepdims=True))
    total = jnp.sum(exponent, axis=0, keepdims=True)
    probs = exponent * (1.0 / total)
    mean = jnp.sum(probs * prob_grad, axis=0, keepdims=True)
    score_grad = (probs * (prob_grad - mean) * scale).astype(BF16)
    return stacked, jnp.concatenate([score_grad, probs.astype(BF16)], axis=1)


def matched(block, wrap):
    return [lax.rem(block - r - wrap + 2 * Y, Y) for r in range(ROUNDS)]


def gradients(scalars, flags, mine, ahead, arrived, x0, x1, bundle, total, both):
    low = low_lanes((BLOCK, BLOCK))
    for block in range(Y):
        listed = [mine[block, :, :BLOCK]] + [arrived[s] for s in matched(block, flags[0])]
        listed = jnp.concatenate(listed, axis=0)
        stacked, terms = attention(
            mine[block, :, BLOCK:], listed, flags[2 + block] > 0
        )
        query_side = matmul(terms[:, :BLOCK], listed, ((0,), (0,)))
        query_side = jnp.where(low, query_side, pltpu.roll(query_side, HEAD_DIM, 1))
        both[block, :, BLOCK:] = query_side.astype(BF16)
        total[block] = matmul(terms[:BLOCK], stacked, ((1,), (0,)))
    for block in range(Y):
        sources = matched(block, flags[1])
        listed = [ahead[block, :, :BLOCK]] + [mine[s, :, :BLOCK] for s in sources]
        listed = jnp.concatenate(listed, axis=0)
        stacked, terms = attention(
            ahead[block, :, BLOCK:], listed, flags[2 + Y + block] > 0
        )
        side = matmul(terms[BLOCK:], stacked, ((1,), (0,)))
        for r in range(ROUNDS):
            part = side[r * BLOCK : (r + 1) * BLOCK].astype(BF16).astype(F32)
            total[sources[r]] += part
    for block in range(Y):
        side = total[block].astype(BF16)
        both[block, :, :BLOCK] = side
        turned = side.T
        turned = jnp.concatenate([turned[:HEAD_DIM], turned[HEAD_DIM:]], axis=1)
        for part in range(XL):
            bundle[block, part, BLOCK:] = turned
    right = both[...].reshape(Y * BLOCK, 256)
    terms = lax.broadcasted_iota(jnp.int32, (BLOCK, 256), 1) < 3 * HEAD_DIM
    for half, pair in enumerate((x0, x1)):
        for core in range(CORE):
            product = matmul(pair[core].reshape(Y * BLOCK, 256), right, ((0,), (0,)))
            product = product.astype(BF16)
            quarter = CORE * scalars[half] + core
            for part in range(XL):
                rows = product[part * BLOCK : (part + 1) * BLOCK]
                bundle[quarter, part, :BLOCK] = jnp.where(terms, rows, both[quarter])


def add_terms(bundle, out):
    for source in range(Y):
        near, far = bundle[XL * source, :BLOCK], bundle[XL * source + 1, :BLOCK]
        total = (near.astype(F32) + far.astype(F32)).astype(BF16)
        for place, lower in ((1, 0), (2, HEAD_DIM), (0, 2 * HEAD_DIM)):
            at = place * 256 + source * HEAD_DIM
            out[:, at : at + HEAD_DIM] = total[:, lower : lower + HEAD_DIM]


def input_terms(scalars, bundle, w0, w1, w2, w3, out):
    sides, queries = [], []
    for slot in range(Y):
        entry = XL * lax.rem(scalars[2] + slot, Y) + scalars[3]
        folded = bundle[entry, BLOCK:]
        sides.append(jnp.concatenate([folded[:, :BLOCK], folded[:, BLOCK:]], axis=0))
        queries.append(bundle[entry, :BLOCK, 3 * HEAD_DIM :])
    for quarter in range(4):
        total = jnp.zeros((BLOCK, 256), F32)
        lower = quarter * 256
        for side, query, weights in zip(sides, queries, (w0, w1, w2, w3)):
            columns = weights[:, lower : lower + 256]
            total += matmul(side, columns[: 2 * HEAD_DIM], ((0,), (0,)))
            total += matmul(query, columns[2 * HEAD_DIM :], ((1,), (0,)))
        out[quarter] = total.astype(BF16)


def sum_terms(terms, out):
    out[...] = jnp.sum(terms[...].astype(F32), axis=0)


def shards(node_features, cotangent, proj_weights, local_mask, matching):
    xl = lax.axis_index("xl")
    z = lax.axis_index("z")
    xh = lax.axis_index("xh")
    core = lax.axis_index("core")
    y = lax.axis_index("y")
    scalars = jnp.stack([xh, 1 - xh, y, xl]).astype(jnp.int32)

    packed, rows = kernel_call(
        pack,
        [((2 * BLOCK, 256), BF16), ((Z, Y, 8, 256), BF16)],
        [HBM] * 3,
        1000,
        600000,
        (node_features, cotangent, proj_weights),
        (pltpu.VMEM((8, 4, 256), BF16), pltpu.SemaphoreType.DMA((3,))),
        60,
    )
    near = lax.all_to_all(rows, "z", 0, 0, tiled=True)
    p0 = lax.all_gather(packed, "y", axis=0)
    p1 = swapped(p0, "xh")
    (rows,) = kernel_call(
        spread, [((Y, XL, BLOCK, 256), BF16)], [VMEM], 1000, 800000, (near,)
    )
    weights = lax.all_to_all(
        rows.reshape(Y * XL, BLOCK, 256), ("y", "xl"), 0, 0, tiled=True
    ).reshape(4, 256, 256)
    x0 = lax.all_gather(p0[:, :BLOCK], "core", axis=0)
    c0 = lax.all_gather(p0[:, BLOCK:], "core", axis=0)
    x1 = lax.all_gather(p1[:, :BLOCK], "core", axis=0)

    key_value, query = kernel_call(
        project_features,
        [((512, BLOCK), BF16), ((512, BLOCK), BF16)],
        [SMEM] + [VMEM] * 3,
        2 * 512 * 1024 * 256,
        2000000,
        (scalars, x0, x1, weights),
    )
    arrived = shifted(key_value, 1)
    p1, query = lax.optimization_barrier((p1, query))
    c1 = lax.all_gather(p1[:, BLOCK:], "core", axis=0)
    both, turned = kernel_call(
        project_cotangents,
        [((512, 256), BF16), ((192, 1024), BF16)],
        [SMEM] + [VMEM] * 5,
        2 * 512 * 1024 * 128,
        3500000,
        (scalars, c0, c1, weights, key_value, query),
    )
    ahead = shifted(both, -1)
    group_weights = [turned] + [
        lax.ppermute(turned, "y", [(i, (i - k) % Y) for i in range(Y)]) for k in range(1, Y)
    ]

    mask = lax.all_gather(local_mask, "y", axis=0).reshape(Y, 1)
    usable = (mask > 0) | jnp.eye(1, dtype=bool)
    next_usable = (shifted(mask, -1) > 0) | jnp.eye(1, dtype=bool)
    at = xl * Z + z
    wraps = jnp.stack([at == 0, at == RING_SIZE - 1])
    flags = jnp.concatenate([wraps, usable.reshape(Y), next_usable.reshape(Y)])
    (bundle,) = kernel_call(
        gradients,
        [((Y, XL, 192, 256), BF16)],
        [SMEM] * 2 + [VMEM] * 5,
        7 * 1000 * 1000 * 1000,
        3000000,
        (
            scalars,
            flags.astype(jnp.int32),
            both.reshape(Y, BLOCK, 256),
            ahead.reshape(Y, BLOCK, 256),
            arrived.reshape(Y, BLOCK, BLOCK),
            x0,
            x1,
        ),
        (pltpu.VMEM((Y, BLOCK, BLOCK), F32), pltpu.VMEM((Y, BLOCK, 256), BF16)),
    )
    bundle, group_weights[2] = lax.optimization_barrier((bundle, group_weights[2]))
    bundle = lax.all_to_all(
        bundle.reshape(Y * XL, 192, 256), ("y", "xl"), 0, 0, tiled=True
    )
    (term,) = kernel_call(
        add_terms, [((BLOCK, 768), BF16)], [VMEM], 1000000, 800000, (bundle,)
    )
    term, bundle = lax.optimization_barrier((term, bundle))
    term = lax.all_to_all(term.reshape(Z, 8, 768), "z", 0, 0, tiled=True)
    (partial,) = kernel_call(
        input_terms,
        [((4, BLOCK, 256), BF16)],
        [SMEM] + [VMEM] * 5,
        2 * 128 * 1024 * 1024,
        2500000,
        (scalars, bundle, *group_weights),
    )
    partial = lax.all_gather(partial, "core", axis=0).reshape(CORE, XH, CORE, BLOCK, 256)
    partial = lax.dynamic_index_in_dim(partial, core, 2, keepdims=False)
    pair = jnp.sum(partial.astype(F32), axis=0)
    remote = lax.dynamic_index_in_dim(pair, 1 - xh, 0, keepdims=False)
    remote = lax.all_gather(remote, "xh", axis=0)
    remote = lax.dynamic_index_in_dim(remote, 1 - xh, 0, keepdims=False)
    pair = lax.dynamic_index_in_dim(pair, xh, 0, keepdims=False)
    input_grad = (pair + remote).astype(BF16)

    (weight_grads,) = kernel_call(
        sum_terms, [((8, 768), F32)], [VMEM], 1000000, 300000, (term,)
    )
    return (input_grad, weight_grads.reshape(8, 3, 256))


def solution(mesh):
    fine = Mesh(mesh.devices.reshape(Y, XL, Z, XH, CORE), AXES)
    head = ("xh", "core")
    return jax.shard_map(
        shards,
        mesh=fine,
        in_specs=(
            P(DOM, head),
            P(DOM, head),
            P(DOM, None, head),
            P(DOM, None),
            P(None, DOM),
        ),
        out_specs=(P(DOM, head), P(DOM, None, head)),
        check_vma=False,
    )
```

```python
import jax
import jax.numpy as jnp
from jax import lax
from jax.experimental import pallas as pl
from jax.experimental.pallas import tpu as pltpu
from jax.sharding import Mesh
from jax.sharding import PartitionSpec as P

HEAD_DIM = 64
BLOCK = 128
ROUNDS = 3
Y, XL, Z, XH, CORE = 4, 2, 16, 2, 2
AXES = ("y", "xl", "z", "xh", "core")
DOM = ("y", "xl", "z")
RING = ("xl", "z")
RING_SIZE = XL * Z
F32 = jnp.float32
BF16 = jnp.bfloat16
SMEM = pl.BlockSpec(memory_space=pltpu.SMEM)
VMEM = pl.BlockSpec(memory_space=pltpu.VMEM)
HBM = pl.BlockSpec(memory_space=pltpu.HBM)


def swapped(block, axis):
    return lax.ppermute(block, axis, [(0, 1), (1, 0)])


def shifted(block, distance):
    route = [(i, (i + distance) % RING_SIZE) for i in range(RING_SIZE)]
    return lax.ppermute(block, RING, route)


def matmul(left, right, dims):
    return lax.dot_general(left, right, (dims, ((), ())), preferred_element_type=F32)


def low_lanes(shape):
    return lax.broadcasted_iota(jnp.int32, shape, len(shape) - 1) < HEAD_DIM


def kernel_call(kernel, shapes, specs, flops, size, args, scratch=(), limit=16):
    return pl.pallas_call(
        kernel,
        out_shape=[jax.ShapeDtypeStruct(shape, dtype) for shape, dtype in shapes],
        in_specs=specs,
        out_specs=[VMEM] * len(shapes),
        scratch_shapes=list(scratch),
        compiler_params=pltpu.CompilerParams(vmem_limit_bytes=limit * 1024 * 1024),
        cost_estimate=pl.CostEstimate(flops=flops, bytes_accessed=size, transcendentals=0),
    )(*args)


def pack(features, cotangents, weights, packed, rows, held, arrivals):
    copies = [
        pltpu.make_async_copy(weights, held, arrivals.at[0]),
        pltpu.make_async_copy(features, packed.at[pl.ds(0, BLOCK)], arrivals.at[1]),
        pltpu.make_async_copy(cotangents, packed.at[pl.ds(BLOCK, BLOCK)], arrivals.at[2]),
    ]
    for copy in copies:
        copy.start()
    copies[0].wait()
    for quarter in range(Y):
        lower = quarter * HEAD_DIM
        part = jnp.concatenate(
            [held[:, t, lower : lower + HEAD_DIM] for t in (1, 2, 0, 3)], axis=1
        )
        rows[:, quarter] = jnp.broadcast_to(part[None], (Z, 8, 256))
    copies[1].wait()
    copies[2].wait()


def spread(gathered, rows):
    for quarter in range(Y):
        part = gathered[:, quarter].reshape(BLOCK, 256)
        rows[quarter, 0] = part
        rows[quarter, 1] = part


def project_features(scalars, x0, x1, weights, key_value, query):
    total = jnp.zeros((Y * BLOCK, 256), F32)
    for half, pair in enumerate((x0, x1)):
        for core in range(CORE):
            rows = weights[CORE * scalars[half] + core]
            total += matmul(pair[core].reshape(Y * BLOCK, 256), rows, ((1,), (0,)))
    key_value[...] = total[:, :BLOCK].astype(BF16)
    query[...] = total[:, BLOCK:].astype(BF16)


def project_cotangents(scalars, c0, c1, weights, key_value, query, both, turned):
    total = jnp.zeros((Y * BLOCK, BLOCK), F32)
    for half, pair in enumerate((c0, c1)):
        for core in range(CORE):
            rows = weights[CORE * scalars[half] + core, :, BLOCK:]
            total += matmul(pair[core].reshape(Y * BLOCK, 256), rows, ((1,), (0,)))
    low = low_lanes((Y * BLOCK, BLOCK))
    both[:, :BLOCK] = key_value[...]
    both[:, BLOCK:] = jnp.where(low, query[...], total.astype(BF16))
    for quarter in range(Y):
        part = weights[quarter, :, : 3 * HEAD_DIM].T
        turned[:, quarter * 256 : (quarter + 1) * 256] = part


def attention(pair, listed, usable):
    scale = HEAD_DIM ** (-0.5)
    low = low_lanes((BLOCK, BLOCK))
    zero = jnp.zeros((BLOCK, BLOCK), BF16)
    stacked = jnp.concatenate(
        [jnp.where(low, pair, zero), jnp.where(low, zero, pair)], axis=0
    )
    inner = matmul(listed, stacked, ((1,), (1,)))
    scores = inner[:, :BLOCK] * scale
    prob_grad = inner[:, BLOCK:]
    local_scores = jnp.where(usable, scores[:BLOCK], -1e30)
    scores = jnp.concatenate([local_scores, scores[BLOCK:]], axis=0)
    exponent = jnp.exp(scores - jnp.max(scores, axis=0, keepdims=True))
    total = jnp.sum(exponent, axis=0, keepdims=True)
    probs = exponent * (1.0 / total)
    mean = jnp.sum(probs * prob_grad, axis=0, keepdims=True)
    score_grad = (probs * (prob_grad - mean) * scale).astype(BF16)
    return stacked, jnp.concatenate([score_grad, probs.astype(BF16)], axis=1)


def matched(block, wrap):
    return [lax.rem(block - r - wrap + 2 * Y, Y) for r in range(ROUNDS)]


def gradients(scalars, flags, mine, ahead, arrived, x0, x1, bundle, total, both):
    low = low_lanes((BLOCK, BLOCK))
    for block in range(Y):
        listed = [mine[block, :, :BLOCK]] + [arrived[s] for s in matched(block, flags[0])]
        listed = jnp.concatenate(listed, axis=0)
        stacked, terms = attention(
            mine[block, :, BLOCK:], listed, flags[2 + block] > 0
        )
        query_side = matmul(terms[:, :BLOCK], listed, ((0,), (0,)))
        query_side = jnp.where(low, query_side, pltpu.roll(query_side, HEAD_DIM, 1))
        both[block, :, BLOCK:] = query_side.astype(BF16)
        total[block] = matmul(terms[:BLOCK], stacked, ((1,), (0,)))
    for block in range(Y):
        sources = matched(block, flags[1])
        listed = [ahead[block, :, :BLOCK]] + [mine[s, :, :BLOCK] for s in sources]
        listed = jnp.concatenate(listed, axis=0)
        stacked, terms = attention(
            ahead[block, :, BLOCK:], listed, flags[2 + Y + block] > 0
        )
        side = matmul(terms[BLOCK:], stacked, ((1,), (0,)))
        for r in range(ROUNDS):
            part = side[r * BLOCK : (r + 1) * BLOCK].astype(BF16).astype(F32)
            total[sources[r]] += part
    for block in range(Y):
        side = total[block].astype(BF16)
        both[block, :, :BLOCK] = side
        turned = side.T
        turned = jnp.concatenate([turned[:HEAD_DIM], turned[HEAD_DIM:]], axis=1)
        for part in range(XL):
            bundle[block, part, BLOCK:] = turned
    right = both[...].reshape(Y * BLOCK, 256)
    terms = lax.broadcasted_iota(jnp.int32, (BLOCK, 256), 1) < 3 * HEAD_DIM
    for half, pair in enumerate((x0, x1)):
        for core in range(CORE):
            product = matmul(pair[core].reshape(Y * BLOCK, 256), right, ((0,), (0,)))
            product = product.astype(BF16)
            quarter = CORE * scalars[half] + core
            for part in range(XL):
                rows = product[part * BLOCK : (part + 1) * BLOCK]
                bundle[quarter, part, :BLOCK] = jnp.where(terms, rows, both[quarter])


def add_terms(bundle, out):
    for source in range(Y):
        near, far = bundle[XL * source, :BLOCK], bundle[XL * source + 1, :BLOCK]
        total = (near.astype(F32) + far.astype(F32)).astype(BF16)
        for place, lower in ((1, 0), (2, HEAD_DIM), (0, 2 * HEAD_DIM)):
            at = place * 256 + source * HEAD_DIM
            out[:, at : at + HEAD_DIM] = total[:, lower : lower + HEAD_DIM]


def input_terms(scalars, bundle, w0, w1, w2, w3, out):
    sides, queries = [], []
    for slot in range(Y):
        entry = XL * lax.rem(scalars[2] + slot, Y) + scalars[3]
        folded = bundle[entry, BLOCK:]
        sides.append(jnp.concatenate([folded[:, :BLOCK], folded[:, BLOCK:]], axis=0))
        queries.append(bundle[entry, :BLOCK, 3 * HEAD_DIM :])
    for quarter in range(4):
        total = jnp.zeros((BLOCK, 256), F32)
        lower = quarter * 256
        for side, query, weights in zip(sides, queries, (w0, w1, w2, w3)):
            columns = weights[:, lower : lower + 256]
            total += matmul(side, columns[: 2 * HEAD_DIM], ((0,), (0,)))
            total += matmul(query, columns[2 * HEAD_DIM :], ((1,), (0,)))
        out[quarter] = total.astype(BF16)


def sum_terms(terms, out):
    out[...] = jnp.sum(terms[...].astype(F32), axis=0)


def shards(node_features, cotangent, proj_weights, local_mask, matching):
    xl = lax.axis_index("xl")
    z = lax.axis_index("z")
    xh = lax.axis_index("xh")
    core = lax.axis_index("core")
    y = lax.axis_index("y")
    scalars = jnp.stack([xh, 1 - xh, y, xl]).astype(jnp.int32)

    packed, rows = kernel_call(
        pack,
        [((2 * BLOCK, 256), BF16), ((Z, Y, 8, 256), BF16)],
        [HBM] * 3,
        1000,
        600000,
        (node_features, cotangent, proj_weights),
        (pltpu.VMEM((8, 4, 256), BF16), pltpu.SemaphoreType.DMA((3,))),
        60,
    )
    near = lax.all_to_all(rows, "z", 0, 0, tiled=True)
    p0 = lax.all_gather(packed, "y", axis=0)
    p1 = swapped(p0, "xh")
    (rows,) = kernel_call(
        spread, [((Y, XL, BLOCK, 256), BF16)], [VMEM], 1000, 800000, (near,)
    )
    weights = lax.all_to_all(
        rows.reshape(Y * XL, BLOCK, 256), ("y", "xl"), 0, 0, tiled=True
    ).reshape(4, 256, 256)
    x0 = lax.all_gather(p0[:, :BLOCK], "core", axis=0)
    c0 = lax.all_gather(p0[:, BLOCK:], "core", axis=0)
    x1 = lax.all_gather(p1[:, :BLOCK], "core", axis=0)

    key_value, query = kernel_call(
        project_features,
        [((512, BLOCK), BF16), ((512, BLOCK), BF16)],
        [SMEM] + [VMEM] * 3,
        2 * 512 * 1024 * 256,
        2000000,
        (scalars, x0, x1, weights),
    )
    arrived = shifted(key_value, 1)
    p1, query = lax.optimization_barrier((p1, query))
    c1 = lax.all_gather(p1[:, BLOCK:], "core", axis=0)
    both, turned = kernel_call(
        project_cotangents,
        [((512, 256), BF16), ((192, 1024), BF16)],
        [SMEM] + [VMEM] * 5,
        2 * 512 * 1024 * 128,
        3500000,
        (scalars, c0, c1, weights, key_value, query),
    )
    ahead = shifted(both, -1)
    group_weights = [turned] + [
        lax.ppermute(turned, "y", [(i, (i - k) % Y) for i in range(Y)]) for k in range(1, Y)
    ]

    mask = lax.all_gather(local_mask, "y", axis=0).reshape(Y, 1)
    usable = (mask > 0) | jnp.eye(1, dtype=bool)
    next_usable = (shifted(mask, -1) > 0) | jnp.eye(1, dtype=bool)
    at = xl * Z + z
    wraps = jnp.stack([at == 0, at == RING_SIZE - 1])
    flags = jnp.concatenate([wraps, usable.reshape(Y), next_usable.reshape(Y)])
    (bundle,) = kernel_call(
        gradients,
        [((Y, XL, 192, 256), BF16)],
        [SMEM] * 2 + [VMEM] * 5,
        7 * 1000 * 1000 * 1000,
        3000000,
        (
            scalars,
            flags.astype(jnp.int32),
            both.reshape(Y, BLOCK, 256),
            ahead.reshape(Y, BLOCK, 256),
            arrived.reshape(Y, BLOCK, BLOCK),
            x0,
            x1,
        ),
        (pltpu.VMEM((Y, BLOCK, BLOCK), F32), pltpu.VMEM((Y, BLOCK, 256), BF16)),
    )
    bundle, group_weights[1] = lax.optimization_barrier((bundle, group_weights[1]))
    bundle = lax.all_to_all(
        bundle.reshape(Y * XL, 192, 256), ("y", "xl"), 0, 0, tiled=True
    )
    (term,) = kernel_call(
        add_terms, [((BLOCK, 768), BF16)], [VMEM], 1000000, 800000, (bundle,)
    )
    term, bundle = lax.optimization_barrier((term, bundle))
    term = lax.all_to_all(term.reshape(Z, 8, 768), "z", 0, 0, tiled=True)
    (partial,) = kernel_call(
        input_terms,
        [((4, BLOCK, 256), BF16)],
        [SMEM] + [VMEM] * 5,
        2 * 128 * 1024 * 1024,
        2500000,
        (scalars, bundle, *group_weights),
    )
    partial = lax.all_gather(partial, "core", axis=0).reshape(CORE, XH, CORE, BLOCK, 256)
    partial = lax.dynamic_index_in_dim(partial, core, 2, keepdims=False)
    pair = jnp.sum(partial.astype(F32), axis=0)
    remote = lax.dynamic_index_in_dim(pair, 1 - xh, 0, keepdims=False)
    remote = lax.all_gather(remote, "xh", axis=0)
    remote = lax.dynamic_index_in_dim(remote, 1 - xh, 0, keepdims=False)
    pair = lax.dynamic_index_in_dim(pair, xh, 0, keepdims=False)
    input_grad = (pair + remote).astype(BF16)

    (weight_grads,) = kernel_call(
        sum_terms, [((8, 768), F32)], [VMEM], 1000000, 300000, (term,)
    )
    return (input_grad, weight_grads.reshape(8, 3, 256))


def solution(mesh):
    fine = Mesh(mesh.devices.reshape(Y, XL, Z, XH, CORE), AXES)
    head = ("xh", "core")
    return jax.shard_map(
        shards,
        mesh=fine,
        in_specs=(
            P(DOM, head),
            P(DOM, head),
            P(DOM, None, head),
            P(DOM, None),
            P(None, DOM),
        ),
        out_specs=(P(DOM, head), P(DOM, None, head)),
        check_vma=False,
    )
```

```python
import jax
import jax.numpy as jnp
from jax import lax
from jax.experimental import pallas as pl
from jax.experimental.pallas import tpu as pltpu
from jax.sharding import Mesh
from jax.sharding import PartitionSpec as P

HEAD_DIM = 64
BLOCK = 128
ROUNDS = 3
Y, XL, Z, XH, CORE = 4, 2, 16, 2, 2
AXES = ("y", "xl", "z", "xh", "core")
DOM = ("y", "xl", "z")
RING = ("xl", "z")
RING_SIZE = XL * Z
F32 = jnp.float32
BF16 = jnp.bfloat16
SMEM = pl.BlockSpec(memory_space=pltpu.SMEM)
VMEM = pl.BlockSpec(memory_space=pltpu.VMEM)
HBM = pl.BlockSpec(memory_space=pltpu.HBM)


def swapped(block, axis):
    return lax.ppermute(block, axis, [(0, 1), (1, 0)])


def shifted(block, distance):
    route = [(i, (i + distance) % RING_SIZE) for i in range(RING_SIZE)]
    return lax.ppermute(block, RING, route)


def matmul(left, right, dims):
    return lax.dot_general(left, right, (dims, ((), ())), preferred_element_type=F32)


def low_lanes(shape):
    return lax.broadcasted_iota(jnp.int32, shape, len(shape) - 1) < HEAD_DIM


def kernel_call(kernel, shapes, specs, flops, size, args, scratch=(), limit=16):
    return pl.pallas_call(
        kernel,
        out_shape=[jax.ShapeDtypeStruct(shape, dtype) for shape, dtype in shapes],
        in_specs=specs,
        out_specs=[VMEM] * len(shapes),
        scratch_shapes=list(scratch),
        compiler_params=pltpu.CompilerParams(vmem_limit_bytes=limit * 1024 * 1024),
        cost_estimate=pl.CostEstimate(flops=flops, bytes_accessed=size, transcendentals=0),
    )(*args)


def pack(features, cotangents, weights, packed, rows, held, arrivals):
    copies = [
        pltpu.make_async_copy(weights, held, arrivals.at[0]),
        pltpu.make_async_copy(features, packed.at[pl.ds(0, BLOCK)], arrivals.at[1]),
        pltpu.make_async_copy(cotangents, packed.at[pl.ds(BLOCK, BLOCK)], arrivals.at[2]),
    ]
    for copy in copies:
        copy.start()
    copies[0].wait()
    for quarter in range(Y):
        lower = quarter * HEAD_DIM
        part = jnp.concatenate(
            [held[:, t, lower : lower + HEAD_DIM] for t in (1, 2, 0, 3)], axis=1
        )
        rows[:, quarter] = jnp.broadcast_to(part[None], (Z, 8, 256))
    copies[1].wait()
    copies[2].wait()


def spread(gathered, rows):
    for quarter in range(Y):
        part = gathered[:, quarter].reshape(BLOCK, 256)
        rows[quarter, 0] = part
        rows[quarter, 1] = part


def project(scalars, x0, x1, c0, c1, weights, key_value, both, turned):
    total = jnp.zeros((Y * BLOCK, 256), F32)
    out_total = jnp.zeros((Y * BLOCK, BLOCK), F32)
    for half, (pair, other) in enumerate(((x0, c0), (x1, c1))):
        for core in range(CORE):
            rows = weights[CORE * scalars[half] + core]
            total += matmul(pair[core].reshape(Y * BLOCK, 256), rows, ((1,), (0,)))
            part = other[core].reshape(Y * BLOCK, 256)
            out_total += matmul(part, rows[:, BLOCK:], ((1,), (0,)))
    low = low_lanes((Y * BLOCK, BLOCK))
    key_value[...] = total[:, :BLOCK].astype(BF16)
    both[:, :BLOCK] = total[:, :BLOCK].astype(BF16)
    both[:, BLOCK:] = jnp.where(low, total[:, BLOCK:], out_total).astype(BF16)
    for quarter in range(Y):
        part = weights[quarter, :, : 3 * HEAD_DIM].T
        turned[:, quarter * 256 : (quarter + 1) * 256] = part


def attention(pair, listed, usable):
    scale = HEAD_DIM ** (-0.5)
    low = low_lanes((BLOCK, BLOCK))
    zero = jnp.zeros((BLOCK, BLOCK), BF16)
    stacked = jnp.concatenate(
        [jnp.where(low, pair, zero), jnp.where(low, zero, pair)], axis=0
    )
    inner = matmul(listed, stacked, ((1,), (1,)))
    scores = inner[:, :BLOCK] * scale
    prob_grad = inner[:, BLOCK:]
    local_scores = jnp.where(usable, scores[:BLOCK], -1e30)
    scores = jnp.concatenate([local_scores, scores[BLOCK:]], axis=0)
    exponent = jnp.exp(scores - jnp.max(scores, axis=0, keepdims=True))
    total = jnp.sum(exponent, axis=0, keepdims=True)
    probs = exponent * (1.0 / total)
    mean = jnp.sum(probs * prob_grad, axis=0, keepdims=True)
    score_grad = (probs * (prob_grad - mean) * scale).astype(BF16)
    return stacked, jnp.concatenate([score_grad, probs.astype(BF16)], axis=1)


def matched(block, wrap):
    return [lax.rem(block - r - wrap + 2 * Y, Y) for r in range(ROUNDS)]


def gradients(scalars, flags, mine, ahead, arrived, x0, x1, bundle, total, both):
    low = low_lanes((BLOCK, BLOCK))
    for block in range(Y):
        listed = [mine[block, :, :BLOCK]] + [arrived[s] for s in matched(block, flags[0])]
        listed = jnp.concatenate(listed, axis=0)
        stacked, terms = attention(
            mine[block, :, BLOCK:], listed, flags[2 + block] > 0
        )
        query_side = matmul(terms[:, :BLOCK], listed, ((0,), (0,)))
        query_side = jnp.where(low, query_side, pltpu.roll(query_side, HEAD_DIM, 1))
        both[block, :, BLOCK:] = query_side.astype(BF16)
        total[block] = matmul(terms[:BLOCK], stacked, ((1,), (0,)))
    for block in range(Y):
        sources = matched(block, flags[1])
        listed = [ahead[block, :, :BLOCK]] + [mine[s, :, :BLOCK] for s in sources]
        listed = jnp.concatenate(listed, axis=0)
        stacked, terms = attention(
            ahead[block, :, BLOCK:], listed, flags[2 + Y + block] > 0
        )
        side = matmul(terms[BLOCK:], stacked, ((1,), (0,)))
        for r in range(ROUNDS):
            part = side[r * BLOCK : (r + 1) * BLOCK].astype(BF16).astype(F32)
            total[sources[r]] += part
    for block in range(Y):
        side = total[block].astype(BF16)
        both[block, :, :BLOCK] = side
        turned = side.T
        turned = jnp.concatenate([turned[:HEAD_DIM], turned[HEAD_DIM:]], axis=1)
        for part in range(XL):
            bundle[block, part, BLOCK:] = turned
    right = both[...].reshape(Y * BLOCK, 256)
    terms = lax.broadcasted_iota(jnp.int32, (BLOCK, 256), 1) < 3 * HEAD_DIM
    for half, pair in enumerate((x0, x1)):
        for core in range(CORE):
            product = matmul(pair[core].reshape(Y * BLOCK, 256), right, ((0,), (0,)))
            product = product.astype(BF16)
            quarter = CORE * scalars[half] + core
            for part in range(XL):
                rows = product[part * BLOCK : (part + 1) * BLOCK]
                bundle[quarter, part, :BLOCK] = jnp.where(terms, rows, both[quarter])


def add_terms(bundle, out):
    for source in range(Y):
        near, far = bundle[XL * source, :BLOCK], bundle[XL * source + 1, :BLOCK]
        total = (near.astype(F32) + far.astype(F32)).astype(BF16)
        for place, lower in ((1, 0), (2, HEAD_DIM), (0, 2 * HEAD_DIM)):
            at = place * 256 + source * HEAD_DIM
            out[:, at : at + HEAD_DIM] = total[:, lower : lower + HEAD_DIM]


def input_terms(scalars, bundle, w0, w1, w2, w3, out):
    sides, queries = [], []
    for slot in range(Y):
        entry = XL * lax.rem(scalars[2] + slot, Y) + scalars[3]
        folded = bundle[entry, BLOCK:]
        sides.append(jnp.concatenate([folded[:, :BLOCK], folded[:, BLOCK:]], axis=0))
        queries.append(bundle[entry, :BLOCK, 3 * HEAD_DIM :])
    for quarter in range(4):
        total = jnp.zeros((BLOCK, 256), F32)
        lower = quarter * 256
        for side, query, weights in zip(sides, queries, (w0, w1, w2, w3)):
            columns = weights[:, lower : lower + 256]
            total += matmul(side, columns[: 2 * HEAD_DIM], ((0,), (0,)))
            total += matmul(query, columns[2 * HEAD_DIM :], ((1,), (0,)))
        out[quarter] = total.astype(BF16)


def sum_terms(terms, out):
    out[...] = jnp.sum(terms[...].astype(F32), axis=0)


def shards(node_features, cotangent, proj_weights, local_mask, matching):
    xl = lax.axis_index("xl")
    z = lax.axis_index("z")
    xh = lax.axis_index("xh")
    core = lax.axis_index("core")
    y = lax.axis_index("y")
    scalars = jnp.stack([xh, 1 - xh, y, xl]).astype(jnp.int32)

    packed, rows = kernel_call(
        pack,
        [((2 * BLOCK, 256), BF16), ((Z, Y, 8, 256), BF16)],
        [HBM] * 3,
        1000,
        600000,
        (node_features, cotangent, proj_weights),
        (pltpu.VMEM((8, 4, 256), BF16), pltpu.SemaphoreType.DMA((3,))),
        60,
    )
    near = lax.all_to_all(rows, "z", 0, 0, tiled=True)
    p0 = lax.all_gather(packed, "y", axis=0)
    p1 = swapped(p0, "xh")
    (rows,) = kernel_call(
        spread, [((Y, XL, BLOCK, 256), BF16)], [VMEM], 1000, 800000, (near,)
    )
    weights = lax.all_to_all(
        rows.reshape(Y * XL, BLOCK, 256), ("y", "xl"), 0, 0, tiled=True
    ).reshape(4, 256, 256)
    x0 = lax.all_gather(p0[:, :BLOCK], "core", axis=0)
    c0 = lax.all_gather(p0[:, BLOCK:], "core", axis=0)
    x1 = lax.all_gather(p1[:, :BLOCK], "core", axis=0)

    c1 = lax.all_gather(p1[:, BLOCK:], "core", axis=0)
    key_value, both, turned = kernel_call(
        project,
        [((512, BLOCK), BF16), ((512, 256), BF16), ((192, 1024), BF16)],
        [SMEM] + [VMEM] * 5,
        2 * 512 * 1024 * 384,
        5000000,
        (scalars, x0, x1, c0, c1, weights),
    )
    arrived = shifted(key_value, 1)
    ahead = shifted(both, -1)
    group_weights = [turned] + [
        lax.ppermute(turned, "y", [(i, (i - k) % Y) for i in range(Y)]) for k in range(1, Y)
    ]

    mask = lax.all_gather(local_mask, "y", axis=0).reshape(Y, 1)
    usable = (mask > 0) | jnp.eye(1, dtype=bool)
    next_usable = (shifted(mask, -1) > 0) | jnp.eye(1, dtype=bool)
    at = xl * Z + z
    wraps = jnp.stack([at == 0, at == RING_SIZE - 1])
    flags = jnp.concatenate([wraps, usable.reshape(Y), next_usable.reshape(Y)])
    (bundle,) = kernel_call(
        gradients,
        [((Y, XL, 192, 256), BF16)],
        [SMEM] * 2 + [VMEM] * 5,
        7 * 1000 * 1000 * 1000,
        3000000,
        (
            scalars,
            flags.astype(jnp.int32),
            both.reshape(Y, BLOCK, 256),
            ahead.reshape(Y, BLOCK, 256),
            arrived.reshape(Y, BLOCK, BLOCK),
            x0,
            x1,
        ),
        (pltpu.VMEM((Y, BLOCK, BLOCK), F32), pltpu.VMEM((Y, BLOCK, 256), BF16)),
    )
    bundle, group_weights[2] = lax.optimization_barrier((bundle, group_weights[2]))
    bundle = lax.all_to_all(
        bundle.reshape(Y * XL, 192, 256), ("y", "xl"), 0, 0, tiled=True
    )
    (term,) = kernel_call(
        add_terms, [((BLOCK, 768), BF16)], [VMEM], 1000000, 800000, (bundle,)
    )
    term, bundle = lax.optimization_barrier((term, bundle))
    term = lax.all_to_all(term.reshape(Z, 8, 768), "z", 0, 0, tiled=True)
    (partial,) = kernel_call(
        input_terms,
        [((4, BLOCK, 256), BF16)],
        [SMEM] + [VMEM] * 5,
        2 * 128 * 1024 * 1024,
        2500000,
        (scalars, bundle, *group_weights),
    )
    partial = lax.all_gather(partial, "core", axis=0).reshape(CORE, XH, CORE, BLOCK, 256)
    partial = lax.dynamic_index_in_dim(partial, core, 2, keepdims=False)
    pair = jnp.sum(partial.astype(F32), axis=0)
    remote = lax.dynamic_index_in_dim(pair, 1 - xh, 0, keepdims=False)
    remote = lax.all_gather(remote, "xh", axis=0)
    remote = lax.dynamic_index_in_dim(remote, 1 - xh, 0, keepdims=False)
    pair = lax.dynamic_index_in_dim(pair, xh, 0, keepdims=False)
    input_grad = (pair + remote).astype(BF16)

    (weight_grads,) = kernel_call(
        sum_terms, [((8, 768), F32)], [VMEM], 1000000, 300000, (term,)
    )
    return (input_grad, weight_grads.reshape(8, 3, 256))


def solution(mesh):
    fine = Mesh(mesh.devices.reshape(Y, XL, Z, XH, CORE), AXES)
    head = ("xh", "core")
    return jax.shard_map(
        shards,
        mesh=fine,
        in_specs=(
            P(DOM, head),
            P(DOM, head),
            P(DOM, None, head),
            P(DOM, None),
            P(None, DOM),
        ),
        out_specs=(P(DOM, head), P(DOM, None, head)),
        check_vma=False,
    )
```
